32 devices in a mesh: segment: 2 (over x), tile: 8 (over z, y), mp: 2 (over core).
Axes of the slice: x: 2, y: 2, z: 4, core: 2. Of those that a mesh axis runs over, the one named last changes fastest.
Arguments:
- fine_qkv: bfloat16 [2, 3072, 3, 1792], P('segment', 'tile', None, 'mp'), may hold values from -6 to 6
- panels: bfloat16 [2, 32, 14, 2, 64, 128], P('segment', 'tile', 'mp'), may hold values from -6 to 6
- owners: int32 [2, 8, 14, 6, 2], P('segment', 'tile', 'mp'), may hold values from 0 to 7, all different within a row; in each aligned block of 42 rows (0 to 41, 42 to 83, ..., all dimensions but the last counted through in order) at most 11 rows name the same one
- picks: int32 [2, 8, 14, 6, 2], P('segment', 'tile', 'mp'), may hold values from 0 to 3
- out_proj: bfloat16 [1792, 3200], P('mp'), may hold values from -0.5 to 0.5
Outputs:
- merged: bfloat16 [2, 3072, 3200], P('segment', ('tile', 'mp'))
The draws below stay inside these ranges and needn't reach their ends.
Inputs may be any that keep to these rules, and one draw needn't show every extreme that they name: `owners`: each row's 2 entries name different tiles. Among the list entries of one segment, tile and mp index, no tile is named more than 11 times.
All inputs are finite; a program needn't handle non-finite values.
Results may differ from the reference program's by a relative error of at most 0.0075.
Values may be sent and summed in bfloat16 or wider, within the bound.
A program may use at most 64 MiB of HBM per device.

```python
import math
import jax
import jax.numpy as jnp
import numpy as np
from jax import lax

D = 3200
H = 14
HEAD = 128
PANEL = 64
K_LIST = 2
BLK_DEV = 6
P_DEV = 4
SEGMENTS = 2
HEADS_DEV = 7
FINE_ROWS = 3072
PANELS = 32
CAP = 11
N_TILE = 8
N_MP = 2


def draw_fine_qkv(key, part):
    full_shape = (SEGMENTS, FINE_ROWS, 3, H * HEAD)
    key_one = jax.random.fold_in(key, 0)
    return jnp.clip(jax.random.normal(key_one, full_shape, jnp.float32), -6.0, 6.0).astype(jnp.bfloat16)


def plant(values, key, low, top_value):
    index_at = [jax.random.randint(jax.random.fold_in(key, axis), (), 0, length) for axis, length in enumerate(values.shape)]
    widest = values.shape.index(max(values.shape))
    beside = index_at[:widest] + [(index_at[widest] + 1) % values.shape[widest]] + index_at[widest + 1:]
    return values.at[tuple(index_at)].set(low).at[tuple(beside)].set(top_value)


def block_scale(key, extent, pieces, least, top_value):
    gain, own = 1.0, jax.random.fold_in(key, 6)
    for axis_at, shards_of in pieces:
        heights = jnp.exp(jax.random.uniform(jax.random.fold_in(own, axis_at), (shards_of,), jnp.float32, least / len(pieces), top_value / len(pieces)))
        gain = gain * jnp.repeat(heights, extent[axis_at] // shards_of).reshape([-1 if axis == axis_at else 1 for axis in range(len(extent))])
    return gain


def deal_out(key, own, number, rows, number_of, top, reach, slope):
    sequence = jax.random.permutation(key, number_of)
    crowded, common = load_shares(number_of, rows * top, reach, slope, True), load_shares(number_of, rows * top, reach, slope, False)
    places = jnp.arange(number_of)

    def named(tallies, rotation):
        used = int((tallies > 0).sum())
        fixed = max(1, used // 4)
        passed = fixed + (places - fixed + rotation * (used - fixed)) % max(1, number_of - fixed)
        return jnp.zeros((number_of,), jnp.int32).at[sequence[jnp.where(places < fixed, places, passed)]].set(jnp.asarray(tallies, jnp.int32))

    tallies = jnp.where(number % 4 == 0, named(crowded, number // 4), named(common, number - number // 4 - 1))
    mixed = jax.random.permutation(jax.random.fold_in(own, 3), number_of)
    donor, sink = mixed[0:number_of // 2 * 2:2], mixed[1:number_of // 2 * 2:2]
    slack = jnp.minimum(tallies[donor] - 1, reach - tallies[sink]) // 2
    slack = jnp.where((donor == sequence[0]) | (sink == sequence[0]) | (tallies[sink] == 0), 0, jnp.maximum(slack, 0))
    passed = jax.random.randint(jax.random.fold_in(own, 4), (number_of // 2,), 0, 1 << 20) % (slack + 1)
    tallies = tallies.at[donor].add(-passed).at[sink].add(passed)
    items = jnp.searchsorted(jnp.cumsum(tallies), jnp.arange(rows * top), side="right").astype(jnp.int32)
    table = items.reshape(top, rows).T
    table = table[jax.random.permutation(jax.random.fold_in(own, 1), rows)]
    rotation = jax.random.randint(jax.random.fold_in(own, 2), (rows, 1), 0, top)
    return jnp.take_along_axis(table, (jnp.arange(top)[None, :] + rotation) % top, axis=1)


def load_shares(amount, total, most, slope, full):
    weights = [(1 << 20) // math.isqrt(standing ** slope) + 1 for standing in range(1, amount + 1)]
    largest = most if full else min(most, max(-(-total // amount), total * weights[0] // sum(weights)))
    least = 1 if total - largest >= amount - 1 else 0
    given, rest = [largest] + [least] * (amount - 1), total - largest - least * (amount - 1)
    while rest > 0:
        movable = [i for i in range(1, amount) if given[i] < largest] or [i for i in range(1, amount) if given[i] < most]
        mass, left = sum([weights[i] for i in movable]), rest
        for i in movable:
            addition = min(most - given[i], max(1, left * weights[i] // mass), rest)
            given[i] = given[i] + addition
            rest = rest - addition
    return np.array(given)


def noise(rng, dims, spread, reach, cuts=(), kind=jnp.bfloat16):
    values = spread * jax.random.normal(rng, dims, jnp.float32)
    if cuts:
        values = values * block_scale(rng, dims, cuts, -0.22, 0.18)
    return jnp.clip(values, -reach, reach).astype(kind)


def setup_inputs(seed: int = 0) -> dict:
    splits = jax.random.split(jax.random.key(seed), 6)
    fine_qkv = draw_fine_qkv(jax.random.fold_in(splits[5], 71), 0)
    panels = noise(splits[1], (SEGMENTS, PANELS, H, 2, PANEL, HEAD), 1.0, 6.0, ((0, 2), (1, 8), (2, 2)))
    owners_keys = jax.random.split(jax.random.fold_in(splits[2], 1), SEGMENTS * N_TILE * H * BLK_DEV // (HEADS_DEV * BLK_DEV))
    owners_turns = jax.random.permutation(jax.random.fold_in(splits[2], 3), SEGMENTS * N_TILE * H * BLK_DEV // (HEADS_DEV * BLK_DEV))
    owners = jax.vmap(lambda own, number: deal_out(jax.random.fold_in(splits[2], 2), own, number, HEADS_DEV * BLK_DEV, N_TILE, K_LIST, CAP, 1))(owners_keys, owners_turns).reshape((SEGMENTS, N_TILE, H, BLK_DEV, K_LIST))
    picks = plant(jax.random.randint(splits[3], (SEGMENTS, N_TILE, H, BLK_DEV, K_LIST), 0, P_DEV), jax.random.fold_in(splits[3], 1), 0, P_DEV - 1).astype(jnp.int32)
    out_proj = noise(splits[4], (H * HEAD, D), HEAD ** -0.5, 0.5, ((0, 2),))
    return {"fine_qkv": fine_qkv, "panels": panels, "owners": owners, "picks": picks, "out_proj": out_proj}


def merge_segment(fine_rows, held_panels, owner_lists, pick_lists, out_proj):
    fine_parts = fine_rows.reshape(N_TILE, BLK_DEV, PANEL, 3, H, HEAD).astype(jnp.float32)
    queries = fine_parts[:, :, :, 0]
    fine_keys = fine_parts[:, :, :, 1]
    fine_values = fine_parts[:, :, :, 2]
    chosen = owner_lists * P_DEV + pick_lists
    head_index = jnp.broadcast_to(jnp.arange(H, dtype=jnp.int32)[None, :, None, None], chosen.shape)
    coarse = held_panels[chosen, head_index].astype(jnp.float32)
    score_scale = 1.0 / math.sqrt(HEAD)
    near_scores = jnp.einsum('tbqhd,tbkhd->thbqk', queries, fine_keys)
    far_scores = jnp.einsum('tbqhd,thbjkd->thbqjk', queries, coarse[:, :, :, :, 0])
    scores = jnp.concatenate([near_scores, far_scores.reshape(N_TILE, H, BLK_DEV, PANEL, K_LIST * PANEL)], axis=-1) * score_scale
    row_max = lax.optimization_barrier(jnp.max(scores, axis=-1, keepdims=True))
    exponent = jnp.exp(scores - row_max)
    weights = (exponent / lax.optimization_barrier(jnp.sum(exponent, axis=-1, keepdims=True))).astype(jnp.bfloat16)
    weights = lax.optimization_barrier(weights).astype(jnp.float32)
    near_weights = weights[..., :PANEL]
    far_weights = weights[..., PANEL:].reshape(N_TILE, H, BLK_DEV, PANEL, K_LIST, PANEL)
    attended = jnp.einsum('thbqk,tbkhd->tbqhd', near_weights, fine_values)
    attended = attended + jnp.einsum('thbqjk,thbjkd->tbqhd', far_weights, coarse[:, :, :, :, 1])
    attended = attended.astype(jnp.bfloat16).reshape(FINE_ROWS, N_MP, HEADS_DEV * HEAD)
    proj_rows = out_proj.reshape(N_MP, HEADS_DEV * HEAD, D)
    summed = jnp.zeros((FINE_ROWS, D), jnp.float32)
    for core_index in range(N_MP):
        core_part = jnp.dot(attended[:, core_index], proj_rows[core_index], preferred_element_type=jnp.float32).astype(jnp.bfloat16)
        summed = summed + lax.optimization_barrier(core_part).astype(jnp.float32)
    return summed.astype(jnp.bfloat16)

def reference(fine_qkv, panels, owners, picks, out_proj):

    def one_segment(segment_index):
        return merge_segment(fine_qkv[segment_index], panels[segment_index], owners[segment_index], picks[segment_index], out_proj)
    segment_results = lax.map(one_segment, jnp.arange(SEGMENTS, dtype=jnp.int32))
    return jnp.roll(segment_results, 1, axis=0)
```

```python
import functools
import math

import jax
import jax.numpy as jnp
from jax import lax
from jax.experimental import pallas as pl
from jax.experimental.pallas import tpu as pltpu
from jax.sharding import PartitionSpec as P

MESH = pl.DeviceIdType.MESH
LANES = 128
AHEAD = 3


def request_kernel(capacity, owners_ref, picks_ref, req_ref, slot_ref, count_ref):
    tiles = req_ref.shape[0]
    blocks, lists, heads = owners_ref.shape[2:]
    for tile in range(tiles):
        count_ref[tile] = 0

    def clear(tile, carry):
        for rank in range(capacity):
            req_ref[tile, rank] = 0
        return carry

    lax.fori_loop(0, tiles, clear, 0)
    for head in range(heads):
        for block in range(blocks):
            for entry in range(lists):
                owner = owners_ref[0, 0, block, entry, head]
                rank = count_ref[owner]
                count_ref[owner] = rank + 1
                req_ref[owner, rank] = picks_ref[0, 0, block, entry, head] * heads + head
                slot_ref[(head * blocks + block) * lists + entry] = owner * capacity + rank


def main_kernel(
    cfg,
    req_ref,
    slot_ref,
    fine_hbm,
    held_hbm,
    proj_hbm,
    out_ref,
    fine_ref,
    held_ref,
    relay_ref,
    proj_ref,
    asked_ref,
    asked_smem,
    serve_ref,
    recv_ref,
    att_ref,
    moved_ref,
    psend_ref,
    precv_ref,
    total_ref,
    load_sem,
    smem_sem,
    relay_send,
    relay_recv,
    gate_sem,
    req_send,
    req_recv,
    pan_send,
    pan_recv,
    x_send,
    x_recv,
    mp_send,
    mp_recv,
):
    tiles, segments, capacity, heads, blocks, lists, panel, width, chunks = cfg
    tile = lax.axis_index("tile")
    segment = lax.axis_index("segment")
    core = lax.axis_index("mp")
    half_blocks = blocks // 2
    half = half_blocks * panel
    scale = 1.0 / math.sqrt(width)

    loads = [
        pltpu.make_async_copy(held_hbm, held_ref, load_sem.at[0]),
        pltpu.make_async_copy(fine_hbm, fine_ref, load_sem.at[1]),
        pltpu.make_async_copy(proj_hbm, proj_ref, load_sem.at[2]),
    ]
    for load in loads:
        load.start()

    nxt = lax.rem(segment + 1, segments)
    prv = lax.rem(segment + segments - 1, segments)
    barrier = pltpu.get_barrier_semaphore()

    def greet(step, carry):
        pl.semaphore_signal(
            barrier,
            inc=1,
            device_id=(segment, lax.rem(tile + step, tiles), core),
            device_id_type=MESH,
        )
        return carry

    lax.fori_loop(1, tiles, greet, 0)
    pl.semaphore_signal(barrier, inc=1, device_id=(nxt, tile, core), device_id_type=MESH)
    pl.semaphore_signal(barrier, inc=1, device_id=(prv, tile, core), device_id_type=MESH)
    pl.semaphore_signal(barrier, inc=1, device_id=(segment, tile, 1 - core), device_id_type=MESH)
    pl.semaphore_wait(barrier, tiles + 2)

    half_tiles = tiles // 2
    quarter = tiles // 4
    plane = tile // quarter
    inner = jnp.logical_or(plane == 1, plane == 2)
    partner = jnp.where(plane == 1, tile + quarter, tile - quarter)
    base = (tile // half_tiles) * half_tiles
    far_base = half_tiles - base

    def near_tile(step):
        return base + lax.rem(tile - base + step, half_tiles)

    def far_tile(step):
        return far_base + lax.rem(tile - base + step, half_tiles)

    def mirror(row):
        return lax.rem(row + half_tiles, tiles)

    relay_copy = pltpu.make_async_remote_copy(
        src_ref=held_hbm,
        dst_ref=relay_ref,
        send_sem=relay_send,
        recv_sem=relay_recv,
        device_id=(segment, jnp.where(inner, partner, mirror(tile)), core),
        device_id_type=MESH,
    )

    def request_copy(owner, server, row):
        return pltpu.make_async_remote_copy(
            src_ref=req_ref.at[owner],
            dst_ref=asked_ref.at[row],
            send_sem=req_send.at[owner],
            recv_sem=req_recv.at[row],
            device_id=(segment, server, core),
            device_id_type=MESH,
        )

    def far_request(owner):
        far_plane = owner // quarter
        relayed = jnp.logical_or(far_plane == 1, far_plane == 2)
        through = jnp.where(far_plane == 1, owner + quarter, owner - quarter)
        return request_copy(
            owner, jnp.where(relayed, through, owner), jnp.where(relayed, mirror(tile), tile)
        )

    def start_near(step, carry):
        owner = near_tile(step)
        request_copy(owner, owner, tile).start()
        return carry

    def start_far(step, carry):
        owner = far_tile(step)

        @pl.when(jnp.logical_not(jnp.logical_and(inner, owner == partner)))
        def _():
            far_request(owner).start()

        return carry

    def sent_near(step, carry):
        owner = near_tile(step)
        request_copy(owner, owner, owner).wait_send()
        return carry

    def sent_far(step, carry):
        owner = far_tile(step)

        @pl.when(jnp.logical_not(jnp.logical_and(inner, owner == partner)))
        def _():
            far_request(owner).wait_send()

        return carry

    def wait_near(step, carry):
        owner = near_tile(step)
        request_copy(owner, owner, owner).wait_recv()
        return carry

    def wait_far(step, carry):
        owner = far_tile(step)

        @pl.when(jnp.logical_not(jnp.logical_and(inner, owner == mirror(tile))))
        def _():
            request_copy(owner, owner, owner).wait_recv()

        return carry

    lax.fori_loop(1, half_tiles, start_near, 0)
    lax.fori_loop(0, half_tiles, start_far, 0)
    asked_ref[tile] = req_ref[tile]

    @pl.when(inner)
    def _():
        asked_ref[mirror(tile)] = req_ref[partner]

    lax.fori_loop(1, half_tiles, sent_near, 0)
    lax.fori_loop(0, half_tiles, sent_far, 0)

    @pl.when(inner)
    def _():
        relay_copy.start()

    loads[0].wait()
    lax.fori_loop(1, half_tiles, wait_near, 0)
    lax.fori_loop(0, half_tiles, wait_far, 0)
    to_smem = pltpu.make_async_copy(asked_ref, asked_smem, smem_sem)
    to_smem.start()
    to_smem.wait()

    def panel_copy(row, dest, owner):
        return pltpu.make_async_remote_copy(
            src_ref=serve_ref.at[row],
            dst_ref=recv_ref.at[pl.ds(owner * capacity, capacity)],
            send_sem=pan_send.at[row],
            recv_sem=pan_recv.at[owner],
            device_id=(segment, dest, core),
            device_id_type=MESH,
        )

    def pack(bank_ref, row):
        for rank in range(capacity):
            serve_ref[row, rank] = bank_ref[asked_smem[row, rank]]

    def serve_near(step, carry):
        dest = near_tile(step)
        pack(held_ref, dest)
        panel_copy(dest, dest, tile).start()
        return carry

    def pack_far(step, carry):
        pack(held_ref, far_tile(step))
        return carry

    def start_far_panels(step, carry):
        dest = far_tile(step)
        panel_copy(dest, dest, tile).start()
        return carry

    def serve_relay(step, carry):
        dest = near_tile(step)
        pack(relay_ref, mirror(dest))
        panel_copy(mirror(dest), dest, partner).start()
        return carry

    lax.fori_loop(1, half_tiles, serve_near, 0)
    for rank in range(capacity):
        recv_ref[tile * capacity + rank] = held_ref[asked_smem[tile, rank]]

    @pl.when(jnp.logical_not(inner))
    def _():
        lax.fori_loop(0, half_tiles, pack_far, 0)
        pl.semaphore_wait(gate_sem, 1)
        lax.fori_loop(0, half_tiles, start_far_panels, 0)

    @pl.when(inner)
    def _():
        relay_copy.wait_recv()
        pl.semaphore_signal(
            gate_sem, inc=1, device_id=(segment, mirror(tile), core), device_id_type=MESH
        )
        lax.fori_loop(1, half_tiles, serve_relay, 0)
        for rank in range(capacity):
            recv_ref[partner * capacity + rank] = relay_ref[asked_smem[mirror(tile), rank]]
        relay_copy.wait_send()

    loads[1].wait()
    loads[2].wait()

    def land_near(step, carry):
        peer = near_tile(step)
        copy = panel_copy(peer, peer, peer)
        copy.wait_send()
        copy.wait_recv()
        return carry

    def land_far(step, carry):
        peer = far_tile(step)

        @pl.when(jnp.logical_not(jnp.logical_and(inner, peer == mirror(tile))))
        def _():
            panel_copy(peer, peer, peer).wait_send()

        @pl.when(jnp.logical_not(jnp.logical_and(inner, peer == partner)))
        def _():
            panel_copy(peer, peer, peer).wait_recv()

        return carry

    lax.fori_loop(1, half_tiles, land_near, 0)
    lax.fori_loop(0, half_tiles, land_far, 0)

    def attend(block, group):
        rows = pl.ds(pl.multiple_of(block * panel, panel), panel)
        scores, values = [], []
        for head in group:
            cols = slice(head * width, (head + 1) * width)
            keys, vals = [fine_ref[1, rows, cols]], [fine_ref[2, rows, cols]]
            for entry in range(lists):
                slot = slot_ref[(head * blocks + block) * lists + entry]
                keys.append(recv_ref[slot, 0])
                vals.append(recv_ref[slot, 1])
            values.append(jnp.concatenate(vals, axis=0))
            scores.append(
                lax.dot_general(
                    fine_ref[0, rows, cols],
                    jnp.concatenate(keys, axis=0),
                    (((1,), (1,)), ((), ())),
                    preferred_element_type=jnp.float32,
                )
                * scale
            )
        weights = []
        for score in scores:
            exponent = jnp.exp(score - jnp.max(score, axis=-1, keepdims=True))
            inverse = 1.0 / jnp.sum(exponent, axis=-1, keepdims=True)
            weights.append((exponent * inverse).astype(jnp.bfloat16))
        for at, head in enumerate(group):
            att_ref[rows, head * width : (head + 1) * width] = jnp.dot(
                weights[at], values[at], preferred_element_type=jnp.float32
            ).astype(jnp.bfloat16)

    def hop(place):
        rows = pl.ds(pl.multiple_of((theirs + place) * panel, panel), panel)
        return pltpu.make_async_remote_copy(
            src_ref=att_ref.at[rows],
            dst_ref=moved_ref.at[rows],
            send_sem=x_send.at[place],
            recv_sem=x_recv.at[place],
            device_id=(nxt, tile, core),
            device_id_type=MESH,
        )

    theirs = (1 - core) * half_blocks
    mine = core * half_blocks
    mine_rows = pl.ds(pl.multiple_of(mine * panel, panel), half)
    theirs_rows = pl.ds(pl.multiple_of(theirs * panel, panel), half)
    groups = (tuple(range(heads - 2)), tuple(range(heads - 2, heads)))

    def hop_mine(at):
        group = groups[at]
        cols = pl.ds(group[0] * width, len(group) * width)
        return pltpu.make_async_remote_copy(
            src_ref=att_ref.at[mine_rows, cols],
            dst_ref=moved_ref.at[mine_rows, cols],
            send_sem=x_send.at[half_blocks + at],
            recv_sem=x_recv.at[half_blocks + at],
            device_id=(nxt, tile, core),
            device_id_type=MESH,
        )

    def send_theirs(place, carry):
        attend(theirs + place, tuple(range(heads)))
        hop(place).start()
        return carry

    lax.fori_loop(0, half_blocks, send_theirs, 0)
    for at in range(2):
        def attend_mine(place, carry):
            attend(mine + place, groups[at])
            return carry

        lax.fori_loop(0, half_blocks, attend_mine, 0)
        hop_mine(at).start()

    step_cols = proj_ref.shape[1] // chunks

    def product(rows, group, chunk):
        depth = slice(group[0] * width, (group[-1] + 1) * width)
        return jnp.dot(
            moved_ref[rows, depth],
            proj_ref[depth, chunk * step_cols : (chunk + 1) * step_cols],
            preferred_element_type=jnp.float32,
        )

    def swap(chunk):
        return pltpu.make_async_remote_copy(
            src_ref=psend_ref.at[chunk],
            dst_ref=precv_ref.at[chunk],
            send_sem=mp_send.at[chunk],
            recv_sem=mp_recv.at[chunk],
            device_id=(segment, tile, 1 - core),
            device_id_type=MESH,
        )

    for place in range(half_blocks):
        hop(place).wait()
    for chunk in range(chunks):
        psend_ref[chunk] = product(theirs_rows, tuple(range(heads)), chunk).astype(jnp.bfloat16)
        swap(chunk).start()
    hop_mine(0).wait()
    for chunk in range(chunks):
        total_ref[chunk] = product(mine_rows, groups[0], chunk)
    for chunk in range(chunks):
        swap(chunk).wait()
    hop_mine(1).wait()
    for chunk in range(chunks):
        own = (total_ref[chunk] + product(mine_rows, groups[1], chunk)).astype(jnp.bfloat16)
        out_ref[:, chunk * step_cols : (chunk + 1) * step_cols] = (
            own.astype(jnp.float32) + precv_ref[chunk].astype(jnp.float32)
        ).astype(jnp.bfloat16)


def on_device(fine_qkv, panels, owners, picks, out_proj):
    tiles = lax.axis_size("tile")
    segments = lax.axis_size("segment")
    heads, blocks, lists = owners.shape[2:]
    entries = heads * blocks * lists
    capacity = max(2, (entries + tiles - 1) // tiles)
    rows = fine_qkv.shape[1]
    held = panels.reshape((-1,) + panels.shape[3:])
    panel, width = held.shape[-2:]
    depth, columns = out_proj.shape
    chunks = 5
    smem = pl.BlockSpec(memory_space=pltpu.SMEM)
    vmem = pl.BlockSpec(memory_space=pltpu.VMEM)
    anywhere = pl.BlockSpec(memory_space=pl.ANY)
    requests, slots = pl.pallas_call(
        functools.partial(request_kernel, capacity),
        out_shape=(
            jax.ShapeDtypeStruct((tiles, LANES), jnp.int32),
            jax.ShapeDtypeStruct((entries,), jnp.int32),
        ),
        in_specs=[smem, smem],
        out_specs=(smem, smem),
        scratch_shapes=[pltpu.SMEM((tiles,), jnp.int32)],
        name="requests",
    )(owners.transpose(0, 1, 3, 4, 2), picks.transpose(0, 1, 3, 4, 2))
    cfg = (tiles, segments, capacity, heads, blocks, lists, panel, width, chunks)
    dma = pltpu.SemaphoreType.DMA
    bf16 = jnp.bfloat16
    merged = pl.pallas_call(
        functools.partial(main_kernel, cfg),
        out_shape=jax.ShapeDtypeStruct((rows // 2, columns), bf16),
        in_specs=[vmem, smem, anywhere, anywhere, anywhere],
        out_specs=vmem,
        scratch_shapes=[
            pltpu.VMEM((3, rows, fine_qkv.shape[3]), bf16),
            pltpu.VMEM(held.shape, bf16),
            pltpu.VMEM(held.shape, bf16),
            pltpu.VMEM(out_proj.shape, bf16),
            pltpu.VMEM((tiles, LANES), jnp.int32),
            pltpu.SMEM((tiles, LANES), jnp.int32),
            pltpu.VMEM((tiles, capacity) + held.shape[1:], bf16),
            pltpu.VMEM((tiles * capacity,) + held.shape[1:], bf16),
            pltpu.VMEM((rows, depth), bf16),
            pltpu.VMEM((rows, depth), bf16),
            pltpu.VMEM((chunks, rows // 2, columns // chunks), bf16),
            pltpu.VMEM((chunks, rows // 2, columns // chunks), bf16),
            pltpu.VMEM((chunks, rows // 2, columns // chunks), jnp.float32),
            dma((3,)),
            dma,
            dma,
            dma,
            pltpu.SemaphoreType.REGULAR,
            dma((tiles,)),
            dma((tiles,)),
            dma((tiles,)),
            dma((tiles,)),
            dma((blocks,)),
            dma((blocks,)),
            dma((chunks,)),
            dma((chunks,)),
        ],
        compiler_params=pltpu.CompilerParams(
            collective_id=0, has_side_effects=True, vmem_limit_bytes=56 * 1024 * 1024
        ),
        name="merging",
    )(requests, slots, fine_qkv.transpose(0, 2, 1, 3)[0], held, out_proj)
    return merged[None]


def column_kernel(
    cfg,
    owners_ref,
    picks_ref,
    fine_hbm,
    held_hbm,
    proj_hbm,
    out_ref,
    fine_ref,
    ask_ref,
    asked_ref,
    query_ref,
    near_ref,
    near_lse,
    give_ref,
    give_lse,
    take_ref,
    take_lse,
    att_ref,
    moved_ref,
    proj_ref,
    total_ref,
    load_sem,
    bank_sem,
    list_send,
    list_recv,
    proj_send,
    proj_recv,
    up_send,
    up_recv,
    over_send,
    over_recv,
    pass_send,
    pass_recv,
    qup_send,
    qup_recv,
    qside_send,
    qside_recv,
    give_send,
    take_recv,
    lse_send,
    lse_recv,
    hop_send,
    hop_recv,
    *bank_refs,
):
    segments, heads, blocks, lists, panel, width, picks, chunks = cfg
    tile = lax.axis_index("tile")
    segment = lax.axis_index("segment")
    core = lax.axis_index("mp")
    plane = tile // 2
    column = lax.rem(tile, 2)
    inner = jnp.logical_or(plane == 1, plane == 2)
    outer = jnp.logical_not(inner)
    low = plane < 2
    server = jnp.where(low, 2, 4) + column
    server_side = jnp.where(low, 2, 4) + 1 - column
    buddy = jnp.where(low, 0, 6) + column
    buddy_side = jnp.where(low, 0, 6) + 1 - column
    cross = jnp.where(plane == 1, tile + 2, tile - 2)
    nxt = lax.rem(segment + 1, segments)
    half = blocks * panel // 2
    scale = 1.0 / math.sqrt(width)
    far_away = -1e30

    def at(where_to):
        return (segment, where_to, core)

    def remote(src, dst, send, recv, device):
        return pltpu.make_async_remote_copy(
            src_ref=src,
            dst_ref=dst,
            send_sem=send,
            recv_sem=recv,
            device_id=device,
            device_id_type=MESH,
        )

    def held_of(head):
        return held_hbm.at[:, head]

    def fine_cols(part, head):
        return fine_hbm.at[part, :, pl.ds(head * width, width)]

    def bank_of(head, which):
        return bank_refs[head].at[pl.ds(which * picks, picks)]

    def up(head):
        return remote(
            held_of(head), bank_of(head, plane), up_send.at[head], up_recv.at[head], at(server)
        )

    def over(head):
        return remote(
            held_of(head), bank_of(head, plane), over_send.at[head], over_recv.at[head], at(cross)
        )

    def passed(head):
        far = buddy // 2
        return remote(
            bank_of(head, far), bank_of(head, far), pass_send.at[head], pass_recv.at[head], at(cross)
        )

    def q_up(head):
        return remote(
            fine_cols(0, head), query_ref.at[2, head], qup_send.at[head], qup_recv.at[head], at(server)
        )

    def q_side(head):
        return remote(
            fine_cols(0, head),
            query_ref.at[1, head],
            qside_send.at[1, head],
            qside_recv.at[1, head],
            at(server_side),
        )

    def q_pass(head):
        return remote(
            query_ref.at[2, head],
            query_ref.at[0, head],
            qside_send.at[0, head],
            qside_recv.at[0, head],
            at(server_side),
        )

    def own_bank(head):
        return pltpu.make_async_copy(held_of(head), bank_of(head, plane), bank_sem.at[head])

    def own_query(head):
        return pltpu.make_async_copy(
            fine_cols(0, head), query_ref.at[3, head], bank_sem.at[heads + head]
        )

    def ask(place, device):
        return remote(
            ask_ref, asked_ref.at[place], list_send.at[place], list_recv.at[place], device
        )

    proj_load = pltpu.make_async_copy(proj_hbm, proj_ref.at[:, core], load_sem.at[1])
    proj_swap = remote(
        proj_hbm, proj_ref.at[:, core], proj_send, proj_recv, (segment, tile, 1 - core)
    )
    fine_load = pltpu.make_async_copy(fine_hbm, fine_ref, load_sem.at[0])
    fine_load.start()

    barrier = pltpu.get_barrier_semaphore()

    def greet(device):
        pl.semaphore_signal(barrier, inc=1, device_id=device, device_id_type=MESH)

    greet((nxt, tile, core))
    greet((nxt, tile, 1 - core))
    greet((segment, tile, 1 - core))
    greet(at(server_side))

    @pl.when(outer)
    def _():
        greet(at(server))
        pl.semaphore_wait(barrier, 5)
        for head in range(AHEAD):
            up(head).start()
            q_up(head).start()

    @pl.when(inner)
    def _():
        greet(at(buddy))
        greet(at(buddy_side))
        greet(at(cross))
        pl.semaphore_wait(barrier, 7)
        over(0).start()
        q_side(0).start()
        for head in range(heads):
            own_bank(head).start()
            own_query(head).start()

    def pack(block, carry):
        for head in range(heads):
            for entry in range(lists):
                owner = owners_ref[0, 0, block, entry, head]
                pick = picks_ref[0, 0, block, entry, head]
                place = (head * blocks + block) * lists + entry
                code = (owner - lax.rem(owner, 2)) * picks + pick * 2 + lax.rem(owner, 2)
                ask_ref[place] = code
                asked_ref[3, place] = code
        return carry

    lax.fori_loop(0, blocks, pack, 0)

    @pl.when(outer)
    def _():
        ask(2, at(server)).start()
        ask(0, at(server_side)).start()

    @pl.when(inner)
    def _():
        ask(1, at(server_side)).start()
        up(0).wait_recv()
        passed(0).start()
        over(1).start()
        q_up(0).wait_recv()
        q_pass(0).start()
        q_side(1).start()

    proj_load.start()
    proj_swap.start()
    lane = lax.broadcasted_iota(jnp.int32, (panel, LANES), 1)

    def partials(queries, keys, values, biases):
        scores = []
        for place in range(blocks):
            score = (
                lax.dot_general(
                    queries[place],
                    keys[place],
                    (((1,), (1,)), ((), ())),
                    preferred_element_type=jnp.float32,
                )
                * scale
            )
            scores.append(score if biases is None else score + biases[place])
        stat = jnp.ones((panel, LANES), jnp.float32)
        weights, inverses = [], []
        for place in range(blocks):
            top = jnp.max(scores[place], axis=-1, keepdims=True)
            exponent = jnp.exp(scores[place] - top)
            total = jnp.sum(exponent, axis=-1, keepdims=True)
            weights.append(exponent.astype(jnp.bfloat16))
            inverses.append(1.0 / total)
            stat = jnp.where(lane == place, top, stat)
            stat = jnp.where(lane == 8 + place, total, stat)
        outs = []
        for place in range(blocks):
            outs.append(
                (
                    jnp.dot(weights[place], values[place], preferred_element_type=jnp.float32)
                    * inverses[place]
                ).astype(jnp.bfloat16)
            )
        turned = jnp.concatenate([stat, stat], axis=0).T
        return outs, turned[0:8] + jnp.log(turned[8:16])

    def rows_of(place):
        return slice(place * panel, (place + 1) * panel)

    fine_load.wait()

    def attend_fine(head, carry):
        cols = pl.ds(pl.multiple_of(head * width, width), width)
        outs, lse = partials(
            [fine_ref[0, rows_of(place), cols] for place in range(blocks)],
            [fine_ref[1, rows_of(place), cols] for place in range(blocks)],
            [fine_ref[2, rows_of(place), cols] for place in range(blocks)],
            None,
        )
        for place in range(blocks):
            near_ref[head, rows_of(place)] = outs[place]
        near_lse[head] = lse
        return carry

    lax.fori_loop(0, heads, attend_fine, 0)

    def give(place, head):
        goal = jnp.where(place == 0, buddy_side, jnp.where(place == 1, server_side, buddy))
        land = jnp.where(place == 2, 0, 1)
        return (
            remote(
                give_ref.at[place, head],
                take_ref.at[land, head],
                give_send.at[place, head],
                take_recv.at[land, head],
                at(goal),
            ),
            remote(
                give_lse.at[place, head],
                take_lse.at[land, head],
                lse_send.at[place, head],
                lse_recv.at[land, head],
                at(goal),
            ),
        )

    def take(land, head):
        return (
            remote(
                give_ref.at[0, head],
                take_ref.at[land, head],
                give_send.at[0, head],
                take_recv.at[land, head],
                at(server_side),
            ),
            remote(
                give_lse.at[0, head],
                take_lse.at[land, head],
                lse_send.at[0, head],
                lse_recv.at[land, head],
                at(server_side),
            ),
        )

    def attend(head):
        bank = bank_refs[head]

        def one_tile(place, carry):
            queries, keys, values, biases = [], [], [], []
            for block in range(blocks):
                codes = [
                    asked_ref[place, (head * blocks + block) * lists + entry]
                    for entry in range(lists)
                ]
                queries.append(query_ref[place, head, rows_of(block)])
                keys.append(
                    jnp.concatenate([bank[lax.div(code, 2), 0] for code in codes], axis=0)
                )
                values.append(
                    jnp.concatenate([bank[lax.div(code, 2), 1] for code in codes], axis=0)
                )
                there = [
                    jnp.where(lax.rem(code, 2) == column, 0.0, far_away) for code in codes
                ]
                biases.append(jnp.where(lane < panel, there[0], there[1]))
            outs, lse = partials(queries, keys, values, biases)
            for block in range(blocks):
                give_ref[place, head, rows_of(block)] = outs[block]
            give_lse[place, head] = lse

            @pl.when(place < 3)
            def _():
                for copy in give(place, head):
                    copy.start()

            return carry

        lax.fori_loop(0, 4, one_tile, 0)

    def merge(head, first, first_lse, second, second_lse):
        top = jnp.maximum(jnp.maximum(near_lse[head], first_lse), second_lse)
        shares = [jnp.exp(lse - top) for lse in (near_lse[head], first_lse, second_lse)]
        inverse = 1.0 / (shares[0] + shares[1] + shares[2])
        shares = [share * inverse for share in shares]
        turned = jnp.concatenate(
            shares + [jnp.zeros((LANES - 24, LANES), jnp.float32)], axis=0
        ).T[:panel]
        for block in range(blocks):
            rows = rows_of(block)
            total = near_ref[head, rows].astype(jnp.float32) * turned[:, block : block + 1]
            total = total + first(rows).astype(jnp.float32) * turned[:, 8 + block : 9 + block]
            total = total + second(rows).astype(jnp.float32) * turned[:, 16 + block : 17 + block]
            att_ref[head, rows] = total.astype(jnp.bfloat16)

    def hop(which, head):
        goal = core if which == 0 else 1 - core
        return remote(
            att_ref.at[head, pl.ds(pl.multiple_of(goal * half, half), half)],
            moved_ref.at[head, :, pl.ds(pl.multiple_of(core * width, width), width)],
            hop_send.at[which, head],
            hop_recv.at[which, head],
            (nxt, tile, goal),
        )

    def landed(which, head):
        source = core if which == 0 else 1 - core
        return remote(
            att_ref.at[head, pl.ds(0, half)],
            moved_ref.at[head, :, pl.ds(pl.multiple_of(source * width, width), width)],
            hop_send.at[which, head],
            hop_recv.at[which, head],
            (nxt, tile, source),
        )

    step_cols = out_ref.shape[1] // chunks

    def project(head):
        for which in range(2):
            landed(which, head).wait_recv()
        if head == 0:
            proj_load.wait()
            proj_swap.wait()

        def one_chunk(chunk, carry):
            cols = pl.ds(pl.multiple_of(chunk * step_cols, LANES), step_cols)
            product = jnp.dot(
                moved_ref[head],
                proj_ref[head, :, :, cols].reshape(2 * width, step_cols),
                preferred_element_type=jnp.float32,
            )
            if head == 0:
                total_ref[chunk] = product
            elif head < heads - 1:
                total_ref[chunk] += product
            else:
                out_ref[:, cols] = (total_ref[chunk] + product).astype(jnp.bfloat16)
            return carry

        lax.fori_loop(0, chunks, one_chunk, 0)

    def finish(head):
        @pl.when(inner)
        def _():
            for copy in take(1, head):
                copy.wait_recv()
            merge(
                head,
                lambda rows: give_ref[3, head, rows],
                give_lse[3, head],
                lambda rows: take_ref[1, head, rows],
                take_lse[1, head],
            )
            hop(0, head).start()
            hop(1, head).start()

        @pl.when(outer)
        def _():
            for land in range(2):
                for copy in take(land, head):
                    copy.wait_recv()
            merge(
                head,
                lambda rows: take_ref[0, head, rows],
                take_lse[0, head],
                lambda rows: take_ref[1, head, rows],
                take_lse[1, head],
            )
            hop(0, head).start()
            hop(1, head).start()

    @pl.when(inner)
    def _():
        for place in range(3):
            ask(place, at(server_side)).wait_recv()

    for head in range(heads):
        @pl.when(inner)
        def _():
            if head + 1 < heads:
                up(head + 1).wait_recv()
                passed(head + 1).start()
            if head + 2 < heads:
                over(head + 2).start()
            if head + 1 < heads:
                q_up(head + 1).wait_recv()
                q_pass(head + 1).start()
            if head + 2 < heads:
                q_side(head + 2).start()
            own_bank(head).wait()
            own_query(head).wait()
            over(head).wait_recv()
            passed(head).wait_recv()
            q_side(head).wait_recv()
            q_pass(head).wait_recv()
            attend(head)

        @pl.when(outer)
        def _():
            if head + AHEAD < heads:
                up(head + AHEAD).start()
                q_up(head + AHEAD).start()

        if head >= 1:
            finish(head - 1)
        if head >= 2:
            project(head - 2)
    finish(heads - 1)
    project(heads - 2)
    project(heads - 1)

    for head in range(heads):
        hop(0, head).wait_send()
        hop(1, head).wait_send()

        @pl.when(outer)
        def _():
            up(head).wait_send()
            q_up(head).wait_send()

        @pl.when(inner)
        def _():
            over(head).wait_send()
            passed(head).wait_send()
            q_side(head).wait_send()
            q_pass(head).wait_send()
            for place in range(3):
                for copy in give(place, head):
                    copy.wait_send()

    @pl.when(outer)
    def _():
        ask(2, at(server)).wait_send()
        ask(0, at(server_side)).wait_send()

    @pl.when(inner)
    def _():
        ask(1, at(server_side)).wait_send()


def by_columns(fine_qkv, panels, owners, picks, out_proj):
    segments = lax.axis_size("segment")
    heads, blocks, lists = owners.shape[2:]
    rows = fine_qkv.shape[1]
    held = panels[0]
    each, _, _, panel, width = held.shape
    planes = lax.axis_size("tile") // 2
    columns = out_proj.shape[1]
    chunks = 5
    smem = pl.BlockSpec(memory_space=pltpu.SMEM)
    vmem = pl.BlockSpec(memory_space=pltpu.VMEM)
    anywhere = pl.BlockSpec(memory_space=pl.ANY)
    cfg = (segments, heads, blocks, lists, panel, width, each, chunks)
    dma = pltpu.SemaphoreType.DMA
    bf16 = jnp.bfloat16
    merged = pl.pallas_call(
        functools.partial(column_kernel, cfg),
        out_shape=jax.ShapeDtypeStruct((rows // 2, columns), bf16),
        in_specs=[smem, smem, anywhere, anywhere, anywhere],
        out_specs=vmem,
        scratch_shapes=[
            pltpu.VMEM((3, rows, fine_qkv.shape[3]), bf16),
            pltpu.SMEM((LANES,), jnp.int32),
            pltpu.SMEM((4, LANES), jnp.int32),
            pltpu.VMEM((4, heads, rows, width), bf16),
            pltpu.VMEM((heads, rows, width), bf16),
            pltpu.VMEM((heads, 8, LANES), jnp.float32),
            pltpu.VMEM((4, heads, rows, width), bf16),
            pltpu.VMEM((4, heads, 8, LANES), jnp.float32),
            pltpu.VMEM((2, heads, rows, width), bf16),
            pltpu.VMEM((2, heads, 8, LANES), jnp.float32),
            pltpu.VMEM((heads, rows, width), bf16),
            pltpu.VMEM((heads, rows // 2, 2 * width), bf16),
            pltpu.VMEM((heads, 2, width, columns), bf16),
            pltpu.VMEM((chunks, rows // 2, columns // chunks), jnp.float32),
            dma((2,)),
            dma((2 * heads,)),
            dma((3,)),
            dma((3,)),
            dma,
            dma,
            dma((heads,)),
            dma((heads,)),
            dma((heads,)),
            dma((heads,)),
            dma((heads,)),
            dma((heads,)),
            dma((heads,)),
            dma((heads,)),
            dma((2, heads)),
            dma((2, heads)),
            dma((3, heads)),
            dma((2, heads)),
            dma((3, heads)),
            dma((2, heads)),
            dma((2, heads)),
            dma((2, heads)),
        ]
        + [pltpu.VMEM((planes * each,) + held.shape[2:], bf16) for _ in range(heads)],
        compiler_params=pltpu.CompilerParams(
            collective_id=1, has_side_effects=True, vmem_limit_bytes=56 * 1024 * 1024
        ),
        name="columns",
    )(
        owners.transpose(0, 1, 3, 4, 2),
        picks.transpose(0, 1, 3, 4, 2),
        fine_qkv.transpose(0, 2, 1, 3)[0],
        held,
        out_proj.reshape(heads, width, columns),
    )
    return merged[None]


def solution(mesh):
    placed = (
        P("segment", "tile", None, "mp"),
        P("segment", "tile", "mp", None, None, None),
        P("segment", "tile", "mp", None, None),
        P("segment", "tile", "mp", None, None),
        P("mp", None),
    )
    small = mesh.shape["tile"] == 8 and mesh.shape["segment"] == 2
    return jax.shard_map(
        by_columns if small else on_device,
        mesh=mesh,
        in_specs=placed,
        out_specs=P("segment", ("tile", "mp"), None),
        check_vma=False,
    )
```

```python
import functools
import math

import jax
import jax.numpy as jnp
from jax import lax
from jax.experimental import pallas as pl
from jax.experimental.pallas import tpu as pltpu
from jax.sharding import PartitionSpec as P

MESH = pl.DeviceIdType.MESH
LANES = 128
AHEAD = 2


def request_kernel(capacity, owners_ref, picks_ref, req_ref, slot_ref, count_ref):
    tiles = req_ref.shape[0]
    blocks, lists, heads = owners_ref.shape[2:]
    for tile in range(tiles):
        count_ref[tile] = 0

    def clear(tile, carry):
        for rank in range(capacity):
            req_ref[tile, rank] = 0
        return carry

    lax.fori_loop(0, tiles, clear, 0)
    for head in range(heads):
        for block in range(blocks):
            for entry in range(lists):
                owner = owners_ref[0, 0, block, entry, head]
                rank = count_ref[owner]
                count_ref[owner] = rank + 1
                req_ref[owner, rank] = picks_ref[0, 0, block, entry, head] * heads + head
                slot_ref[(head * blocks + block) * lists + entry] = owner * capacity + rank


def main_kernel(
    cfg,
    req_ref,
    slot_ref,
    fine_hbm,
    held_hbm,
    proj_hbm,
    out_ref,
    fine_ref,
    held_ref,
    relay_ref,
    proj_ref,
    asked_ref,
    asked_smem,
    serve_ref,
    recv_ref,
    att_ref,
    moved_ref,
    psend_ref,
    precv_ref,
    total_ref,
    load_sem,
    smem_sem,
    relay_send,
    relay_recv,
    gate_sem,
    req_send,
    req_recv,
    pan_send,
    pan_recv,
    x_send,
    x_recv,
    mp_send,
    mp_recv,
):
    tiles, segments, capacity, heads, blocks, lists, panel, width, chunks = cfg
    tile = lax.axis_index("tile")
    segment = lax.axis_index("segment")
    core = lax.axis_index("mp")
    half_blocks = blocks // 2
    half = half_blocks * panel
    scale = 1.0 / math.sqrt(width)

    loads = [
        pltpu.make_async_copy(held_hbm, held_ref, load_sem.at[0]),
        pltpu.make_async_copy(fine_hbm, fine_ref, load_sem.at[1]),
        pltpu.make_async_copy(proj_hbm, proj_ref, load_sem.at[2]),
    ]
    for load in loads:
        load.start()

    nxt = lax.rem(segment + 1, segments)
    prv = lax.rem(segment + segments - 1, segments)
    barrier = pltpu.get_barrier_semaphore()

    def greet(step, carry):
        pl.semaphore_signal(
            barrier,
            inc=1,
            device_id=(segment, lax.rem(tile + step, tiles), core),
            device_id_type=MESH,
        )
        return carry

    lax.fori_loop(1, tiles, greet, 0)
    pl.semaphore_signal(barrier, inc=1, device_id=(nxt, tile, core), device_id_type=MESH)
    pl.semaphore_signal(barrier, inc=1, device_id=(prv, tile, core), device_id_type=MESH)
    pl.semaphore_signal(barrier, inc=1, device_id=(segment, tile, 1 - core), device_id_type=MESH)
    pl.semaphore_wait(barrier, tiles + 2)

    half_tiles = tiles // 2
    quarter = tiles // 4
    plane = tile // quarter
    inner = jnp.logical_or(plane == 1, plane == 2)
    partner = jnp.where(plane == 1, tile + quarter, tile - quarter)
    base = (tile // half_tiles) * half_tiles
    far_base = half_tiles - base

    def near_tile(step):
        return base + lax.rem(tile - base + step, half_tiles)

    def far_tile(step):
        return far_base + lax.rem(tile - base + step, half_tiles)

    def mirror(row):
        return lax.rem(row + half_tiles, tiles)

    relay_copy = pltpu.make_async_remote_copy(
        src_ref=held_hbm,
        dst_ref=relay_ref,
        send_sem=relay_send,
        recv_sem=relay_recv,
        device_id=(segment, jnp.where(inner, partner, mirror(tile)), core),
        device_id_type=MESH,
    )

    def request_copy(owner, server, row):
        return pltpu.make_async_remote_copy(
            src_ref=req_ref.at[owner],
            dst_ref=asked_ref.at[row],
            send_sem=req_send.at[owner],
            recv_sem=req_recv.at[row],
            device_id=(segment, server, core),
            device_id_type=MESH,
        )

    def far_request(owner):
        far_plane = owner // quarter
        relayed = jnp.logical_or(far_plane == 1, far_plane == 2)
        through = jnp.where(far_plane == 1, owner + quarter, owner - quarter)
        return request_copy(
            owner, jnp.where(relayed, through, owner), jnp.where(relayed, mirror(tile), tile)
        )

    def start_near(step, carry):
        owner = near_tile(step)
        request_copy(owner, owner, tile).start()
        return carry

    def start_far(step, carry):
        owner = far_tile(step)

        @pl.when(jnp.logical_not(jnp.logical_and(inner, owner == partner)))
        def _():
            far_request(owner).start()

        return carry

    def sent_near(step, carry):
        owner = near_tile(step)
        request_copy(owner, owner, owner).wait_send()
        return carry

    def sent_far(step, carry):
        owner = far_tile(step)

        @pl.when(jnp.logical_not(jnp.logical_and(inner, owner == partner)))
        def _():
            far_request(owner).wait_send()

        return carry

    def wait_near(step, carry):
        owner = near_tile(step)
        request_copy(owner, owner, owner).wait_recv()
        return carry

    def wait_far(step, carry):
        owner = far_tile(step)

        @pl.when(jnp.logical_not(jnp.logical_and(inner, owner == mirror(tile))))
        def _():
            request_copy(owner, owner, owner).wait_recv()

        return carry

    lax.fori_loop(1, half_tiles, start_near, 0)
    lax.fori_loop(0, half_tiles, start_far, 0)
    asked_ref[tile] = req_ref[tile]

    @pl.when(inner)
    def _():
        asked_ref[mirror(tile)] = req_ref[partner]

    lax.fori_loop(1, half_tiles, sent_near, 0)
    lax.fori_loop(0, half_tiles, sent_far, 0)

    @pl.when(inner)
    def _():
        relay_copy.start()

    loads[0].wait()
    lax.fori_loop(1, half_tiles, wait_near, 0)
    lax.fori_loop(0, half_tiles, wait_far, 0)
    to_smem = pltpu.make_async_copy(asked_ref, asked_smem, smem_sem)
    to_smem.start()
    to_smem.wait()

    def panel_copy(row, dest, owner):
        return pltpu.make_async_remote_copy(
            src_ref=serve_ref.at[row],
            dst_ref=recv_ref.at[pl.ds(owner * capacity, capacity)],
            send_sem=pan_send.at[row],
            recv_sem=pan_recv.at[owner],
            device_id=(segment, dest, core),
            device_id_type=MESH,
        )

    def pack(bank_ref, row):
        for rank in range(capacity):
            serve_ref[row, rank] = bank_ref[asked_smem[row, rank]]

    def serve_near(step, carry):
        dest = near_tile(step)
        pack(held_ref, dest)
        panel_copy(dest, dest, tile).start()
        return carry

    def pack_far(step, carry):
        pack(held_ref, far_tile(step))
        return carry

    def start_far_panels(step, carry):
        dest = far_tile(step)
        panel_copy(dest, dest, tile).start()
        return carry

    def serve_relay(step, carry):
        dest = near_tile(step)
        pack(relay_ref, mirror(dest))
        panel_copy(mirror(dest), dest, partner).start()
        return carry

    lax.fori_loop(1, half_tiles, serve_near, 0)
    for rank in range(capacity):
        recv_ref[tile * capacity + rank] = held_ref[asked_smem[tile, rank]]

    @pl.when(jnp.logical_not(inner))
    def _():
        lax.fori_loop(0, half_tiles, pack_far, 0)
        pl.semaphore_wait(gate_sem, 1)
        lax.fori_loop(0, half_tiles, start_far_panels, 0)

    @pl.when(inner)
    def _():
        relay_copy.wait_recv()
        pl.semaphore_signal(
            gate_sem, inc=1, device_id=(segment, mirror(tile), core), device_id_type=MESH
        )
        lax.fori_loop(1, half_tiles, serve_relay, 0)
        for rank in range(capacity):
            recv_ref[partner * capacity + rank] = relay_ref[asked_smem[mirror(tile), rank]]
        relay_copy.wait_send()

    loads[1].wait()
    loads[2].wait()

    def land_near(step, carry):
        peer = near_tile(step)
        copy = panel_copy(peer, peer, peer)
        copy.wait_send()
        copy.wait_recv()
        return carry

    def land_far(step, carry):
        peer = far_tile(step)

        @pl.when(jnp.logical_not(jnp.logical_and(inner, peer == mirror(tile))))
        def _():
            panel_copy(peer, peer, peer).wait_send()

        @pl.when(jnp.logical_not(jnp.logical_and(inner, peer == partner)))
        def _():
            panel_copy(peer, peer, peer).wait_recv()

        return carry

    lax.fori_loop(1, half_tiles, land_near, 0)
    lax.fori_loop(0, half_tiles, land_far, 0)

    def attend(block, group):
        rows = pl.ds(pl.multiple_of(block * panel, panel), panel)
        scores, values = [], []
        for head in group:
            cols = slice(head * width, (head + 1) * width)
            keys, vals = [fine_ref[1, rows, cols]], [fine_ref[2, rows, cols]]
            for entry in range(lists):
                slot = slot_ref[(head * blocks + block) * lists + entry]
                keys.append(recv_ref[slot, 0])
                vals.append(recv_ref[slot, 1])
            values.append(jnp.concatenate(vals, axis=0))
            scores.append(
                lax.dot_general(
                    fine_ref[0, rows, cols],
                    jnp.concatenate(keys, axis=0),
                    (((1,), (1,)), ((), ())),
                    preferred_element_type=jnp.float32,
                )
                * scale
            )
        weights = []
        for score in scores:
            exponent = jnp.exp(score - jnp.max(score, axis=-1, keepdims=True))
            inverse = 1.0 / jnp.sum(exponent, axis=-1, keepdims=True)
            weights.append((exponent * inverse).astype(jnp.bfloat16))
        for at, head in enumerate(group):
            att_ref[rows, head * width : (head + 1) * width] = jnp.dot(
                weights[at], values[at], preferred_element_type=jnp.float32
            ).astype(jnp.bfloat16)

    def hop(place):
        rows = pl.ds(pl.multiple_of((theirs + place) * panel, panel), panel)
        return pltpu.make_async_remote_copy(
            src_ref=att_ref.at[rows],
            dst_ref=moved_ref.at[rows],
            send_sem=x_send.at[place],
            recv_sem=x_recv.at[place],
            device_id=(nxt, tile, core),
            device_id_type=MESH,
        )

    theirs = (1 - core) * half_blocks
    mine = core * half_blocks
    mine_rows = pl.ds(pl.multiple_of(mine * panel, panel), half)
    theirs_rows = pl.ds(pl.multiple_of(theirs * panel, panel), half)
    groups = (tuple(range(heads - 2)), tuple(range(heads - 2, heads)))

    def hop_mine(at):
        group = groups[at]
        cols = pl.ds(group[0] * width, len(group) * width)
        return pltpu.make_async_remote_copy(
            src_ref=att_ref.at[mine_rows, cols],
            dst_ref=moved_ref.at[mine_rows, cols],
            send_sem=x_send.at[half_blocks + at],
            recv_sem=x_recv.at[half_blocks + at],
            device_id=(nxt, tile, core),
            device_id_type=MESH,
        )

    def send_theirs(place, carry):
        attend(theirs + place, tuple(range(heads)))
        hop(place).start()
        return carry

    lax.fori_loop(0, half_blocks, send_theirs, 0)
    for at in range(2):
        def attend_mine(place, carry):
            attend(mine + place, groups[at])
            return carry

        lax.fori_loop(0, half_blocks, attend_mine, 0)
        hop_mine(at).start()

    step_cols = proj_ref.shape[1] // chunks

    def product(rows, group, chunk):
        depth = slice(group[0] * width, (group[-1] + 1) * width)
        return jnp.dot(
            moved_ref[rows, depth],
            proj_ref[depth, chunk * step_cols : (chunk + 1) * step_cols],
            preferred_element_type=jnp.float32,
        )

    def swap(chunk):
        return pltpu.make_async_remote_copy(
            src_ref=psend_ref.at[chunk],
            dst_ref=precv_ref.at[chunk],
            send_sem=mp_send.at[chunk],
            recv_sem=mp_recv.at[chunk],
            device_id=(segment, tile, 1 - core),
            device_id_type=MESH,
        )

    for place in range(half_blocks):
        hop(place).wait()
    for chunk in range(chunks):
        psend_ref[chunk] = product(theirs_rows, tuple(range(heads)), chunk).astype(jnp.bfloat16)
        swap(chunk).start()
    hop_mine(0).wait()
    for chunk in range(chunks):
        total_ref[chunk] = product(mine_rows, groups[0], chunk)
    for chunk in range(chunks):
        swap(chunk).wait()
    hop_mine(1).wait()
    for chunk in range(chunks):
        own = (total_ref[chunk] + product(mine_rows, groups[1], chunk)).astype(jnp.bfloat16)
        out_ref[:, chunk * step_cols : (chunk + 1) * step_cols] = (
            own.astype(jnp.float32) + precv_ref[chunk].astype(jnp.float32)
        ).astype(jnp.bfloat16)


def on_device(fine_qkv, panels, owners, picks, out_proj):
    tiles = lax.axis_size("tile")
    segments = lax.axis_size("segment")
    heads, blocks, lists = owners.shape[2:]
    entries = heads * blocks * lists
    capacity = max(2, (entries + tiles - 1) // tiles)
    rows = fine_qkv.shape[1]
    held = panels.reshape((-1,) + panels.shape[3:])
    panel, width = held.shape[-2:]
    depth, columns = out_proj.shape
    chunks = 5
    smem = pl.BlockSpec(memory_space=pltpu.SMEM)
    vmem = pl.BlockSpec(memory_space=pltpu.VMEM)
    anywhere = pl.BlockSpec(memory_space=pl.ANY)
    requests, slots = pl.pallas_call(
        functools.partial(request_kernel, capacity),
        out_shape=(
            jax.ShapeDtypeStruct((tiles, LANES), jnp.int32),
            jax.ShapeDtypeStruct((entries,), jnp.int32),
        ),
        in_specs=[smem, smem],
        out_specs=(smem, smem),
        scratch_shapes=[pltpu.SMEM((tiles,), jnp.int32)],
        name="requests",
    )(owners.transpose(0, 1, 3, 4, 2), picks.transpose(0, 1, 3, 4, 2))
    cfg = (tiles, segments, capacity, heads, blocks, lists, panel, width, chunks)
    dma = pltpu.SemaphoreType.DMA
    bf16 = jnp.bfloat16
    merged = pl.pallas_call(
        functools.partial(main_kernel, cfg),
        out_shape=jax.ShapeDtypeStruct((rows // 2, columns), bf16),
        in_specs=[vmem, smem, anywhere, anywhere, anywhere],
        out_specs=vmem,
        scratch_shapes=[
            pltpu.VMEM((3, rows, fine_qkv.shape[3]), bf16),
            pltpu.VMEM(held.shape, bf16),
            pltpu.VMEM(held.shape, bf16),
            pltpu.VMEM(out_proj.shape, bf16),
            pltpu.VMEM((tiles, LANES), jnp.int32),
            pltpu.SMEM((tiles, LANES), jnp.int32),
            pltpu.VMEM((tiles, capacity) + held.shape[1:], bf16),
            pltpu.VMEM((tiles * capacity,) + held.shape[1:], bf16),
            pltpu.VMEM((rows, depth), bf16),
            pltpu.VMEM((rows, depth), bf16),
            pltpu.VMEM((chunks, rows // 2, columns // chunks), bf16),
            pltpu.VMEM((chunks, rows // 2, columns // chunks), bf16),
            pltpu.VMEM((chunks, rows // 2, columns // chunks), jnp.float32),
            dma((3,)),
            dma,
            dma,
            dma,
            pltpu.SemaphoreType.REGULAR,
            dma((tiles,)),
            dma((tiles,)),
            dma((tiles,)),
            dma((tiles,)),
            dma((blocks,)),
            dma((blocks,)),
            dma((chunks,)),
            dma((chunks,)),
        ],
        compiler_params=pltpu.CompilerParams(
            collective_id=0, has_side_effects=True, vmem_limit_bytes=56 * 1024 * 1024
        ),
        name="merging",
    )(requests, slots, fine_qkv.transpose(0, 2, 1, 3)[0], held, out_proj)
    return merged[None]


def column_kernel(
    cfg,
    owners_ref,
    picks_ref,
    fine_hbm,
    held_hbm,
    proj_hbm,
    out_ref,
    fine_ref,
    ask_ref,
    asked_ref,
    query_ref,
    near_ref,
    near_lse,
    give_ref,
    give_lse,
    take_ref,
    take_lse,
    att_ref,
    moved_ref,
    proj_ref,
    total_ref,
    load_sem,
    bank_sem,
    list_send,
    list_recv,
    proj_send,
    proj_recv,
    up_send,
    up_recv,
    over_send,
    over_recv,
    pass_send,
    pass_recv,
    qup_send,
    qup_recv,
    qside_send,
    qside_recv,
    give_send,
    take_recv,
    lse_send,
    lse_recv,
    hop_send,
    hop_recv,
    *bank_refs,
):
    segments, heads, blocks, lists, panel, width, picks, chunks = cfg
    tile = lax.axis_index("tile")
    segment = lax.axis_index("segment")
    core = lax.axis_index("mp")
    plane = tile // 2
    column = lax.rem(tile, 2)
    inner = jnp.logical_or(plane == 1, plane == 2)
    outer = jnp.logical_not(inner)
    low = plane < 2
    server = jnp.where(low, 2, 4) + column
    server_side = jnp.where(low, 2, 4) + 1 - column
    buddy = jnp.where(low, 0, 6) + column
    buddy_side = jnp.where(low, 0, 6) + 1 - column
    cross = jnp.where(plane == 1, tile + 2, tile - 2)
    nxt = lax.rem(segment + 1, segments)
    half = blocks * panel // 2
    scale = 1.0 / math.sqrt(width)
    far_away = -1e30

    def at(where_to):
        return (segment, where_to, core)

    def remote(src, dst, send, recv, device):
        return pltpu.make_async_remote_copy(
            src_ref=src,
            dst_ref=dst,
            send_sem=send,
            recv_sem=recv,
            device_id=device,
            device_id_type=MESH,
        )

    def held_of(head):
        return held_hbm.at[:, head]

    def fine_cols(part, head):
        return fine_hbm.at[part, :, pl.ds(head * width, width)]

    def bank_of(head, which):
        return bank_refs[head].at[pl.ds(which * picks, picks)]

    def up(head):
        return remote(
            held_of(head), bank_of(head, plane), up_send.at[head], up_recv.at[head], at(server)
        )

    def over(head):
        return remote(
            held_of(head), bank_of(head, plane), over_send.at[head], over_recv.at[head], at(cross)
        )

    def passed(head):
        far = buddy // 2
        return remote(
            bank_of(head, far), bank_of(head, far), pass_send.at[head], pass_recv.at[head], at(cross)
        )

    def q_up(head):
        return remote(
            fine_cols(0, head), query_ref.at[2, head], qup_send.at[head], qup_recv.at[head], at(server)
        )

    def q_side(head):
        return remote(
            fine_cols(0, head),
            query_ref.at[1, head],
            qside_send.at[1, head],
            qside_recv.at[1, head],
            at(server_side),
        )

    def q_pass(head):
        return remote(
            query_ref.at[2, head],
            query_ref.at[0, head],
            qside_send.at[0, head],
            qside_recv.at[0, head],
            at(server_side),
        )

    def own_bank(head):
        return pltpu.make_async_copy(held_of(head), bank_of(head, plane), bank_sem.at[head])

    def own_query(head):
        return pltpu.make_async_copy(
            fine_cols(0, head), query_ref.at[3, head], bank_sem.at[heads + head]
        )

    def ask(place, device):
        return remote(
            ask_ref, asked_ref.at[place], list_send.at[place], list_recv.at[place], device
        )

    proj_load = pltpu.make_async_copy(proj_hbm, proj_ref.at[:, core], load_sem.at[1])
    proj_swap = remote(
        proj_hbm, proj_ref.at[:, core], proj_send, proj_recv, (segment, tile, 1 - core)
    )
    fine_load = pltpu.make_async_copy(fine_hbm, fine_ref, load_sem.at[0])
    fine_load.start()

    barrier = pltpu.get_barrier_semaphore()

    def greet(device):
        pl.semaphore_signal(barrier, inc=1, device_id=device, device_id_type=MESH)

    greet((nxt, tile, core))
    greet((nxt, tile, 1 - core))
    greet((segment, tile, 1 - core))
    greet(at(server_side))

    @pl.when(outer)
    def _():
        greet(at(server))

    @pl.when(inner)
    def _():
        greet(at(buddy))
        greet(at(buddy_side))
        greet(at(cross))

    def pack(block, carry):
        for head in range(heads):
            for entry in range(lists):
                owner = owners_ref[0, 0, block, entry, head]
                pick = picks_ref[0, 0, block, entry, head]
                place = (head * blocks + block) * lists + entry
                code = (owner - lax.rem(owner, 2)) * picks + pick * 2 + lax.rem(owner, 2)
                ask_ref[place] = code
                asked_ref[3, place] = code
        return carry

    lax.fori_loop(0, blocks, pack, 0)

    @pl.when(outer)
    def _():
        pl.semaphore_wait(barrier, 5)
        ask(2, at(server)).start()
        ask(0, at(server_side)).start()
        q_up(0).start()
        up(0).start()
        for head in range(1, heads):
            up(head).start()
            q_up(head).start()

    @pl.when(inner)
    def _():
        pl.semaphore_wait(barrier, 7)
        ask(1, at(server_side)).start()
        for head in range(AHEAD):
            over(head).start()
            q_side(head).start()
        for head in range(heads):
            own_bank(head).start()
            own_query(head).start()

    def relay(head):
        q_up(head).wait_recv()
        q_pass(head).start()
        up(head).wait_recv()
        passed(head).start()
        if head + AHEAD < heads:
            over(head + AHEAD).start()
            q_side(head + AHEAD).start()

    @pl.when(inner)
    def _():
        relay(0)

    proj_load.start()
    proj_swap.start()
    lane = lax.broadcasted_iota(jnp.int32, (panel, LANES), 1)

    def partials(queries, keys, values, biases):
        scores = []
        for place in range(blocks):
            score = (
                lax.dot_general(
                    queries[place],
                    keys[place],
                    (((1,), (1,)), ((), ())),
                    preferred_element_type=jnp.float32,
                )
                * scale
            )
            scores.append(score if biases is None else score + biases[place])
        stat = jnp.ones((panel, LANES), jnp.float32)
        weights, inverses = [], []
        for place in range(blocks):
            top = jnp.max(scores[place], axis=-1, keepdims=True)
            exponent = jnp.exp(scores[place] - top)
            total = jnp.sum(exponent, axis=-1, keepdims=True)
            weights.append(exponent.astype(jnp.bfloat16))
            inverses.append(1.0 / total)
            stat = jnp.where(lane == place, top, stat)
            stat = jnp.where(lane == 8 + place, total, stat)
        outs = []
        for place in range(blocks):
            outs.append(
                (
                    jnp.dot(weights[place], values[place], preferred_element_type=jnp.float32)
                    * inverses[place]
                ).astype(jnp.bfloat16)
            )
        turned = jnp.concatenate([stat, stat], axis=0).T
        return outs, turned[0:8] + jnp.log(turned[8:16])

    def rows_of(place):
        return slice(place * panel, (place + 1) * panel)

    fine_load.wait()

    def attend_fine(head, carry):
        cols = pl.ds(pl.multiple_of(head * width, width), width)
        outs, lse = partials(
            [fine_ref[0, rows_of(place), cols] for place in range(blocks)],
            [fine_ref[1, rows_of(place), cols] for place in range(blocks)],
            [fine_ref[2, rows_of(place), cols] for place in range(blocks)],
            None,
        )
        for place in range(blocks):
            near_ref[head, rows_of(place)] = outs[place]
        near_lse[head] = lse
        return carry

    lax.fori_loop(0, heads, attend_fine, 0)

    def give(place, head):
        goal = jnp.where(place == 0, buddy_side, jnp.where(place == 1, server_side, buddy))
        land = jnp.where(place == 2, 0, 1)
        return (
            remote(
                give_ref.at[place, head],
                take_ref.at[land, head],
                give_send.at[place, head],
                take_recv.at[land, head],
                at(goal),
            ),
            remote(
                give_lse.at[place, head],
                take_lse.at[land, head],
                lse_send.at[place, head],
                lse_recv.at[land, head],
                at(goal),
            ),
        )

    def take(land, head):
        return (
            remote(
                give_ref.at[0, head],
                take_ref.at[land, head],
                give_send.at[0, head],
                take_recv.at[land, head],
                at(server_side),
            ),
            remote(
                give_lse.at[0, head],
                take_lse.at[land, head],
                lse_send.at[0, head],
                lse_recv.at[land, head],
                at(server_side),
            ),
        )

    def attend(head):
        bank = bank_refs[head]

        def one_tile(place, carry):
            queries, keys, values, biases = [], [], [], []
            for block in range(blocks):
                codes = [
                    asked_ref[place, (head * blocks + block) * lists + entry]
                    for entry in range(lists)
                ]
                queries.append(query_ref[place, head, rows_of(block)])
                keys.append(
                    jnp.concatenate([bank[lax.div(code, 2), 0] for code in codes], axis=0)
                )
                values.append(
                    jnp.concatenate([bank[lax.div(code, 2), 1] for code in codes], axis=0)
                )
                there = [
                    jnp.where(lax.rem(code, 2) == column, 0.0, far_away) for code in codes
                ]
                biases.append(jnp.where(lane < panel, there[0], there[1]))
            outs, lse = partials(queries, keys, values, biases)
            for block in range(blocks):
                give_ref[place, head, rows_of(block)] = outs[block]
            give_lse[place, head] = lse

            @pl.when(place < 3)
            def _():
                for copy in give(place, head):
                    copy.start()

            return carry

        lax.fori_loop(0, 4, one_tile, 0)

    def merge(head, first, first_lse, second, second_lse):
        top = jnp.maximum(jnp.maximum(near_lse[head], first_lse), second_lse)
        shares = [jnp.exp(lse - top) for lse in (near_lse[head], first_lse, second_lse)]
        inverse = 1.0 / (shares[0] + shares[1] + shares[2])
        shares = [share * inverse for share in shares]
        turned = jnp.concatenate(
            shares + [jnp.zeros((LANES - 24, LANES), jnp.float32)], axis=0
        ).T[:panel]
        for block in range(blocks):
            rows = rows_of(block)
            total = near_ref[head, rows].astype(jnp.float32) * turned[:, block : block + 1]
            total = total + first(rows).astype(jnp.float32) * turned[:, 8 + block : 9 + block]
            total = total + second(rows).astype(jnp.float32) * turned[:, 16 + block : 17 + block]
            att_ref[head, rows] = total.astype(jnp.bfloat16)

    def hop(which, head):
        goal = core if which == 0 else 1 - core
        return remote(
            att_ref.at[head, pl.ds(pl.multiple_of(goal * half, half), half)],
            moved_ref.at[head, :, pl.ds(pl.multiple_of(core * width, width), width)],
            hop_send.at[which, head],
            hop_recv.at[which, head],
            (nxt, tile, goal),
        )

    def landed(which, head):
        source = core if which == 0 else 1 - core
        return remote(
            att_ref.at[head, pl.ds(0, half)],
            moved_ref.at[head, :, pl.ds(pl.multiple_of(source * width, width), width)],
            hop_send.at[which, head],
            hop_recv.at[which, head],
            (nxt, tile, source),
        )

    step_cols = out_ref.shape[1] // chunks

    def project(head):
        for which in range(2):
            landed(which, head).wait_recv()
        if head == 0:
            proj_load.wait()
            proj_swap.wait()

        def one_chunk(chunk, carry):
            cols = pl.ds(pl.multiple_of(chunk * step_cols, LANES), step_cols)
            product = jnp.dot(
                moved_ref[head],
                proj_ref[head, :, :, cols].reshape(2 * width, step_cols),
                preferred_element_type=jnp.float32,
            )
            if head == 0:
                total_ref[chunk] = product
            elif head < heads - 1:
                total_ref[chunk] += product
            else:
                out_ref[:, cols] = (total_ref[chunk] + product).astype(jnp.bfloat16)
            return carry

        lax.fori_loop(0, chunks, one_chunk, 0)

    def finish(head):
        @pl.when(inner)
        def _():
            for copy in take(1, head):
                copy.wait_recv()
            merge(
                head,
                lambda rows: give_ref[3, head, rows],
                give_lse[3, head],
                lambda rows: take_ref[1, head, rows],
                take_lse[1, head],
            )
            hop(0, head).start()
            hop(1, head).start()

        @pl.when(outer)
        def _():
            for land in range(2):
                for copy in take(land, head):
                    copy.wait_recv()
            merge(
                head,
                lambda rows: take_ref[0, head, rows],
                take_lse[0, head],
                lambda rows: take_ref[1, head, rows],
                take_lse[1, head],
            )
            hop(0, head).start()
            hop(1, head).start()

    @pl.when(inner)
    def _():
        relay(1)
        for place in range(3):
            ask(place, at(server_side)).wait_recv()

    for head in range(heads):
        @pl.when(inner)
        def _():
            own_bank(head).wait()
            own_query(head).wait()
            over(head).wait_recv()
            passed(head).wait_recv()
            q_side(head).wait_recv()
            q_pass(head).wait_recv()
            attend(head)

        if head >= 1:
            finish(head - 1)
        if head + 2 < heads:
            @pl.when(inner)
            def _():
                relay(head + 2)

        if head >= 2:
            project(head - 2)
    finish(heads - 1)
    project(heads - 2)
    project(heads - 1)

    for head in range(heads):
        hop(0, head).wait_send()
        hop(1, head).wait_send()

        @pl.when(outer)
        def _():
            up(head).wait_send()
            q_up(head).wait_send()

        @pl.when(inner)
        def _():
            over(head).wait_send()
            passed(head).wait_send()
            q_side(head).wait_send()
            q_pass(head).wait_send()
            for place in range(3):
                for copy in give(place, head):
                    copy.wait_send()

    @pl.when(outer)
    def _():
        ask(2, at(server)).wait_send()
        ask(0, at(server_side)).wait_send()

    @pl.when(inner)
    def _():
        ask(1, at(server_side)).wait_send()


def by_columns(fine_qkv, panels, owners, picks, out_proj):
    segments = lax.axis_size("segment")
    heads, blocks, lists = owners.shape[2:]
    rows = fine_qkv.shape[1]
    held = panels[0]
    each, _, _, panel, width = held.shape
    planes = lax.axis_size("tile") // 2
    columns = out_proj.shape[1]
    chunks = 5
    smem = pl.BlockSpec(memory_space=pltpu.SMEM)
    vmem = pl.BlockSpec(memory_space=pltpu.VMEM)
    anywhere = pl.BlockSpec(memory_space=pl.ANY)
    cfg = (segments, heads, blocks, lists, panel, width, each, chunks)
    dma = pltpu.SemaphoreType.DMA
    bf16 = jnp.bfloat16
    merged = pl.pallas_call(
        functools.partial(column_kernel, cfg),
        out_shape=pltpu.VMEM((rows // 2, columns), bf16),
        in_specs=[smem, smem, anywhere, anywhere, anywhere],
        out_specs=vmem,
        scratch_shapes=[
            pltpu.VMEM((3, rows, fine_qkv.shape[3]), bf16),
            pltpu.SMEM((LANES,), jnp.int32),
            pltpu.SMEM((4, LANES), jnp.int32),
            pltpu.VMEM((4, heads, rows, width), bf16),
            pltpu.VMEM((heads, rows, width), bf16),
            pltpu.VMEM((heads, 8, LANES), jnp.float32),
            pltpu.VMEM((4, heads, rows, width), bf16),
            pltpu.VMEM((4, heads, 8, LANES), jnp.float32),
            pltpu.VMEM((2, heads, rows, width), bf16),
            pltpu.VMEM((2, heads, 8, LANES), jnp.float32),
            pltpu.VMEM((heads, rows, width), bf16),
            pltpu.VMEM((heads, rows // 2, 2 * width), bf16),
            pltpu.VMEM((heads, 2, width, columns), bf16),
            pltpu.VMEM((chunks, rows // 2, columns // chunks), jnp.float32),
            dma((2,)),
            dma((2 * heads,)),
            dma((3,)),
            dma((3,)),
            dma,
            dma,
            dma((heads,)),
            dma((heads,)),
            dma((heads,)),
            dma((heads,)),
            dma((heads,)),
            dma((heads,)),
            dma((heads,)),
            dma((heads,)),
            dma((2, heads)),
            dma((2, heads)),
            dma((3, heads)),
            dma((2, heads)),
            dma((3, heads)),
            dma((2, heads)),
            dma((2, heads)),
            dma((2, heads)),
        ]
        + [pltpu.VMEM((planes * each,) + held.shape[2:], bf16) for _ in range(heads)],
        compiler_params=pltpu.CompilerParams(
            collective_id=1, has_side_effects=True, vmem_limit_bytes=56 * 1024 * 1024
        ),
        name="columns",
    )(
        owners.transpose(0, 1, 3, 4, 2),
        picks.transpose(0, 1, 3, 4, 2),
        fine_qkv.transpose(0, 2, 1, 3)[0],
        held,
        out_proj.reshape(heads, width, columns),
    )
    return merged[None]


def solution(mesh):
    placed = (
        P("segment", "tile", None, "mp"),
        P("segment", "tile", "mp", None, None, None),
        P("segment", "tile", "mp", None, None),
        P("segment", "tile", "mp", None, None),
        P("mp", None),
    )
    small = mesh.shape["tile"] == 8 and mesh.shape["segment"] == 2
    return jax.shard_map(
        by_columns if small else on_device,
        mesh=mesh,
        in_specs=placed,
        out_specs=P("segment", ("tile", "mp"), None),
        check_vma=False,
    )
```

```python
import functools
import math

import jax
import jax.numpy as jnp
from jax import lax
from jax.experimental import pallas as pl
from jax.experimental.pallas import tpu as pltpu
from jax.sharding import PartitionSpec as P

MESH = pl.DeviceIdType.MESH
LANES = 128
AHEAD = 2
QUERY_AHEAD = 5


def request_kernel(capacity, owners_ref, picks_ref, req_ref, slot_ref, count_ref):
    tiles = req_ref.shape[0]
    blocks, lists, heads = owners_ref.shape[2:]
    for tile in range(tiles):
        count_ref[tile] = 0

    def clear(tile, carry):
        for rank in range(capacity):
            req_ref[tile, rank] = 0
        return carry

    lax.fori_loop(0, tiles, clear, 0)
    for head in range(heads):
        for block in range(blocks):
            for entry in range(lists):
                owner = owners_ref[0, 0, block, entry, head]
                rank = count_ref[owner]
                count_ref[owner] = rank + 1
                req_ref[owner, rank] = picks_ref[0, 0, block, entry, head] * heads + head
                slot_ref[(head * blocks + block) * lists + entry] = owner * capacity + rank


def main_kernel(
    cfg,
    req_ref,
    slot_ref,
    fine_hbm,
    held_hbm,
    proj_hbm,
    out_ref,
    fine_ref,
    held_ref,
    relay_ref,
    proj_ref,
    asked_ref,
    asked_smem,
    serve_ref,
    recv_ref,
    att_ref,
    moved_ref,
    psend_ref,
    precv_ref,
    total_ref,
    load_sem,
    smem_sem,
    relay_send,
    relay_recv,
    gate_sem,
    req_send,
    req_recv,
    pan_send,
    pan_recv,
    x_send,
    x_recv,
    mp_send,
    mp_recv,
):
    tiles, segments, capacity, heads, blocks, lists, panel, width, chunks = cfg
    tile = lax.axis_index("tile")
    segment = lax.axis_index("segment")
    core = lax.axis_index("mp")
    half_blocks = blocks // 2
    half = half_blocks * panel
    scale = 1.0 / math.sqrt(width)

    loads = [
        pltpu.make_async_copy(held_hbm, held_ref, load_sem.at[0]),
        pltpu.make_async_copy(fine_hbm, fine_ref, load_sem.at[1]),
        pltpu.make_async_copy(proj_hbm, proj_ref, load_sem.at[2]),
    ]
    for load in loads:
        load.start()

    nxt = lax.rem(segment + 1, segments)
    prv = lax.rem(segment + segments - 1, segments)
    barrier = pltpu.get_barrier_semaphore()

    def greet(step, carry):
        pl.semaphore_signal(
            barrier,
            inc=1,
            device_id=(segment, lax.rem(tile + step, tiles), core),
            device_id_type=MESH,
        )
        return carry

    lax.fori_loop(1, tiles, greet, 0)
    pl.semaphore_signal(barrier, inc=1, device_id=(nxt, tile, core), device_id_type=MESH)
    pl.semaphore_signal(barrier, inc=1, device_id=(prv, tile, core), device_id_type=MESH)
    pl.semaphore_signal(barrier, inc=1, device_id=(segment, tile, 1 - core), device_id_type=MESH)
    pl.semaphore_wait(barrier, tiles + 2)

    half_tiles = tiles // 2
    quarter = tiles // 4
    plane = tile // quarter
    inner = jnp.logical_or(plane == 1, plane == 2)
    partner = jnp.where(plane == 1, tile + quarter, tile - quarter)
    base = (tile // half_tiles) * half_tiles
    far_base = half_tiles - base

    def near_tile(step):
        return base + lax.rem(tile - base + step, half_tiles)

    def far_tile(step):
        return far_base + lax.rem(tile - base + step, half_tiles)

    def mirror(row):
        return lax.rem(row + half_tiles, tiles)

    relay_copy = pltpu.make_async_remote_copy(
        src_ref=held_hbm,
        dst_ref=relay_ref,
        send_sem=relay_send,
        recv_sem=relay_recv,
        device_id=(segment, jnp.where(inner, partner, mirror(tile)), core),
        device_id_type=MESH,
    )

    def request_copy(owner, server, row):
        return pltpu.make_async_remote_copy(
            src_ref=req_ref.at[owner],
            dst_ref=asked_ref.at[row],
            send_sem=req_send.at[owner],
            recv_sem=req_recv.at[row],
            device_id=(segment, server, core),
            device_id_type=MESH,
        )

    def far_request(owner):
        far_plane = owner // quarter
        relayed = jnp.logical_or(far_plane == 1, far_plane == 2)
        through = jnp.where(far_plane == 1, owner + quarter, owner - quarter)
        return request_copy(
            owner, jnp.where(relayed, through, owner), jnp.where(relayed, mirror(tile), tile)
        )

    def start_near(step, carry):
        owner = near_tile(step)
        request_copy(owner, owner, tile).start()
        return carry

    def start_far(step, carry):
        owner = far_tile(step)

        @pl.when(jnp.logical_not(jnp.logical_and(inner, owner == partner)))
        def _():
            far_request(owner).start()

        return carry

    def sent_near(step, carry):
        owner = near_tile(step)
        request_copy(owner, owner, owner).wait_send()
        return carry

    def sent_far(step, carry):
        owner = far_tile(step)

        @pl.when(jnp.logical_not(jnp.logical_and(inner, owner == partner)))
        def _():
            far_request(owner).wait_send()

        return carry

    def wait_near(step, carry):
        owner = near_tile(step)
        request_copy(owner, owner, owner).wait_recv()
        return carry

    def wait_far(step, carry):
        owner = far_tile(step)

        @pl.when(jnp.logical_not(jnp.logical_and(inner, owner == mirror(tile))))
        def _():
            request_copy(owner, owner, owner).wait_recv()

        return carry

    lax.fori_loop(1, half_tiles, start_near, 0)
    lax.fori_loop(0, half_tiles, start_far, 0)
    asked_ref[tile] = req_ref[tile]

    @pl.when(inner)
    def _():
        asked_ref[mirror(tile)] = req_ref[partner]

    lax.fori_loop(1, half_tiles, sent_near, 0)
    lax.fori_loop(0, half_tiles, sent_far, 0)

    @pl.when(inner)
    def _():
        relay_copy.start()

    loads[0].wait()
    lax.fori_loop(1, half_tiles, wait_near, 0)
    lax.fori_loop(0, half_tiles, wait_far, 0)
    to_smem = pltpu.make_async_copy(asked_ref, asked_smem, smem_sem)
    to_smem.start()
    to_smem.wait()

    def panel_copy(row, dest, owner):
        return pltpu.make_async_remote_copy(
            src_ref=serve_ref.at[row],
            dst_ref=recv_ref.at[pl.ds(owner * capacity, capacity)],
            send_sem=pan_send.at[row],
            recv_sem=pan_recv.at[owner],
            device_id=(segment, dest, core),
            device_id_type=MESH,
        )

    def pack(bank_ref, row):
        for rank in range(capacity):
            serve_ref[row, rank] = bank_ref[asked_smem[row, rank]]

    def serve_near(step, carry):
        dest = near_tile(step)
        pack(held_ref, dest)
        panel_copy(dest, dest, tile).start()
        return carry

    def pack_far(step, carry):
        pack(held_ref, far_tile(step))
        return carry

    def start_far_panels(step, carry):
        dest = far_tile(step)
        panel_copy(dest, dest, tile).start()
        return carry

    def serve_relay(step, carry):
        dest = near_tile(step)
        pack(relay_ref, mirror(dest))
        panel_copy(mirror(dest), dest, partner).start()
        return carry

    lax.fori_loop(1, half_tiles, serve_near, 0)
    for rank in range(capacity):
        recv_ref[tile * capacity + rank] = held_ref[asked_smem[tile, rank]]

    @pl.when(jnp.logical_not(inner))
    def _():
        lax.fori_loop(0, half_tiles, pack_far, 0)
        pl.semaphore_wait(gate_sem, 1)
        lax.fori_loop(0, half_tiles, start_far_panels, 0)

    @pl.when(inner)
    def _():
        relay_copy.wait_recv()
        pl.semaphore_signal(
            gate_sem, inc=1, device_id=(segment, mirror(tile), core), device_id_type=MESH
        )
        lax.fori_loop(1, half_tiles, serve_relay, 0)
        for rank in range(capacity):
            recv_ref[partner * capacity + rank] = relay_ref[asked_smem[mirror(tile), rank]]
        relay_copy.wait_send()

    loads[1].wait()
    loads[2].wait()

    def land_near(step, carry):
        peer = near_tile(step)
        copy = panel_copy(peer, peer, peer)
        copy.wait_send()
        copy.wait_recv()
        return carry

    def land_far(step, carry):
        peer = far_tile(step)

        @pl.when(jnp.logical_not(jnp.logical_and(inner, peer == mirror(tile))))
        def _():
            panel_copy(peer, peer, peer).wait_send()

        @pl.when(jnp.logical_not(jnp.logical_and(inner, peer == partner)))
        def _():
            panel_copy(peer, peer, peer).wait_recv()

        return carry

    lax.fori_loop(1, half_tiles, land_near, 0)
    lax.fori_loop(0, half_tiles, land_far, 0)

    def attend(block, group):
        rows = pl.ds(pl.multiple_of(block * panel, panel), panel)
        scores, values = [], []
        for head in group:
            cols = slice(head * width, (head + 1) * width)
            keys, vals = [fine_ref[1, rows, cols]], [fine_ref[2, rows, cols]]
            for entry in range(lists):
                slot = slot_ref[(head * blocks + block) * lists + entry]
                keys.append(recv_ref[slot, 0])
                vals.append(recv_ref[slot, 1])
            values.append(jnp.concatenate(vals, axis=0))
            scores.append(
                lax.dot_general(
                    fine_ref[0, rows, cols],
                    jnp.concatenate(keys, axis=0),
                    (((1,), (1,)), ((), ())),
                    preferred_element_type=jnp.float32,
                )
                * scale
            )
        weights = []
        for score in scores:
            exponent = jnp.exp(score - jnp.max(score, axis=-1, keepdims=True))
            inverse = 1.0 / jnp.sum(exponent, axis=-1, keepdims=True)
            weights.append((exponent * inverse).astype(jnp.bfloat16))
        for at, head in enumerate(group):
            att_ref[rows, head * width : (head + 1) * width] = jnp.dot(
                weights[at], values[at], preferred_element_type=jnp.float32
            ).astype(jnp.bfloat16)

    def hop(place):
        rows = pl.ds(pl.multiple_of((theirs + place) * panel, panel), panel)
        return pltpu.make_async_remote_copy(
            src_ref=att_ref.at[rows],
            dst_ref=moved_ref.at[rows],
            send_sem=x_send.at[place],
            recv_sem=x_recv.at[place],
            device_id=(nxt, tile, core),
            device_id_type=MESH,
        )

    theirs = (1 - core) * half_blocks
    mine = core * half_blocks
    mine_rows = pl.ds(pl.multiple_of(mine * panel, panel), half)
    theirs_rows = pl.ds(pl.multiple_of(theirs * panel, panel), half)
    groups = (tuple(range(heads - 2)), tuple(range(heads - 2, heads)))

    def hop_mine(at):
        group = groups[at]
        cols = pl.ds(group[0] * width, len(group) * width)
        return pltpu.make_async_remote_copy(
            src_ref=att_ref.at[mine_rows, cols],
            dst_ref=moved_ref.at[mine_rows, cols],
            send_sem=x_send.at[half_blocks + at],
            recv_sem=x_recv.at[half_blocks + at],
            device_id=(nxt, tile, core),
            device_id_type=MESH,
        )

    def send_theirs(place, carry):
        attend(theirs + place, tuple(range(heads)))
        hop(place).start()
        return carry

    lax.fori_loop(0, half_blocks, send_theirs, 0)
    for at in range(2):
        def attend_mine(place, carry):
            attend(mine + place, groups[at])
            return carry

        lax.fori_loop(0, half_blocks, attend_mine, 0)
        hop_mine(at).start()

    step_cols = proj_ref.shape[1] // chunks

    def product(rows, group, chunk):
        depth = slice(group[0] * width, (group[-1] + 1) * width)
        return jnp.dot(
            moved_ref[rows, depth],
            proj_ref[depth, chunk * step_cols : (chunk + 1) * step_cols],
            preferred_element_type=jnp.float32,
        )

    def swap(chunk):
        return pltpu.make_async_remote_copy(
            src_ref=psend_ref.at[chunk],
            dst_ref=precv_ref.at[chunk],
            send_sem=mp_send.at[chunk],
            recv_sem=mp_recv.at[chunk],
            device_id=(segment, tile, 1 - core),
            device_id_type=MESH,
        )

    for place in range(half_blocks):
        hop(place).wait()
    for chunk in range(chunks):
        psend_ref[chunk] = product(theirs_rows, tuple(range(heads)), chunk).astype(jnp.bfloat16)
        swap(chunk).start()
    hop_mine(0).wait()
    for chunk in range(chunks):
        total_ref[chunk] = product(mine_rows, groups[0], chunk)
    for chunk in range(chunks):
        swap(chunk).wait()
    hop_mine(1).wait()
    for chunk in range(chunks):
        own = (total_ref[chunk] + product(mine_rows, groups[1], chunk)).astype(jnp.bfloat16)
        out_ref[:, chunk * step_cols : (chunk + 1) * step_cols] = (
            own.astype(jnp.float32) + precv_ref[chunk].astype(jnp.float32)
        ).astype(jnp.bfloat16)


def on_device(fine_qkv, panels, owners, picks, out_proj):
    tiles = lax.axis_size("tile")
    segments = lax.axis_size("segment")
    heads, blocks, lists = owners.shape[2:]
    entries = heads * blocks * lists
    capacity = max(2, (entries + tiles - 1) // tiles)
    rows = fine_qkv.shape[1]
    held = panels.reshape((-1,) + panels.shape[3:])
    panel, width = held.shape[-2:]
    depth, columns = out_proj.shape
    chunks = 5
    smem = pl.BlockSpec(memory_space=pltpu.SMEM)
    vmem = pl.BlockSpec(memory_space=pltpu.VMEM)
    anywhere = pl.BlockSpec(memory_space=pl.ANY)
    requests, slots = pl.pallas_call(
        functools.partial(request_kernel, capacity),
        out_shape=(
            jax.ShapeDtypeStruct((tiles, LANES), jnp.int32),
            jax.ShapeDtypeStruct((entries,), jnp.int32),
        ),
        in_specs=[smem, smem],
        out_specs=(smem, smem),
        scratch_shapes=[pltpu.SMEM((tiles,), jnp.int32)],
        name="requests",
    )(owners.transpose(0, 1, 3, 4, 2), picks.transpose(0, 1, 3, 4, 2))
    cfg = (tiles, segments, capacity, heads, blocks, lists, panel, width, chunks)
    dma = pltpu.SemaphoreType.DMA
    bf16 = jnp.bfloat16
    merged = pl.pallas_call(
        functools.partial(main_kernel, cfg),
        out_shape=jax.ShapeDtypeStruct((rows // 2, columns), bf16),
        in_specs=[vmem, smem, anywhere, anywhere, anywhere],
        out_specs=vmem,
        scratch_shapes=[
            pltpu.VMEM((3, rows, fine_qkv.shape[3]), bf16),
            pltpu.VMEM(held.shape, bf16),
            pltpu.VMEM(held.shape, bf16),
            pltpu.VMEM(out_proj.shape, bf16),
            pltpu.VMEM((tiles, LANES), jnp.int32),
            pltpu.SMEM((tiles, LANES), jnp.int32),
            pltpu.VMEM((tiles, capacity) + held.shape[1:], bf16),
            pltpu.VMEM((tiles * capacity,) + held.shape[1:], bf16),
            pltpu.VMEM((rows, depth), bf16),
            pltpu.VMEM((rows, depth), bf16),
            pltpu.VMEM((chunks, rows // 2, columns // chunks), bf16),
            pltpu.VMEM((chunks, rows // 2, columns // chunks), bf16),
            pltpu.VMEM((chunks, rows // 2, columns // chunks), jnp.float32),
            dma((3,)),
            dma,
            dma,
            dma,
            pltpu.SemaphoreType.REGULAR,
            dma((tiles,)),
            dma((tiles,)),
            dma((tiles,)),
            dma((tiles,)),
            dma((blocks,)),
            dma((blocks,)),
            dma((chunks,)),
            dma((chunks,)),
        ],
        compiler_params=pltpu.CompilerParams(
            collective_id=0, has_side_effects=True, vmem_limit_bytes=56 * 1024 * 1024
        ),
        name="merging",
    )(requests, slots, fine_qkv.transpose(0, 2, 1, 3)[0], held, out_proj)
    return merged[None]


def column_kernel(
    cfg,
    owners_ref,
    picks_ref,
    fine_hbm,
    held_hbm,
    proj_hbm,
    out_ref,
    fine_ref,
    ask_ref,
    asked_ref,
    query_ref,
    near_ref,
    near_lse,
    give_ref,
    give_lse,
    take_ref,
    take_lse,
    att_ref,
    moved_ref,
    proj_ref,
    total_ref,
    load_sem,
    bank_sem,
    list_send,
    list_recv,
    proj_send,
    proj_recv,
    up_send,
    up_recv,
    over_send,
    over_recv,
    pass_send,
    pass_recv,
    qup_send,
    qup_recv,
    qside_send,
    qside_recv,
    give_send,
    take_recv,
    lse_send,
    lse_recv,
    hop_send,
    hop_recv,
    *bank_refs,
):
    segments, heads, blocks, lists, panel, width, picks, chunks = cfg
    tile = lax.axis_index("tile")
    segment = lax.axis_index("segment")
    core = lax.axis_index("mp")
    plane = tile // 2
    column = lax.rem(tile, 2)
    inner = jnp.logical_or(plane == 1, plane == 2)
    outer = jnp.logical_not(inner)
    low = plane < 2
    server = jnp.where(low, 2, 4) + column
    server_side = jnp.where(low, 2, 4) + 1 - column
    buddy = jnp.where(low, 0, 6) + column
    buddy_side = jnp.where(low, 0, 6) + 1 - column
    cross = jnp.where(plane == 1, tile + 2, tile - 2)
    nxt = lax.rem(segment + 1, segments)
    half = blocks * panel // 2
    scale = 1.0 / math.sqrt(width)
    far_away = -1e30

    def at(where_to):
        return (segment, where_to, core)

    def remote(src, dst, send, recv, device):
        return pltpu.make_async_remote_copy(
            src_ref=src,
            dst_ref=dst,
            send_sem=send,
            recv_sem=recv,
            device_id=device,
            device_id_type=MESH,
        )

    def held_of(head):
        return held_hbm.at[:, head]

    def fine_cols(part, head):
        return fine_hbm.at[part, :, pl.ds(head * width, width)]

    def bank_of(head, which):
        return bank_refs[head].at[pl.ds(which * picks, picks)]

    def up(head):
        return remote(
            held_of(head), bank_of(head, plane), up_send.at[head], up_recv.at[head], at(server)
        )

    def over(head):
        return remote(
            held_of(head), bank_of(head, plane), over_send.at[head], over_recv.at[head], at(cross)
        )

    def passed(head):
        far = buddy // 2
        return remote(
            bank_of(head, far), bank_of(head, far), pass_send.at[head], pass_recv.at[head], at(cross)
        )

    def q_up(head):
        return remote(
            fine_cols(0, head), query_ref.at[2, head], qup_send.at[head], qup_recv.at[head], at(server)
        )

    def q_side(head):
        return remote(
            fine_cols(0, head),
            query_ref.at[1, head],
            qside_send.at[1, head],
            qside_recv.at[1, head],
            at(server_side),
        )

    def q_pass(head):
        return remote(
            query_ref.at[2, head],
            query_ref.at[0, head],
            qside_send.at[0, head],
            qside_recv.at[0, head],
            at(server_side),
        )

    def own_bank(head):
        return pltpu.make_async_copy(held_of(head), bank_of(head, plane), bank_sem.at[head])

    def own_query(head):
        return pltpu.make_async_copy(
            fine_cols(0, head), query_ref.at[3, head], bank_sem.at[heads + head]
        )

    def ask(place, device):
        return remote(
            ask_ref, asked_ref.at[place], list_send.at[place], list_recv.at[place], device
        )

    proj_load = pltpu.make_async_copy(proj_hbm, proj_ref.at[:, core], load_sem.at[1])
    proj_swap = remote(
        proj_hbm, proj_ref.at[:, core], proj_send, proj_recv, (segment, tile, 1 - core)
    )
    fine_load = pltpu.make_async_copy(fine_hbm, fine_ref, load_sem.at[0])
    fine_load.start()

    barrier = pltpu.get_barrier_semaphore()

    def greet(device):
        pl.semaphore_signal(barrier, inc=1, device_id=device, device_id_type=MESH)

    greet((nxt, tile, core))
    greet((nxt, tile, 1 - core))
    greet((segment, tile, 1 - core))
    greet(at(server_side))

    @pl.when(outer)
    def _():
        greet(at(server))

    @pl.when(inner)
    def _():
        greet(at(buddy))
        greet(at(buddy_side))
        greet(at(cross))

    def pack(block, carry):
        for head in range(heads):
            for entry in range(lists):
                owner = owners_ref[0, 0, block, entry, head]
                pick = picks_ref[0, 0, block, entry, head]
                place = (head * blocks + block) * lists + entry
                code = (owner - lax.rem(owner, 2)) * picks + pick * 2 + lax.rem(owner, 2)
                ask_ref[place] = code
                asked_ref[3, place] = code
        return carry

    lax.fori_loop(0, blocks, pack, 0)

    @pl.when(outer)
    def _():
        pl.semaphore_wait(barrier, 5)
        ask(2, at(server)).start()
        ask(0, at(server_side)).start()
        q_up(0).start()
        up(0).start()
        for head in range(1, heads):
            up(head).start()
            q_up(head).start()

    @pl.when(inner)
    def _():
        pl.semaphore_wait(barrier, 7)
        ask(1, at(server_side)).start()
        for head in range(AHEAD):
            over(head).start()
        for head in range(QUERY_AHEAD):
            q_side(head).start()
        for head in range(heads):
            own_bank(head).start()
            own_query(head).start()

    def relay(head):
        if head == 0:
            q_up(head).wait_recv()
            q_pass(head).start()
        up(head).wait_recv()
        passed(head).start()
        if head + AHEAD < heads - 1:
            over(head + AHEAD).start()
        if head + AHEAD == heads:
            over(heads - 1).start()
        if head > 0:
            q_up(head).wait_recv()
            q_pass(head).start()
        if head + QUERY_AHEAD < heads:
            q_side(head + QUERY_AHEAD).start()

    @pl.when(inner)
    def _():
        relay(0)

    proj_load.start()
    proj_swap.start()
    lane = lax.broadcasted_iota(jnp.int32, (panel, LANES), 1)

    def partials(queries, keys, values, biases):
        scores = []
        for place in range(blocks):
            score = (
                lax.dot_general(
                    queries[place],
                    keys[place],
                    (((1,), (1,)), ((), ())),
                    preferred_element_type=jnp.float32,
                )
                * scale
            )
            scores.append(score if biases is None else score + biases[place])
        stat = jnp.ones((panel, LANES), jnp.float32)
        weights, inverses = [], []
        for place in range(blocks):
            top = jnp.max(scores[place], axis=-1, keepdims=True)
            exponent = jnp.exp(scores[place] - top)
            total = jnp.sum(exponent, axis=-1, keepdims=True)
            weights.append(exponent.astype(jnp.bfloat16))
            inverses.append(1.0 / total)
            stat = jnp.where(lane == place, top, stat)
            stat = jnp.where(lane == 8 + place, total, stat)
        outs = []
        for place in range(blocks):
            outs.append(
                (
                    jnp.dot(weights[place], values[place], preferred_element_type=jnp.float32)
                    * inverses[place]
                ).astype(jnp.bfloat16)
            )
        turned = jnp.concatenate([stat, stat], axis=0).T
        return outs, turned[0:8] + jnp.log(turned[8:16])

    def rows_of(place):
        return slice(place * panel, (place + 1) * panel)

    fine_load.wait()

    def attend_fine(head, carry):
        cols = pl.ds(pl.multiple_of(head * width, width), width)
        outs, lse = partials(
            [fine_ref[0, rows_of(place), cols] for place in range(blocks)],
            [fine_ref[1, rows_of(place), cols] for place in range(blocks)],
            [fine_ref[2, rows_of(place), cols] for place in range(blocks)],
            None,
        )
        for place in range(blocks):
            near_ref[head, rows_of(place)] = outs[place]
        near_lse[head] = lse
        return carry

    lax.fori_loop(0, heads, attend_fine, 0)

    def give(place, head):
        goal = jnp.where(place == 0, buddy_side, jnp.where(place == 1, server_side, buddy))
        land = jnp.where(place == 2, 0, 1)
        return (
            remote(
                give_ref.at[place, head],
                take_ref.at[land, head],
                give_send.at[place, head],
                take_recv.at[land, head],
                at(goal),
            ),
            remote(
                give_lse.at[place, head],
                take_lse.at[land, head],
                lse_send.at[place, head],
                lse_recv.at[land, head],
                at(goal),
            ),
        )

    def take(land, head):
        return (
            remote(
                give_ref.at[0, head],
                take_ref.at[land, head],
                give_send.at[0, head],
                take_recv.at[land, head],
                at(server_side),
            ),
            remote(
                give_lse.at[0, head],
                take_lse.at[land, head],
                lse_send.at[0, head],
                lse_recv.at[land, head],
                at(server_side),
            ),
        )

    def attend(head):
        bank = bank_refs[head]

        def one_tile(place, carry):
            queries, keys, values, biases = [], [], [], []
            for block in range(blocks):
                codes = [
                    asked_ref[place, (head * blocks + block) * lists + entry]
                    for entry in range(lists)
                ]
                queries.append(query_ref[place, head, rows_of(block)])
                keys.append(
                    jnp.concatenate([bank[lax.div(code, 2), 0] for code in codes], axis=0)
                )
                values.append(
                    jnp.concatenate([bank[lax.div(code, 2), 1] for code in codes], axis=0)
                )
                there = [
                    jnp.where(lax.rem(code, 2) == column, 0.0, far_away) for code in codes
                ]
                biases.append(jnp.where(lane < panel, there[0], there[1]))
            outs, lse = partials(queries, keys, values, biases)
            for block in range(blocks):
                give_ref[place, head, rows_of(block)] = outs[block]
            give_lse[place, head] = lse

            @pl.when(place < 3)
            def _():
                for copy in give(place, head):
                    copy.start()

            return carry

        lax.fori_loop(0, 4, one_tile, 0)

    def merge(head, first, first_lse, second, second_lse):
        top = jnp.maximum(jnp.maximum(near_lse[head], first_lse), second_lse)
        shares = [jnp.exp(lse - top) for lse in (near_lse[head], first_lse, second_lse)]
        inverse = 1.0 / (shares[0] + shares[1] + shares[2])
        shares = [share * inverse for share in shares]
        turned = jnp.concatenate(
            shares + [jnp.zeros((LANES - 24, LANES), jnp.float32)], axis=0
        ).T[:panel]
        for block in range(blocks):
            rows = rows_of(block)
            total = near_ref[head, rows].astype(jnp.float32) * turned[:, block : block + 1]
            total = total + first(rows).astype(jnp.float32) * turned[:, 8 + block : 9 + block]
            total = total + second(rows).astype(jnp.float32) * turned[:, 16 + block : 17 + block]
            att_ref[head, rows] = total.astype(jnp.bfloat16)

    def hop(which, head):
        goal = core if which == 0 else 1 - core
        return remote(
            att_ref.at[head, pl.ds(pl.multiple_of(goal * half, half), half)],
            moved_ref.at[head, :, pl.ds(pl.multiple_of(core * width, width), width)],
            hop_send.at[which, head],
            hop_recv.at[which, head],
            (nxt, tile, goal),
        )

    def landed(which, head):
        source = core if which == 0 else 1 - core
        return remote(
            att_ref.at[head, pl.ds(0, half)],
            moved_ref.at[head, :, pl.ds(pl.multiple_of(source * width, width), width)],
            hop_send.at[which, head],
            hop_recv.at[which, head],
            (nxt, tile, source),
        )

    step_cols = out_ref.shape[1] // chunks

    def project(head):
        for which in range(2):
            landed(which, head).wait_recv()
        if head == 0:
            proj_load.wait()
            proj_swap.wait()

        def one_chunk(chunk, carry):
            cols = pl.ds(pl.multiple_of(chunk * step_cols, LANES), step_cols)
            product = jnp.dot(
                moved_ref[head],
                proj_ref[head, :, :, cols].reshape(2 * width, step_cols),
                preferred_element_type=jnp.float32,
            )
            if head == 0:
                total_ref[chunk] = product
            elif head < heads - 1:
                total_ref[chunk] += product
            else:
                out_ref[:, cols] = (total_ref[chunk] + product).astype(jnp.bfloat16)
            return carry

        lax.fori_loop(0, chunks, one_chunk, 0)

    def finish(head):
        @pl.when(inner)
        def _():
            for copy in take(1, head):
                copy.wait_recv()
            merge(
                head,
                lambda rows: give_ref[3, head, rows],
                give_lse[3, head],
                lambda rows: take_ref[1, head, rows],
                take_lse[1, head],
            )
            hop(0, head).start()
            hop(1, head).start()

        @pl.when(outer)
        def _():
            for land in range(2):
                for copy in take(land, head):
                    copy.wait_recv()
            merge(
                head,
                lambda rows: take_ref[0, head, rows],
                take_lse[0, head],
                lambda rows: take_ref[1, head, rows],
                take_lse[1, head],
            )
            hop(0, head).start()
            hop(1, head).start()

    @pl.when(inner)
    def _():
        relay(1)
        for place in range(3):
            ask(place, at(server_side)).wait_recv()

    def settle(head):
        hop(0, head).wait_send()
        hop(1, head).wait_send()

        @pl.when(outer)
        def _():
            up(head).wait_send()
            q_up(head).wait_send()

        @pl.when(inner)
        def _():
            over(head).wait_send()
            passed(head).wait_send()
            q_side(head).wait_send()
            q_pass(head).wait_send()
            for place in range(3):
                for copy in give(place, head):
                    copy.wait_send()

    for head in range(heads):
        @pl.when(inner)
        def _():
            own_bank(head).wait()
            own_query(head).wait()
            over(head).wait_recv()
            passed(head).wait_recv()
            q_side(head).wait_recv()
            q_pass(head).wait_recv()
            attend(head)
            if head + 2 < heads:
                relay(head + 2)

        if head >= 1:
            finish(head - 1)
        if head >= 2:
            project(head - 2)
            settle(head - 2)
    finish(heads - 1)
    project(heads - 2)
    project(heads - 1)

    for head in range(heads - 2, heads):
        settle(head)

    @pl.when(outer)
    def _():
        ask(2, at(server)).wait_send()
        ask(0, at(server_side)).wait_send()

    @pl.when(inner)
    def _():
        ask(1, at(server_side)).wait_send()


def by_columns(fine_qkv, panels, owners, picks, out_proj):
    segments = lax.axis_size("segment")
    heads, blocks, lists = owners.shape[2:]
    rows = fine_qkv.shape[1]
    held = panels[0]
    each, _, _, panel, width = held.shape
    planes = lax.axis_size("tile") // 2
    columns = out_proj.shape[1]
    chunks = 5
    smem = pl.BlockSpec(memory_space=pltpu.SMEM)
    vmem = pl.BlockSpec(memory_space=pltpu.VMEM)
    anywhere = pl.BlockSpec(memory_space=pl.ANY)
    cfg = (segments, heads, blocks, lists, panel, width, each, chunks)
    dma = pltpu.SemaphoreType.DMA
    bf16 = jnp.bfloat16
    merged = pl.pallas_call(
        functools.partial(column_kernel, cfg),
        out_shape=pltpu.VMEM((rows // 2, columns), bf16),
        in_specs=[smem, smem, anywhere, anywhere, anywhere],
        out_specs=vmem,
        scratch_shapes=[
            pltpu.VMEM((3, rows, fine_qkv.shape[3]), bf16),
            pltpu.SMEM((LANES,), jnp.int32),
            pltpu.SMEM((4, LANES), jnp.int32),
            pltpu.VMEM((4, heads, rows, width), bf16),
            pltpu.VMEM((heads, rows, width), bf16),
            pltpu.VMEM((heads, 8, LANES), jnp.float32),
            pltpu.VMEM((4, heads, rows, width), bf16),
            pltpu.VMEM((4, heads, 8, LANES), jnp.float32),
            pltpu.VMEM((2, heads, rows, width), bf16),
            pltpu.VMEM((2, heads, 8, LANES), jnp.float32),
            pltpu.VMEM((heads, rows, width), bf16),
            pltpu.VMEM((heads, rows // 2, 2 * width), bf16),
            pltpu.VMEM((heads, 2, width, columns), bf16),
            pltpu.VMEM((chunks, rows // 2, columns // chunks), jnp.float32),
            dma((2,)),
            dma((2 * heads,)),
            dma((3,)),
            dma((3,)),
            dma,
            dma,
            dma((heads,)),
            dma((heads,)),
            dma((heads,)),
            dma((heads,)),
            dma((heads,)),
            dma((heads,)),
            dma((heads,)),
            dma((heads,)),
            dma((2, heads)),
            dma((2, heads)),
            dma((3, heads)),
            dma((2, heads)),
            dma((3, heads)),
            dma((2, heads)),
            dma((2, heads)),
            dma((2, heads)),
        ]
        + [pltpu.VMEM((planes * each,) + held.shape[2:], bf16) for _ in range(heads)],
        compiler_params=pltpu.CompilerParams(
            collective_id=1, has_side_effects=True, vmem_limit_bytes=56 * 1024 * 1024
        ),
        name="columns",
    )(
        owners.transpose(0, 1, 3, 4, 2),
        picks.transpose(0, 1, 3, 4, 2),
        fine_qkv.transpose(0, 2, 1, 3)[0],
        held,
        out_proj.reshape(heads, width, columns),
    )
    return merged[None]


def solution(mesh):
    placed = (
        P("segment", "tile", None, "mp"),
        P("segment", "tile", "mp", None, None, None),
        P("segment", "tile", "mp", None, None),
        P("segment", "tile", "mp", None, None),
        P("mp", None),
    )
    small = mesh.shape["tile"] == 8 and mesh.shape["segment"] == 2
    return jax.shard_map(
        by_columns if small else on_device,
        mesh=mesh,
        in_specs=placed,
        out_specs=P("segment", ("tile", "mp"), None),
        check_vma=False,
    )
```

```python
import functools
import math

import jax
import jax.numpy as jnp
from jax import lax
from jax.experimental import pallas as pl
from jax.experimental.pallas import tpu as pltpu
from jax.sharding import PartitionSpec as P

MESH = pl.DeviceIdType.MESH
LANES = 128
AHEAD = 2
QUERY_AHEAD = 5


def request_kernel(capacity, owners_ref, picks_ref, req_ref, slot_ref, count_ref):
    tiles = req_ref.shape[0]
    blocks, lists, heads = owners_ref.shape[2:]
    for tile in range(tiles):
        count_ref[tile] = 0

    def clear(tile, carry):
        for rank in range(capacity):
            req_ref[tile, rank] = 0
        return carry

    lax.fori_loop(0, tiles, clear, 0)
    for head in range(heads):
        for block in range(blocks):
            for entry in range(lists):
                owner = owners_ref[0, 0, block, entry, head]
                rank = count_ref[owner]
                count_ref[owner] = rank + 1
                req_ref[owner, rank] = picks_ref[0, 0, block, entry, head] * heads + head
                slot_ref[(head * blocks + block) * lists + entry] = owner * capacity + rank


def main_kernel(
    cfg,
    req_ref,
    slot_ref,
    fine_hbm,
    held_hbm,
    proj_hbm,
    out_ref,
    fine_ref,
    held_ref,
    relay_ref,
    proj_ref,
    asked_ref,
    asked_smem,
    serve_ref,
    recv_ref,
    att_ref,
    moved_ref,
    psend_ref,
    precv_ref,
    total_ref,
    load_sem,
    smem_sem,
    relay_send,
    relay_recv,
    gate_sem,
    req_send,
    req_recv,
    pan_send,
    pan_recv,
    x_send,
    x_recv,
    mp_send,
    mp_recv,
):
    tiles, segments, capacity, heads, blocks, lists, panel, width, chunks = cfg
    tile = lax.axis_index("tile")
    segment = lax.axis_index("segment")
    core = lax.axis_index("mp")
    half_blocks = blocks // 2
    half = half_blocks * panel
    scale = 1.0 / math.sqrt(width)

    loads = [
        pltpu.make_async_copy(held_hbm, held_ref, load_sem.at[0]),
        pltpu.make_async_copy(fine_hbm, fine_ref, load_sem.at[1]),
        pltpu.make_async_copy(proj_hbm, proj_ref, load_sem.at[2]),
    ]
    for load in loads:
        load.start()

    nxt = lax.rem(segment + 1, segments)
    prv = lax.rem(segment + segments - 1, segments)
    barrier = pltpu.get_barrier_semaphore()

    def greet(step, carry):
        pl.semaphore_signal(
            barrier,
            inc=1,
            device_id=(segment, lax.rem(tile + step, tiles), core),
            device_id_type=MESH,
        )
        return carry

    lax.fori_loop(1, tiles, greet, 0)
    pl.semaphore_signal(barrier, inc=1, device_id=(nxt, tile, core), device_id_type=MESH)
    pl.semaphore_signal(barrier, inc=1, device_id=(prv, tile, core), device_id_type=MESH)
    pl.semaphore_signal(barrier, inc=1, device_id=(segment, tile, 1 - core), device_id_type=MESH)
    pl.semaphore_wait(barrier, tiles + 2)

    half_tiles = tiles // 2
    quarter = tiles // 4
    plane = tile // quarter
    inner = jnp.logical_or(plane == 1, plane == 2)
    partner = jnp.where(plane == 1, tile + quarter, tile - quarter)
    base = (tile // half_tiles) * half_tiles
    far_base = half_tiles - base

    def near_tile(step):
        return base + lax.rem(tile - base + step, half_tiles)

    def far_tile(step):
        return far_base + lax.rem(tile - base + step, half_tiles)

    def mirror(row):
        return lax.rem(row + half_tiles, tiles)

    relay_copy = pltpu.make_async_remote_copy(
        src_ref=held_hbm,
        dst_ref=relay_ref,
        send_sem=relay_send,
        recv_sem=relay_recv,
        device_id=(segment, jnp.where(inner, partner, mirror(tile)), core),
        device_id_type=MESH,
    )

    def request_copy(owner, server, row):
        return pltpu.make_async_remote_copy(
            src_ref=req_ref.at[owner],
            dst_ref=asked_ref.at[row],
            send_sem=req_send.at[owner],
            recv_sem=req_recv.at[row],
            device_id=(segment, server, core),
            device_id_type=MESH,
        )

    def far_request(owner):
        far_plane = owner // quarter
        relayed = jnp.logical_or(far_plane == 1, far_plane == 2)
        through = jnp.where(far_plane == 1, owner + quarter, owner - quarter)
        return request_copy(
            owner, jnp.where(relayed, through, owner), jnp.where(relayed, mirror(tile), tile)
        )

    def start_near(step, carry):
        owner = near_tile(step)
        request_copy(owner, owner, tile).start()
        return carry

    def start_far(step, carry):
        owner = far_tile(step)

        @pl.when(jnp.logical_not(jnp.logical_and(inner, owner == partner)))
        def _():
            far_request(owner).start()

        return carry

    def sent_near(step, carry):
        owner = near_tile(step)
        request_copy(owner, owner, owner).wait_send()
        return carry

    def sent_far(step, carry):
        owner = far_tile(step)

        @pl.when(jnp.logical_not(jnp.logical_and(inner, owner == partner)))
        def _():
            far_request(owner).wait_send()

        return carry

    def wait_near(step, carry):
        owner = near_tile(step)
        request_copy(owner, owner, owner).wait_recv()
        return carry

    def wait_far(step, carry):
        owner = far_tile(step)

        @pl.when(jnp.logical_not(jnp.logical_and(inner, owner == mirror(tile))))
        def _():
            request_copy(owner, owner, owner).wait_recv()

        return carry

    lax.fori_loop(1, half_tiles, start_near, 0)
    lax.fori_loop(0, half_tiles, start_far, 0)
    asked_ref[tile] = req_ref[tile]

    @pl.when(inner)
    def _():
        asked_ref[mirror(tile)] = req_ref[partner]

    lax.fori_loop(1, half_tiles, sent_near, 0)
    lax.fori_loop(0, half_tiles, sent_far, 0)

    @pl.when(inner)
    def _():
        relay_copy.start()

    loads[0].wait()
    lax.fori_loop(1, half_tiles, wait_near, 0)
    lax.fori_loop(0, half_tiles, wait_far, 0)
    to_smem = pltpu.make_async_copy(asked_ref, asked_smem, smem_sem)
    to_smem.start()
    to_smem.wait()

    def panel_copy(row, dest, owner):
        return pltpu.make_async_remote_copy(
            src_ref=serve_ref.at[row],
            dst_ref=recv_ref.at[pl.ds(owner * capacity, capacity)],
            send_sem=pan_send.at[row],
            recv_sem=pan_recv.at[owner],
            device_id=(segment, dest, core),
            device_id_type=MESH,
        )

    def pack(bank_ref, row):
        for rank in range(capacity):
            serve_ref[row, rank] = bank_ref[asked_smem[row, rank]]

    def serve_near(step, carry):
        dest = near_tile(step)
        pack(held_ref, dest)
        panel_copy(dest, dest, tile).start()
        return carry

    def pack_far(step, carry):
        pack(held_ref, far_tile(step))
        return carry

    def start_far_panels(step, carry):
        dest = far_tile(step)
        panel_copy(dest, dest, tile).start()
        return carry

    def serve_relay(step, carry):
        dest = near_tile(step)
        pack(relay_ref, mirror(dest))
        panel_copy(mirror(dest), dest, partner).start()
        return carry

    lax.fori_loop(1, half_tiles, serve_near, 0)
    for rank in range(capacity):
        recv_ref[tile * capacity + rank] = held_ref[asked_smem[tile, rank]]

    @pl.when(jnp.logical_not(inner))
    def _():
        lax.fori_loop(0, half_tiles, pack_far, 0)
        pl.semaphore_wait(gate_sem, 1)
        lax.fori_loop(0, half_tiles, start_far_panels, 0)

    @pl.when(inner)
    def _():
        relay_copy.wait_recv()
        pl.semaphore_signal(
            gate_sem, inc=1, device_id=(segment, mirror(tile), core), device_id_type=MESH
        )
        lax.fori_loop(1, half_tiles, serve_relay, 0)
        for rank in range(capacity):
            recv_ref[partner * capacity + rank] = relay_ref[asked_smem[mirror(tile), rank]]
        relay_copy.wait_send()

    loads[1].wait()
    loads[2].wait()

    def land_near(step, carry):
        peer = near_tile(step)
        copy = panel_copy(peer, peer, peer)
        copy.wait_send()
        copy.wait_recv()
        return carry

    def land_far(step, carry):
        peer = far_tile(step)

        @pl.when(jnp.logical_not(jnp.logical_and(inner, peer == mirror(tile))))
        def _():
            panel_copy(peer, peer, peer).wait_send()

        @pl.when(jnp.logical_not(jnp.logical_and(inner, peer == partner)))
        def _():
            panel_copy(peer, peer, peer).wait_recv()

        return carry

    lax.fori_loop(1, half_tiles, land_near, 0)
    lax.fori_loop(0, half_tiles, land_far, 0)

    def attend(block, group):
        rows = pl.ds(pl.multiple_of(block * panel, panel), panel)
        scores, values = [], []
        for head in group:
            cols = slice(head * width, (head + 1) * width)
            keys, vals = [fine_ref[1, rows, cols]], [fine_ref[2, rows, cols]]
            for entry in range(lists):
                slot = slot_ref[(head * blocks + block) * lists + entry]
                keys.append(recv_ref[slot, 0])
                vals.append(recv_ref[slot, 1])
            values.append(jnp.concatenate(vals, axis=0))
            scores.append(
                lax.dot_general(
                    fine_ref[0, rows, cols],
                    jnp.concatenate(keys, axis=0),
                    (((1,), (1,)), ((), ())),
                    preferred_element_type=jnp.float32,
                )
                * scale
            )
        weights = []
        for score in scores:
            exponent = jnp.exp(score - jnp.max(score, axis=-1, keepdims=True))
            inverse = 1.0 / jnp.sum(exponent, axis=-1, keepdims=True)
            weights.append((exponent * inverse).astype(jnp.bfloat16))
        for at, head in enumerate(group):
            att_ref[rows, head * width : (head + 1) * width] = jnp.dot(
                weights[at], values[at], preferred_element_type=jnp.float32
            ).astype(jnp.bfloat16)

    def hop(place):
        rows = pl.ds(pl.multiple_of((theirs + place) * panel, panel), panel)
        return pltpu.make_async_remote_copy(
            src_ref=att_ref.at[rows],
            dst_ref=moved_ref.at[rows],
            send_sem=x_send.at[place],
            recv_sem=x_recv.at[place],
            device_id=(nxt, tile, core),
            device_id_type=MESH,
        )

    theirs = (1 - core) * half_blocks
    mine = core * half_blocks
    mine_rows = pl.ds(pl.multiple_of(mine * panel, panel), half)
    theirs_rows = pl.ds(pl.multiple_of(theirs * panel, panel), half)
    groups = (tuple(range(heads - 2)), tuple(range(heads - 2, heads)))

    def hop_mine(at):
        group = groups[at]
        cols = pl.ds(group[0] * width, len(group) * width)
        return pltpu.make_async_remote_copy(
            src_ref=att_ref.at[mine_rows, cols],
            dst_ref=moved_ref.at[mine_rows, cols],
            send_sem=x_send.at[half_blocks + at],
            recv_sem=x_recv.at[half_blocks + at],
            device_id=(nxt, tile, core),
            device_id_type=MESH,
        )

    def send_theirs(place, carry):
        attend(theirs + place, tuple(range(heads)))
        hop(place).start()
        return carry

    lax.fori_loop(0, half_blocks, send_theirs, 0)
    for at in range(2):
        def attend_mine(place, carry):
            attend(mine + place, groups[at])
            return carry

        lax.fori_loop(0, half_blocks, attend_mine, 0)
        hop_mine(at).start()

    step_cols = proj_ref.shape[1] // chunks

    def product(rows, group, chunk):
        depth = slice(group[0] * width, (group[-1] + 1) * width)
        return jnp.dot(
            moved_ref[rows, depth],
            proj_ref[depth, chunk * step_cols : (chunk + 1) * step_cols],
            preferred_element_type=jnp.float32,
        )

    def swap(chunk):
        return pltpu.make_async_remote_copy(
            src_ref=psend_ref.at[chunk],
            dst_ref=precv_ref.at[chunk],
            send_sem=mp_send.at[chunk],
            recv_sem=mp_recv.at[chunk],
            device_id=(segment, tile, 1 - core),
            device_id_type=MESH,
        )

    for place in range(half_blocks):
        hop(place).wait()
    for chunk in range(chunks):
        psend_ref[chunk] = product(theirs_rows, tuple(range(heads)), chunk).astype(jnp.bfloat16)
        swap(chunk).start()
    hop_mine(0).wait()
    for chunk in range(chunks):
        total_ref[chunk] = product(mine_rows, groups[0], chunk)
    for chunk in range(chunks):
        swap(chunk).wait()
    hop_mine(1).wait()
    for chunk in range(chunks):
        own = (total_ref[chunk] + product(mine_rows, groups[1], chunk)).astype(jnp.bfloat16)
        out_ref[:, chunk * step_cols : (chunk + 1) * step_cols] = (
            own.astype(jnp.float32) + precv_ref[chunk].astype(jnp.float32)
        ).astype(jnp.bfloat16)


def on_device(fine_qkv, panels, owners, picks, out_proj):
    tiles = lax.axis_size("tile")
    segments = lax.axis_size("segment")
    heads, blocks, lists = owners.shape[2:]
    entries = heads * blocks * lists
    capacity = max(2, (entries + tiles - 1) // tiles)
    rows = fine_qkv.shape[1]
    held = panels.reshape((-1,) + panels.shape[3:])
    panel, width = held.shape[-2:]
    depth, columns = out_proj.shape
    chunks = 5
    smem = pl.BlockSpec(memory_space=pltpu.SMEM)
    vmem = pl.BlockSpec(memory_space=pltpu.VMEM)
    anywhere = pl.BlockSpec(memory_space=pl.ANY)
    requests, slots = pl.pallas_call(
        functools.partial(request_kernel, capacity),
        out_shape=(
            jax.ShapeDtypeStruct((tiles, LANES), jnp.int32),
            jax.ShapeDtypeStruct((entries,), jnp.int32),
        ),
        in_specs=[smem, smem],
        out_specs=(smem, smem),
        scratch_shapes=[pltpu.SMEM((tiles,), jnp.int32)],
        name="requests",
    )(owners.transpose(0, 1, 3, 4, 2), picks.transpose(0, 1, 3, 4, 2))
    cfg = (tiles, segments, capacity, heads, blocks, lists, panel, width, chunks)
    dma = pltpu.SemaphoreType.DMA
    bf16 = jnp.bfloat16
    merged = pl.pallas_call(
        functools.partial(main_kernel, cfg),
        out_shape=jax.ShapeDtypeStruct((rows // 2, columns), bf16),
        in_specs=[vmem, smem, anywhere, anywhere, anywhere],
        out_specs=vmem,
        scratch_shapes=[
            pltpu.VMEM((3, rows, fine_qkv.shape[3]), bf16),
            pltpu.VMEM(held.shape, bf16),
            pltpu.VMEM(held.shape, bf16),
            pltpu.VMEM(out_proj.shape, bf16),
            pltpu.VMEM((tiles, LANES), jnp.int32),
            pltpu.SMEM((tiles, LANES), jnp.int32),
            pltpu.VMEM((tiles, capacity) + held.shape[1:], bf16),
            pltpu.VMEM((tiles * capacity,) + held.shape[1:], bf16),
            pltpu.VMEM((rows, depth), bf16),
            pltpu.VMEM((rows, depth), bf16),
            pltpu.VMEM((chunks, rows // 2, columns // chunks), bf16),
            pltpu.VMEM((chunks, rows // 2, columns // chunks), bf16),
            pltpu.VMEM((chunks, rows // 2, columns // chunks), jnp.float32),
            dma((3,)),
            dma,
            dma,
            dma,
            pltpu.SemaphoreType.REGULAR,
            dma((tiles,)),
            dma((tiles,)),
            dma((tiles,)),
            dma((tiles,)),
            dma((blocks,)),
            dma((blocks,)),
            dma((chunks,)),
            dma((chunks,)),
        ],
        compiler_params=pltpu.CompilerParams(
            collective_id=0, has_side_effects=True, vmem_limit_bytes=56 * 1024 * 1024
        ),
        name="merging",
    )(requests, slots, fine_qkv.transpose(0, 2, 1, 3)[0], held, out_proj)
    return merged[None]


def column_kernel(
    cfg,
    owners_ref,
    picks_ref,
    fine_hbm,
    held_hbm,
    proj_hbm,
    out_ref,
    fine_ref,
    ask_ref,
    asked_ref,
    query_ref,
    near_ref,
    near_lse,
    give_ref,
    give_lse,
    take_ref,
    take_lse,
    att_ref,
    moved_ref,
    proj_ref,
    total_ref,
    load_sem,
    bank_sem,
    list_send,
    list_recv,
    proj_send,
    proj_recv,
    up_send,
    up_recv,
    over_send,
    over_recv,
    pass_send,
    pass_recv,
    qup_send,
    qup_recv,
    qside_send,
    qside_recv,
    give_send,
    take_recv,
    lse_send,
    lse_recv,
    hop_send,
    hop_recv,
    tail_send,
    tail_recv,
    *bank_refs,
):
    segments, heads, blocks, lists, panel, width, picks, chunks = cfg
    tile = lax.axis_index("tile")
    segment = lax.axis_index("segment")
    core = lax.axis_index("mp")
    plane = tile // 2
    column = lax.rem(tile, 2)
    inner = jnp.logical_or(plane == 1, plane == 2)
    outer = jnp.logical_not(inner)
    low = plane < 2
    server = jnp.where(low, 2, 4) + column
    server_side = jnp.where(low, 2, 4) + 1 - column
    buddy = jnp.where(low, 0, 6) + column
    buddy_side = jnp.where(low, 0, 6) + 1 - column
    cross = jnp.where(plane == 1, tile + 2, tile - 2)
    nxt = lax.rem(segment + 1, segments)
    half = blocks * panel // 2
    scale = 1.0 / math.sqrt(width)
    far_away = -1e30

    def at(where_to):
        return (segment, where_to, core)

    def remote(src, dst, send, recv, device):
        return pltpu.make_async_remote_copy(
            src_ref=src,
            dst_ref=dst,
            send_sem=send,
            recv_sem=recv,
            device_id=device,
            device_id_type=MESH,
        )

    def held_of(head):
        return held_hbm.at[:, head]

    def fine_cols(part, head):
        return fine_hbm.at[part, :, pl.ds(head * width, width)]

    def bank_of(head, which):
        return bank_refs[head].at[pl.ds(which * picks, picks)]

    def up(head):
        return remote(
            held_of(head), bank_of(head, plane), up_send.at[head], up_recv.at[head], at(server)
        )

    def over(head):
        return remote(
            held_of(head), bank_of(head, plane), over_send.at[head], over_recv.at[head], at(cross)
        )

    def passed(head):
        far = buddy // 2
        return remote(
            bank_of(head, far), bank_of(head, far), pass_send.at[head], pass_recv.at[head], at(cross)
        )

    def q_up(head):
        return remote(
            fine_cols(0, head), query_ref.at[2, head], qup_send.at[head], qup_recv.at[head], at(server)
        )

    def q_side(head):
        return remote(
            fine_cols(0, head),
            query_ref.at[1, head],
            qside_send.at[1, head],
            qside_recv.at[1, head],
            at(server_side),
        )

    def q_pass(head):
        return remote(
            query_ref.at[2, head],
            query_ref.at[0, head],
            qside_send.at[0, head],
            qside_recv.at[0, head],
            at(server_side),
        )

    def own_bank(head):
        return pltpu.make_async_copy(held_of(head), bank_of(head, plane), bank_sem.at[head])

    def own_query(head):
        return pltpu.make_async_copy(
            fine_cols(0, head), query_ref.at[3, head], bank_sem.at[heads + head]
        )

    def ask(place, device):
        return remote(
            ask_ref, asked_ref.at[place], list_send.at[place], list_recv.at[place], device
        )

    proj_load = pltpu.make_async_copy(proj_hbm, proj_ref.at[:, core], load_sem.at[1])
    proj_swap = remote(
        proj_hbm, proj_ref.at[:, core], proj_send, proj_recv, (segment, tile, 1 - core)
    )
    fine_load = pltpu.make_async_copy(fine_hbm, fine_ref, load_sem.at[0])
    fine_load.start()

    barrier = pltpu.get_barrier_semaphore()

    def greet(device):
        pl.semaphore_signal(barrier, inc=1, device_id=device, device_id_type=MESH)

    greet((nxt, tile, core))
    greet((nxt, tile, 1 - core))
    greet((segment, tile, 1 - core))
    greet(at(server_side))

    @pl.when(outer)
    def _():
        greet(at(server))

    @pl.when(inner)
    def _():
        greet(at(buddy))
        greet(at(buddy_side))
        greet(at(cross))

    def pack(block, carry):
        for head in range(heads):
            for entry in range(lists):
                owner = owners_ref[0, 0, block, entry, head]
                pick = picks_ref[0, 0, block, entry, head]
                place = (head * blocks + block) * lists + entry
                code = (owner - lax.rem(owner, 2)) * picks + pick * 2 + lax.rem(owner, 2)
                ask_ref[place] = code
                asked_ref[3, place] = code
        return carry

    lax.fori_loop(0, blocks, pack, 0)

    @pl.when(outer)
    def _():
        pl.semaphore_wait(barrier, 5)
        ask(2, at(server)).start()
        ask(0, at(server_side)).start()
        q_up(0).start()
        up(0).start()
        for head in range(1, heads):
            up(head).start()
            q_up(head).start()

    @pl.when(inner)
    def _():
        pl.semaphore_wait(barrier, 7)
        ask(1, at(server_side)).start()
        for head in range(AHEAD):
            over(head).start()
        for head in range(QUERY_AHEAD):
            q_side(head).start()
        for head in range(heads):
            own_bank(head).start()
            own_query(head).start()

    def relay(head):
        if head == 0:
            q_up(head).wait_recv()
            q_pass(head).start()
        up(head).wait_recv()
        passed(head).start()
        if head + AHEAD < heads - 1:
            over(head + AHEAD).start()
        if head + AHEAD == heads:
            over(heads - 1).start()
        if head > 0:
            q_up(head).wait_recv()
            q_pass(head).start()
        if head + QUERY_AHEAD < heads:
            q_side(head + QUERY_AHEAD).start()

    @pl.when(inner)
    def _():
        relay(0)

    proj_load.start()
    proj_swap.start()
    lane = lax.broadcasted_iota(jnp.int32, (panel, LANES), 1)

    def partials(queries, keys, values, biases):
        scores = []
        for place in range(blocks):
            score = (
                lax.dot_general(
                    queries[place],
                    keys[place],
                    (((1,), (1,)), ((), ())),
                    preferred_element_type=jnp.float32,
                )
                * scale
            )
            scores.append(score if biases is None else score + biases[place])
        stat = jnp.ones((panel, LANES), jnp.float32)
        weights, inverses = [], []
        for place in range(blocks):
            top = jnp.max(scores[place], axis=-1, keepdims=True)
            exponent = jnp.exp(scores[place] - top)
            total = jnp.sum(exponent, axis=-1, keepdims=True)
            weights.append(exponent.astype(jnp.bfloat16))
            inverses.append(1.0 / total)
            stat = jnp.where(lane == place, top, stat)
            stat = jnp.where(lane == 8 + place, total, stat)
        outs = []
        for place in range(blocks):
            outs.append(
                (
                    jnp.dot(weights[place], values[place], preferred_element_type=jnp.float32)
                    * inverses[place]
                ).astype(jnp.bfloat16)
            )
        turned = jnp.concatenate([stat, stat], axis=0).T
        return outs, turned[0:8] + jnp.log(turned[8:16])

    def rows_of(place):
        return slice(place * panel, (place + 1) * panel)

    fine_load.wait()

    def attend_fine(head, carry):
        cols = pl.ds(pl.multiple_of(head * width, width), width)
        outs, lse = partials(
            [fine_ref[0, rows_of(place), cols] for place in range(blocks)],
            [fine_ref[1, rows_of(place), cols] for place in range(blocks)],
            [fine_ref[2, rows_of(place), cols] for place in range(blocks)],
            None,
        )
        for place in range(blocks):
            near_ref[head, rows_of(place)] = outs[place]
        near_lse[head] = lse
        return carry

    lax.fori_loop(0, heads, attend_fine, 0)

    def give(place, head):
        goal = jnp.where(place == 0, buddy_side, jnp.where(place == 1, server_side, buddy))
        land = jnp.where(place == 2, 0, 1)
        return (
            remote(
                give_ref.at[place, head],
                take_ref.at[land, head],
                give_send.at[place, head],
                take_recv.at[land, head],
                at(goal),
            ),
            remote(
                give_lse.at[place, head],
                take_lse.at[land, head],
                lse_send.at[place, head],
                lse_recv.at[land, head],
                at(goal),
            ),
        )

    def take(land, head):
        return (
            remote(
                give_ref.at[0, head],
                take_ref.at[land, head],
                give_send.at[0, head],
                take_recv.at[land, head],
                at(server_side),
            ),
            remote(
                give_lse.at[0, head],
                take_lse.at[land, head],
                lse_send.at[0, head],
                lse_recv.at[land, head],
                at(server_side),
            ),
        )

    def give_half(place, half_of):
        last = heads - 1
        rows = pl.ds(half_of * half, half)
        land = 0 if place == 2 else 1
        return remote(
            give_ref.at[place, last, rows],
            take_ref.at[land, last, rows],
            tail_send.at[place, half_of],
            tail_recv.at[land, half_of],
            at((buddy_side, server_side, buddy)[place]),
        )

    def take_half(land, half_of):
        last = heads - 1
        rows = pl.ds(half_of * half, half)
        return remote(
            give_ref.at[0, last, rows],
            take_ref.at[land, last, rows],
            tail_send.at[0, half_of],
            tail_recv.at[land, half_of],
            at(server_side),
        )

    def attend(head):
        bank = bank_refs[head]

        def one_tile(place, carry):
            queries, keys, values, biases = [], [], [], []
            for block in range(blocks):
                codes = [
                    asked_ref[place, (head * blocks + block) * lists + entry]
                    for entry in range(lists)
                ]
                queries.append(query_ref[place, head, rows_of(block)])
                keys.append(
                    jnp.concatenate([bank[lax.div(code, 2), 0] for code in codes], axis=0)
                )
                values.append(
                    jnp.concatenate([bank[lax.div(code, 2), 1] for code in codes], axis=0)
                )
                there = [
                    jnp.where(lax.rem(code, 2) == column, 0.0, far_away) for code in codes
                ]
                biases.append(jnp.where(lane < panel, there[0], there[1]))
            outs, lse = partials(queries, keys, values, biases)
            for block in range(blocks):
                give_ref[place, head, rows_of(block)] = outs[block]
            give_lse[place, head] = lse

            if head < heads - 1:
                @pl.when(place < 3)
                def _():
                    for copy in give(place, head):
                        copy.start()

            return carry

        if head < heads - 1:
            lax.fori_loop(0, 4, one_tile, 0)
            return
        one_tile(0, 0)
        give(0, head)[1].start()
        give_half(0, 0).start()
        one_tile(2, 0)
        give(2, head)[1].start()
        give_half(2, 0).start()
        give_half(0, 1).start()
        give_half(2, 1).start()
        one_tile(1, 0)
        give(1, head)[1].start()
        give_half(1, 0).start()
        give_half(1, 1).start()
        one_tile(3, 0)

    def shares_of(head, first_lse, second_lse):
        top = jnp.maximum(jnp.maximum(near_lse[head], first_lse), second_lse)
        shares = [jnp.exp(lse - top) for lse in (near_lse[head], first_lse, second_lse)]
        inverse = 1.0 / (shares[0] + shares[1] + shares[2])
        shares = [share * inverse for share in shares]
        return jnp.concatenate(
            shares + [jnp.zeros((LANES - 24, LANES), jnp.float32)], axis=0
        ).T[:panel]

    def merge(head, turned, first, second, some):
        for block in some:
            rows = rows_of(block)
            total = near_ref[head, rows].astype(jnp.float32) * turned[:, block : block + 1]
            total = total + first(rows).astype(jnp.float32) * turned[:, 8 + block : 9 + block]
            total = total + second(rows).astype(jnp.float32) * turned[:, 16 + block : 17 + block]
            att_ref[head, rows] = total.astype(jnp.bfloat16)

    def hop(which, head):
        goal = core if which == 0 else 1 - core
        return remote(
            att_ref.at[head, pl.ds(pl.multiple_of(goal * half, half), half)],
            moved_ref.at[head, :, pl.ds(pl.multiple_of(core * width, width), width)],
            hop_send.at[which, head],
            hop_recv.at[which, head],
            (nxt, tile, goal),
        )

    def landed(which, head):
        source = core if which == 0 else 1 - core
        return remote(
            att_ref.at[head, pl.ds(0, half)],
            moved_ref.at[head, :, pl.ds(pl.multiple_of(source * width, width), width)],
            hop_send.at[which, head],
            hop_recv.at[which, head],
            (nxt, tile, source),
        )

    step_cols = out_ref.shape[1] // chunks

    def project(head):
        for which in range(2):
            landed(which, head).wait_recv()
        if head == 0:
            proj_load.wait()
            proj_swap.wait()

        def one_chunk(chunk, carry):
            cols = pl.ds(pl.multiple_of(chunk * step_cols, LANES), step_cols)
            product = jnp.dot(
                moved_ref[head],
                proj_ref[head, :, :, cols].reshape(2 * width, step_cols),
                preferred_element_type=jnp.float32,
            )
            if head == 0:
                total_ref[chunk] = product
            elif head < heads - 1:
                total_ref[chunk] += product
            else:
                out_ref[:, cols] = (total_ref[chunk] + product).astype(jnp.bfloat16)
            return carry

        lax.fori_loop(0, chunks, one_chunk, 0)

    def hop_to(half_of, head):
        which = jnp.where(core == half_of, 0, 1)
        return remote(
            att_ref.at[head, pl.ds(half_of * half, half)],
            moved_ref.at[head, :, pl.ds(pl.multiple_of(core * width, width), width)],
            hop_send.at[which, head],
            hop_recv.at[which, head],
            (nxt, tile, half_of),
        )

    def finish(head):
        def join(lands, first, first_lse, second, second_lse):
            for land in lands:
                take(land, head)[1].wait_recv()
            if head < heads - 1:
                for land in lands:
                    take(land, head)[0].wait_recv()
                turned = shares_of(head, first_lse(), second_lse())
                merge(head, turned, first, second, range(blocks))
                hop(0, head).start()
                hop(1, head).start()
                return
            turned = shares_of(head, first_lse(), second_lse())
            for half_of in range(2):
                for land in lands:
                    take_half(land, half_of).wait_recv()
                some = range(half_of * blocks // 2, (half_of + 1) * blocks // 2)
                merge(head, turned, first, second, some)
                hop_to(half_of, head).start()

        @pl.when(inner)
        def _():
            join(
                (1,),
                lambda rows: give_ref[3, head, rows],
                lambda: give_lse[3, head],
                lambda rows: take_ref[1, head, rows],
                lambda: take_lse[1, head],
            )

        @pl.when(outer)
        def _():
            join(
                (0, 1),
                lambda rows: take_ref[0, head, rows],
                lambda: take_lse[0, head],
                lambda rows: take_ref[1, head, rows],
                lambda: take_lse[1, head],
            )

    @pl.when(inner)
    def _():
        relay(1)
        for place in range(3):
            ask(place, at(server_side)).wait_recv()

    def settle(head):
        hop(0, head).wait_send()
        hop(1, head).wait_send()

        @pl.when(outer)
        def _():
            up(head).wait_send()
            q_up(head).wait_send()

        @pl.when(inner)
        def _():
            over(head).wait_send()
            passed(head).wait_send()
            q_side(head).wait_send()
            q_pass(head).wait_send()
            for place in range(3):
                value, lse = give(place, head)
                lse.wait_send()
                if head < heads - 1:
                    value.wait_send()
                else:
                    give_half(place, 0).wait_send()
                    give_half(place, 1).wait_send()

    for head in range(heads):
        @pl.when(inner)
        def _():
            own_bank(head).wait()
            own_query(head).wait()
            over(head).wait_recv()
            passed(head).wait_recv()
            q_side(head).wait_recv()
            q_pass(head).wait_recv()
            attend(head)
            if head + 2 < heads:
                relay(head + 2)

        if head >= 1:
            finish(head - 1)
        if head >= 2:
            project(head - 2)
            settle(head - 2)
    finish(heads - 1)
    project(heads - 2)
    project(heads - 1)

    for head in range(heads - 2, heads):
        settle(head)

    @pl.when(outer)
    def _():
        ask(2, at(server)).wait_send()
        ask(0, at(server_side)).wait_send()

    @pl.when(inner)
    def _():
        ask(1, at(server_side)).wait_send()


def by_columns(fine_qkv, panels, owners, picks, out_proj):
    segments = lax.axis_size("segment")
    heads, blocks, lists = owners.shape[2:]
    rows = fine_qkv.shape[1]
    held = panels[0]
    each, _, _, panel, width = held.shape
    planes = lax.axis_size("tile") // 2
    columns = out_proj.shape[1]
    chunks = 5
    smem = pl.BlockSpec(memory_space=pltpu.SMEM)
    vmem = pl.BlockSpec(memory_space=pltpu.VMEM)
    anywhere = pl.BlockSpec(memory_space=pl.ANY)
    cfg = (segments, heads, blocks, lists, panel, width, each, chunks)
    dma = pltpu.SemaphoreType.DMA
    bf16 = jnp.bfloat16
    merged = pl.pallas_call(
        functools.partial(column_kernel, cfg),
        out_shape=pltpu.VMEM((rows // 2, columns), bf16),
        in_specs=[smem, smem, anywhere, anywhere, anywhere],
        out_specs=vmem,
        scratch_shapes=[
            pltpu.VMEM((3, rows, fine_qkv.shape[3]), bf16),
            pltpu.SMEM((LANES,), jnp.int32),
            pltpu.SMEM((4, LANES), jnp.int32),
            pltpu.VMEM((4, heads, rows, width), bf16),
            pltpu.VMEM((heads, rows, width), bf16),
            pltpu.VMEM((heads, 8, LANES), jnp.float32),
            pltpu.VMEM((4, heads, rows, width), bf16),
            pltpu.VMEM((4, heads, 8, LANES), jnp.float32),
            pltpu.VMEM((2, heads, rows, width), bf16),
            pltpu.VMEM((2, heads, 8, LANES), jnp.float32),
            pltpu.VMEM((heads, rows, width), bf16),
            pltpu.VMEM((heads, rows // 2, 2 * width), bf16),
            pltpu.VMEM((heads, 2, width, columns), bf16),
            pltpu.VMEM((chunks, rows // 2, columns // chunks), jnp.float32),
            dma((2,)),
            dma((2 * heads,)),
            dma((3,)),
            dma((3,)),
            dma,
            dma,
            dma((heads,)),
            dma((heads,)),
            dma((heads,)),
            dma((heads,)),
            dma((heads,)),
            dma((heads,)),
            dma((heads,)),
            dma((heads,)),
            dma((2, heads)),
            dma((2, heads)),
            dma((3, heads)),
            dma((2, heads)),
            dma((3, heads)),
            dma((2, heads)),
            dma((2, heads)),
            dma((2, heads)),
            dma((3, 2)),
            dma((2, 2)),
        ]
        + [pltpu.VMEM((planes * each,) + held.shape[2:], bf16) for _ in range(heads)],
        compiler_params=pltpu.CompilerParams(
            collective_id=1, has_side_effects=True, vmem_limit_bytes=56 * 1024 * 1024
        ),
        name="columns",
    )(
        owners.transpose(0, 1, 3, 4, 2),
        picks.transpose(0, 1, 3, 4, 2),
        fine_qkv.transpose(0, 2, 1, 3)[0],
        held,
        out_proj.reshape(heads, width, columns),
    )
    return merged[None]


def solution(mesh):
    placed = (
        P("segment", "tile", None, "mp"),
        P("segment", "tile", "mp", None, None, None),
        P("segment", "tile", "mp", None, None),
        P("segment", "tile", "mp", None, None),
        P("mp", None),
    )
    small = mesh.shape["tile"] == 8 and mesh.shape["segment"] == 2
    return jax.shard_map(
        by_columns if small else on_device,
        mesh=mesh,
        in_specs=placed,
        out_specs=P("segment", ("tile", "mp"), None),
        check_vma=False,
    )
```

```python
import functools
import math

import jax
import jax.numpy as jnp
from jax import lax
from jax.experimental import pallas as pl
from jax.experimental.pallas import tpu as pltpu
from jax.sharding import PartitionSpec as P

MESH = pl.DeviceIdType.MESH
LANES = 128
AHEAD = 2
QUERY_AHEAD = 5


def request_kernel(capacity, owners_ref, picks_ref, req_ref, slot_ref, count_ref):
    tiles = req_ref.shape[0]
    blocks, lists, heads = owners_ref.shape[2:]
    for tile in range(tiles):
        count_ref[tile] = 0

    def clear(tile, carry):
        for rank in range(capacity):
            req_ref[tile, rank] = 0
        return carry

    lax.fori_loop(0, tiles, clear, 0)
    for head in range(heads):
        for block in range(blocks):
            for entry in range(lists):
                owner = owners_ref[0, 0, block, entry, head]
                rank = count_ref[owner]
                count_ref[owner] = rank + 1
                req_ref[owner, rank] = picks_ref[0, 0, block, entry, head] * heads + head
                slot_ref[(head * blocks + block) * lists + entry] = owner * capacity + rank


def main_kernel(
    cfg,
    req_ref,
    slot_ref,
    fine_hbm,
    held_hbm,
    proj_hbm,
    out_ref,
    fine_ref,
    held_ref,
    relay_ref,
    proj_ref,
    asked_ref,
    asked_smem,
    serve_ref,
    recv_ref,
    att_ref,
    moved_ref,
    psend_ref,
    precv_ref,
    total_ref,
    load_sem,
    smem_sem,
    relay_send,
    relay_recv,
    gate_sem,
    req_send,
    req_recv,
    pan_send,
    pan_recv,
    x_send,
    x_recv,
    mp_send,
    mp_recv,
):
    tiles, segments, capacity, heads, blocks, lists, panel, width, chunks = cfg
    tile = lax.axis_index("tile")
    segment = lax.axis_index("segment")
    core = lax.axis_index("mp")
    half_blocks = blocks // 2
    half = half_blocks * panel
    scale = 1.0 / math.sqrt(width)

    loads = [
        pltpu.make_async_copy(held_hbm, held_ref, load_sem.at[0]),
        pltpu.make_async_copy(fine_hbm, fine_ref, load_sem.at[1]),
        pltpu.make_async_copy(proj_hbm, proj_ref, load_sem.at[2]),
    ]
    for load in loads:
        load.start()

    nxt = lax.rem(segment + 1, segments)
    prv = lax.rem(segment + segments - 1, segments)
    barrier = pltpu.get_barrier_semaphore()

    def greet(step, carry):
        pl.semaphore_signal(
            barrier,
            inc=1,
            device_id=(segment, lax.rem(tile + step, tiles), core),
            device_id_type=MESH,
        )
        return carry

    lax.fori_loop(1, tiles, greet, 0)
    pl.semaphore_signal(barrier, inc=1, device_id=(nxt, tile, core), device_id_type=MESH)
    pl.semaphore_signal(barrier, inc=1, device_id=(prv, tile, core), device_id_type=MESH)
    pl.semaphore_signal(barrier, inc=1, device_id=(segment, tile, 1 - core), device_id_type=MESH)
    pl.semaphore_wait(barrier, tiles + 2)

    half_tiles = tiles // 2
    quarter = tiles // 4
    plane = tile // quarter
    inner = jnp.logical_or(plane == 1, plane == 2)
    partner = jnp.where(plane == 1, tile + quarter, tile - quarter)
    base = (tile // half_tiles) * half_tiles
    far_base = half_tiles - base

    def near_tile(step):
        return base + lax.rem(tile - base + step, half_tiles)

    def far_tile(step):
        return far_base + lax.rem(tile - base + step, half_tiles)

    def mirror(row):
        return lax.rem(row + half_tiles, tiles)

    relay_copy = pltpu.make_async_remote_copy(
        src_ref=held_hbm,
        dst_ref=relay_ref,
        send_sem=relay_send,
        recv_sem=relay_recv,
        device_id=(segment, jnp.where(inner, partner, mirror(tile)), core),
        device_id_type=MESH,
    )

    def request_copy(owner, server, row):
        return pltpu.make_async_remote_copy(
            src_ref=req_ref.at[owner],
            dst_ref=asked_ref.at[row],
            send_sem=req_send.at[owner],
            recv_sem=req_recv.at[row],
            device_id=(segment, server, core),
            device_id_type=MESH,
        )

    def far_request(owner):
        far_plane = owner // quarter
        relayed = jnp.logical_or(far_plane == 1, far_plane == 2)
        through = jnp.where(far_plane == 1, owner + quarter, owner - quarter)
        return request_copy(
            owner, jnp.where(relayed, through, owner), jnp.where(relayed, mirror(tile), tile)
        )

    def start_near(step, carry):
        owner = near_tile(step)
        request_copy(owner, owner, tile).start()
        return carry

    def start_far(step, carry):
        owner = far_tile(step)

        @pl.when(jnp.logical_not(jnp.logical_and(inner, owner == partner)))
        def _():
            far_request(owner).start()

        return carry

    def sent_near(step, carry):
        owner = near_tile(step)
        request_copy(owner, owner, owner).wait_send()
        return carry

    def sent_far(step, carry):
        owner = far_tile(step)

        @pl.when(jnp.logical_not(jnp.logical_and(inner, owner == partner)))
        def _():
            far_request(owner).wait_send()

        return carry

    def wait_near(step, carry):
        owner = near_tile(step)
        request_copy(owner, owner, owner).wait_recv()
        return carry

    def wait_far(step, carry):
        owner = far_tile(step)

        @pl.when(jnp.logical_not(jnp.logical_and(inner, owner == mirror(tile))))
        def _():
            request_copy(owner, owner, owner).wait_recv()

        return carry

    lax.fori_loop(1, half_tiles, start_near, 0)
    lax.fori_loop(0, half_tiles, start_far, 0)
    asked_ref[tile] = req_ref[tile]

    @pl.when(inner)
    def _():
        asked_ref[mirror(tile)] = req_ref[partner]

    lax.fori_loop(1, half_tiles, sent_near, 0)
    lax.fori_loop(0, half_tiles, sent_far, 0)

    @pl.when(inner)
    def _():
        relay_copy.start()

    loads[0].wait()
    lax.fori_loop(1, half_tiles, wait_near, 0)
    lax.fori_loop(0, half_tiles, wait_far, 0)
    to_smem = pltpu.make_async_copy(asked_ref, asked_smem, smem_sem)
    to_smem.start()
    to_smem.wait()

    def panel_copy(row, dest, owner):
        return pltpu.make_async_remote_copy(
            src_ref=serve_ref.at[row],
            dst_ref=recv_ref.at[pl.ds(owner * capacity, capacity)],
            send_sem=pan_send.at[row],
            recv_sem=pan_recv.at[owner],
            device_id=(segment, dest, core),
            device_id_type=MESH,
        )

    def pack(bank_ref, row):
        for rank in range(capacity):
            serve_ref[row, rank] = bank_ref[asked_smem[row, rank]]

    def serve_near(step, carry):
        dest = near_tile(step)
        pack(held_ref, dest)
        panel_copy(dest, dest, tile).start()
        return carry

    def pack_far(step, carry):
        pack(held_ref, far_tile(step))
        return carry

    def start_far_panels(step, carry):
        dest = far_tile(step)
        panel_copy(dest, dest, tile).start()
        return carry

    def serve_relay(step, carry):
        dest = near_tile(step)
        pack(relay_ref, mirror(dest))
        panel_copy(mirror(dest), dest, partner).start()
        return carry

    lax.fori_loop(1, half_tiles, serve_near, 0)
    for rank in range(capacity):
        recv_ref[tile * capacity + rank] = held_ref[asked_smem[tile, rank]]

    @pl.when(jnp.logical_not(inner))
    def _():
        lax.fori_loop(0, half_tiles, pack_far, 0)
        pl.semaphore_wait(gate_sem, 1)
        lax.fori_loop(0, half_tiles, start_far_panels, 0)

    @pl.when(inner)
    def _():
        relay_copy.wait_recv()
        pl.semaphore_signal(
            gate_sem, inc=1, device_id=(segment, mirror(tile), core), device_id_type=MESH
        )
        lax.fori_loop(1, half_tiles, serve_relay, 0)
        for rank in range(capacity):
            recv_ref[partner * capacity + rank] = relay_ref[asked_smem[mirror(tile), rank]]
        relay_copy.wait_send()

    loads[1].wait()
    loads[2].wait()

    def land_near(step, carry):
        peer = near_tile(step)
        copy = panel_copy(peer, peer, peer)
        copy.wait_send()
        copy.wait_recv()
        return carry

    def land_far(step, carry):
        peer = far_tile(step)

        @pl.when(jnp.logical_not(jnp.logical_and(inner, peer == mirror(tile))))
        def _():
            panel_copy(peer, peer, peer).wait_send()

        @pl.when(jnp.logical_not(jnp.logical_and(inner, peer == partner)))
        def _():
            panel_copy(peer, peer, peer).wait_recv()

        return carry

    lax.fori_loop(1, half_tiles, land_near, 0)
    lax.fori_loop(0, half_tiles, land_far, 0)

    def attend(block, group):
        rows = pl.ds(pl.multiple_of(block * panel, panel), panel)
        scores, values = [], []
        for head in group:
            cols = slice(head * width, (head + 1) * width)
            keys, vals = [fine_ref[1, rows, cols]], [fine_ref[2, rows, cols]]
            for entry in range(lists):
                slot = slot_ref[(head * blocks + block) * lists + entry]
                keys.append(recv_ref[slot, 0])
                vals.append(recv_ref[slot, 1])
            values.append(jnp.concatenate(vals, axis=0))
            scores.append(
                lax.dot_general(
                    fine_ref[0, rows, cols],
                    jnp.concatenate(keys, axis=0),
                    (((1,), (1,)), ((), ())),
                    preferred_element_type=jnp.float32,
                )
                * scale
            )
        weights = []
        for score in scores:
            exponent = jnp.exp(score - jnp.max(score, axis=-1, keepdims=True))
            inverse = 1.0 / jnp.sum(exponent, axis=-1, keepdims=True)
            weights.append((exponent * inverse).astype(jnp.bfloat16))
        for at, head in enumerate(group):
            att_ref[rows, head * width : (head + 1) * width] = jnp.dot(
                weights[at], values[at], preferred_element_type=jnp.float32
            ).astype(jnp.bfloat16)

    def hop(place):
        rows = pl.ds(pl.multiple_of((theirs + place) * panel, panel), panel)
        return pltpu.make_async_remote_copy(
            src_ref=att_ref.at[rows],
            dst_ref=moved_ref.at[rows],
            send_sem=x_send.at[place],
            recv_sem=x_recv.at[place],
            device_id=(nxt, tile, core),
            device_id_type=MESH,
        )

    theirs = (1 - core) * half_blocks
    mine = core * half_blocks
    mine_rows = pl.ds(pl.multiple_of(mine * panel, panel), half)
    theirs_rows = pl.ds(pl.multiple_of(theirs * panel, panel), half)
    groups = (tuple(range(heads - 2)), tuple(range(heads - 2, heads)))

    def hop_mine(at):
        group = groups[at]
        cols = pl.ds(group[0] * width, len(group) * width)
        return pltpu.make_async_remote_copy(
            src_ref=att_ref.at[mine_rows, cols],
            dst_ref=moved_ref.at[mine_rows, cols],
            send_sem=x_send.at[half_blocks + at],
            recv_sem=x_recv.at[half_blocks + at],
            device_id=(nxt, tile, core),
            device_id_type=MESH,
        )

    def send_theirs(place, carry):
        attend(theirs + place, tuple(range(heads)))
        hop(place).start()
        return carry

    lax.fori_loop(0, half_blocks, send_theirs, 0)
    for at in range(2):
        def attend_mine(place, carry):
            attend(mine + place, groups[at])
            return carry

        lax.fori_loop(0, half_blocks, attend_mine, 0)
        hop_mine(at).start()

    step_cols = proj_ref.shape[1] // chunks

    def product(rows, group, chunk):
        depth = slice(group[0] * width, (group[-1] + 1) * width)
        return jnp.dot(
            moved_ref[rows, depth],
            proj_ref[depth, chunk * step_cols : (chunk + 1) * step_cols],
            preferred_element_type=jnp.float32,
        )

    def swap(chunk):
        return pltpu.make_async_remote_copy(
            src_ref=psend_ref.at[chunk],
            dst_ref=precv_ref.at[chunk],
            send_sem=mp_send.at[chunk],
            recv_sem=mp_recv.at[chunk],
            device_id=(segment, tile, 1 - core),
            device_id_type=MESH,
        )

    for place in range(half_blocks):
        hop(place).wait()
    for chunk in range(chunks):
        psend_ref[chunk] = product(theirs_rows, tuple(range(heads)), chunk).astype(jnp.bfloat16)
        swap(chunk).start()
    hop_mine(0).wait()
    for chunk in range(chunks):
        total_ref[chunk] = product(mine_rows, groups[0], chunk)
    for chunk in range(chunks):
        swap(chunk).wait()
    hop_mine(1).wait()
    for chunk in range(chunks):
        own = (total_ref[chunk] + product(mine_rows, groups[1], chunk)).astype(jnp.bfloat16)
        out_ref[:, chunk * step_cols : (chunk + 1) * step_cols] = (
            own.astype(jnp.float32) + precv_ref[chunk].astype(jnp.float32)
        ).astype(jnp.bfloat16)


def on_device(fine_qkv, panels, owners, picks, out_proj):
    tiles = lax.axis_size("tile")
    segments = lax.axis_size("segment")
    heads, blocks, lists = owners.shape[2:]
    entries = heads * blocks * lists
    capacity = max(2, (entries + tiles - 1) // tiles)
    rows = fine_qkv.shape[1]
    held = panels.reshape((-1,) + panels.shape[3:])
    panel, width = held.shape[-2:]
    depth, columns = out_proj.shape
    chunks = 5
    smem = pl.BlockSpec(memory_space=pltpu.SMEM)
    vmem = pl.BlockSpec(memory_space=pltpu.VMEM)
    anywhere = pl.BlockSpec(memory_space=pl.ANY)
    requests, slots = pl.pallas_call(
        functools.partial(request_kernel, capacity),
        out_shape=(
            jax.ShapeDtypeStruct((tiles, LANES), jnp.int32),
            jax.ShapeDtypeStruct((entries,), jnp.int32),
        ),
        in_specs=[smem, smem],
        out_specs=(smem, smem),
        scratch_shapes=[pltpu.SMEM((tiles,), jnp.int32)],
        name="requests",
    )(owners.transpose(0, 1, 3, 4, 2), picks.transpose(0, 1, 3, 4, 2))
    cfg = (tiles, segments, capacity, heads, blocks, lists, panel, width, chunks)
    dma = pltpu.SemaphoreType.DMA
    bf16 = jnp.bfloat16
    merged = pl.pallas_call(
        functools.partial(main_kernel, cfg),
        out_shape=jax.ShapeDtypeStruct((rows // 2, columns), bf16),
        in_specs=[vmem, smem, anywhere, anywhere, anywhere],
        out_specs=vmem,
        scratch_shapes=[
            pltpu.VMEM((3, rows, fine_qkv.shape[3]), bf16),
            pltpu.VMEM(held.shape, bf16),
            pltpu.VMEM(held.shape, bf16),
            pltpu.VMEM(out_proj.shape, bf16),
            pltpu.VMEM((tiles, LANES), jnp.int32),
            pltpu.SMEM((tiles, LANES), jnp.int32),
            pltpu.VMEM((tiles, capacity) + held.shape[1:], bf16),
            pltpu.VMEM((tiles * capacity,) + held.shape[1:], bf16),
            pltpu.VMEM((rows, depth), bf16),
            pltpu.VMEM((rows, depth), bf16),
            pltpu.VMEM((chunks, rows // 2, columns // chunks), bf16),
            pltpu.VMEM((chunks, rows // 2, columns // chunks), bf16),
            pltpu.VMEM((chunks, rows // 2, columns // chunks), jnp.float32),
            dma((3,)),
            dma,
            dma,
            dma,
            pltpu.SemaphoreType.REGULAR,
            dma((tiles,)),
            dma((tiles,)),
            dma((tiles,)),
            dma((tiles,)),
            dma((blocks,)),
            dma((blocks,)),
            dma((chunks,)),
            dma((chunks,)),
        ],
        compiler_params=pltpu.CompilerParams(
            collective_id=0, has_side_effects=True, vmem_limit_bytes=56 * 1024 * 1024
        ),
        name="merging",
    )(requests, slots, fine_qkv.transpose(0, 2, 1, 3)[0], held, out_proj)
    return merged[None]


def column_kernel(
    cfg,
    owners_ref,
    picks_ref,
    fine_hbm,
    held_hbm,
    proj_hbm,
    out_ref,
    fine_ref,
    ask_ref,
    asked_ref,
    query_ref,
    near_ref,
    near_lse,
    give_ref,
    give_lse,
    take_ref,
    take_lse,
    att_ref,
    moved_ref,
    proj_ref,
    total_ref,
    load_sem,
    bank_sem,
    list_send,
    list_recv,
    proj_send,
    proj_recv,
    up_send,
    up_recv,
    over_send,
    over_recv,
    pass_send,
    pass_recv,
    qup_send,
    qup_recv,
    qside_send,
    qside_recv,
    give_send,
    take_recv,
    lse_send,
    lse_recv,
    hop_send,
    hop_recv,
    tail_send,
    tail_recv,
    *bank_refs,
):
    segments, heads, blocks, lists, panel, width, picks, chunks = cfg
    tile = lax.axis_index("tile")
    segment = lax.axis_index("segment")
    core = lax.axis_index("mp")
    plane = tile // 2
    column = lax.rem(tile, 2)
    inner = jnp.logical_or(plane == 1, plane == 2)
    outer = jnp.logical_not(inner)
    low = plane < 2
    server = jnp.where(low, 2, 4) + column
    server_side = jnp.where(low, 2, 4) + 1 - column
    buddy = jnp.where(low, 0, 6) + column
    buddy_side = jnp.where(low, 0, 6) + 1 - column
    cross = jnp.where(plane == 1, tile + 2, tile - 2)
    nxt = lax.rem(segment + 1, segments)
    half = blocks * panel // 2
    scale = 1.0 / math.sqrt(width)
    far_away = -1e30

    def at(where_to):
        return (segment, where_to, core)

    def remote(src, dst, send, recv, device):
        return pltpu.make_async_remote_copy(
            src_ref=src,
            dst_ref=dst,
            send_sem=send,
            recv_sem=recv,
            device_id=device,
            device_id_type=MESH,
        )

    def held_of(head):
        return held_hbm.at[:, head]

    def fine_cols(part, head):
        return fine_hbm.at[part, :, pl.ds(head * width, width)]

    def bank_of(head, which):
        return bank_refs[head].at[pl.ds(which * picks, picks)]

    def up(head):
        return remote(
            held_of(head), bank_of(head, plane), up_send.at[head], up_recv.at[head], at(server)
        )

    def over(head):
        return remote(
            held_of(head), bank_of(head, plane), over_send.at[head], over_recv.at[head], at(cross)
        )

    def passed(head):
        far = buddy // 2
        return remote(
            bank_of(head, far), bank_of(head, far), pass_send.at[head], pass_recv.at[head], at(cross)
        )

    def q_up(head):
        return remote(
            fine_cols(0, head), query_ref.at[2, head], qup_send.at[head], qup_recv.at[head], at(server)
        )

    def q_side(head):
        return remote(
            fine_cols(0, head),
            query_ref.at[1, head],
            qside_send.at[1, head],
            qside_recv.at[1, head],
            at(server_side),
        )

    def q_pass(head):
        return remote(
            query_ref.at[2, head],
            query_ref.at[0, head],
            qside_send.at[0, head],
            qside_recv.at[0, head],
            at(server_side),
        )

    def own_bank(head):
        return pltpu.make_async_copy(held_of(head), bank_of(head, plane), bank_sem.at[head])

    def own_query(head):
        return pltpu.make_async_copy(
            fine_cols(0, head), query_ref.at[3, head], bank_sem.at[heads + head]
        )

    def ask(place, device):
        return remote(
            ask_ref, asked_ref.at[place], list_send.at[place], list_recv.at[place], device
        )

    proj_load = pltpu.make_async_copy(proj_hbm, proj_ref.at[:, core], load_sem.at[1])
    proj_swap = remote(
        proj_hbm, proj_ref.at[:, core], proj_send, proj_recv, (segment, tile, 1 - core)
    )
    fine_load = pltpu.make_async_copy(fine_hbm, fine_ref, load_sem.at[0])
    fine_load.start()

    barrier = pltpu.get_barrier_semaphore()

    def greet(device):
        pl.semaphore_signal(barrier, inc=1, device_id=device, device_id_type=MESH)

    greet((nxt, tile, core))
    greet((nxt, tile, 1 - core))
    greet((segment, tile, 1 - core))
    greet(at(server_side))

    @pl.when(outer)
    def _():
        greet(at(server))

    @pl.when(inner)
    def _():
        greet(at(buddy))
        greet(at(buddy_side))
        greet(at(cross))

    def pack(block, carry):
        for head in range(heads):
            for entry in range(lists):
                owner = owners_ref[0, 0, block, entry, head]
                pick = picks_ref[0, 0, block, entry, head]
                place = (head * blocks + block) * lists + entry
                code = (owner - lax.rem(owner, 2)) * picks + pick * 2 + lax.rem(owner, 2)
                ask_ref[place] = code
                asked_ref[3, place] = code
        return carry

    lax.fori_loop(0, blocks, pack, 0)

    @pl.when(outer)
    def _():
        pl.semaphore_wait(barrier, 5)
        ask(2, at(server)).start()
        ask(0, at(server_side)).start()
        q_up(0).start()
        up(0).start()
        for head in range(1, heads):
            up(head).start()
            q_up(head).start()

    @pl.when(inner)
    def _():
        pl.semaphore_wait(barrier, 7)
        ask(1, at(server_side)).start()
        for head in range(AHEAD):
            over(head).start()
        for head in range(QUERY_AHEAD):
            q_side(head).start()
        for head in range(heads):
            own_bank(head).start()
            own_query(head).start()

    def relay(head):
        if head == 0:
            q_up(head).wait_recv()
            q_pass(head).start()
        up(head).wait_recv()
        passed(head).start()
        if head + AHEAD < heads - 1:
            over(head + AHEAD).start()
        if head + AHEAD == heads:
            over(heads - 1).start()
        if head > 0:
            q_up(head).wait_recv()
            q_pass(head).start()
        if head + QUERY_AHEAD < heads:
            q_side(head + QUERY_AHEAD).start()

    @pl.when(inner)
    def _():
        relay(0)

    proj_load.start()
    proj_swap.start()
    lane = lax.broadcasted_iota(jnp.int32, (panel, LANES), 1)

    def partials(queries, keys, values, biases):
        scores = []
        for place in range(blocks):
            score = (
                lax.dot_general(
                    queries[place],
                    keys[place],
                    (((1,), (1,)), ((), ())),
                    preferred_element_type=jnp.float32,
                )
                * scale
            )
            scores.append(score if biases is None else score + biases[place])
        stat = jnp.ones((panel, LANES), jnp.float32)
        weights, inverses = [], []
        for place in range(blocks):
            top = jnp.max(scores[place], axis=-1, keepdims=True)
            exponent = jnp.exp(scores[place] - top)
            total = jnp.sum(exponent, axis=-1, keepdims=True)
            weights.append(exponent.astype(jnp.bfloat16))
            inverses.append(1.0 / total)
            stat = jnp.where(lane == place, top, stat)
            stat = jnp.where(lane == 8 + place, total, stat)
        outs = []
        for place in range(blocks):
            outs.append(
                (
                    jnp.dot(weights[place], values[place], preferred_element_type=jnp.float32)
                    * inverses[place]
                ).astype(jnp.bfloat16)
            )
        turned = jnp.concatenate([stat, stat], axis=0).T
        return outs, turned[0:8] + jnp.log(turned[8:16])

    def rows_of(place):
        return slice(place * panel, (place + 1) * panel)

    fine_load.wait()

    def attend_fine(head, carry):
        cols = pl.ds(pl.multiple_of(head * width, width), width)
        outs, lse = partials(
            [fine_ref[0, rows_of(place), cols] for place in range(blocks)],
            [fine_ref[1, rows_of(place), cols] for place in range(blocks)],
            [fine_ref[2, rows_of(place), cols] for place in range(blocks)],
            None,
        )
        for place in range(blocks):
            near_ref[head, rows_of(place)] = outs[place]
        near_lse[head] = lse
        return carry

    lax.fori_loop(0, heads, attend_fine, 0)

    def give(place, head):
        goal = jnp.where(place == 0, buddy_side, jnp.where(place == 1, server_side, buddy))
        land = jnp.where(place == 2, 0, 1)
        return (
            remote(
                give_ref.at[place, head],
                take_ref.at[land, head],
                give_send.at[place, head],
                take_recv.at[land, head],
                at(goal),
            ),
            remote(
                give_lse.at[place, head],
                take_lse.at[land, head],
                lse_send.at[place, head],
                lse_recv.at[land, head],
                at(goal),
            ),
        )

    def take(land, head):
        return (
            remote(
                give_ref.at[0, head],
                take_ref.at[land, head],
                give_send.at[0, head],
                take_recv.at[land, head],
                at(server_side),
            ),
            remote(
                give_lse.at[0, head],
                take_lse.at[land, head],
                lse_send.at[0, head],
                lse_recv.at[land, head],
                at(server_side),
            ),
        )

    def give_half(place, half_of):
        last = heads - 1
        rows = pl.ds(half_of * half, half)
        land = 0 if place == 2 else 1
        return remote(
            give_ref.at[place, last, rows],
            take_ref.at[land, last, rows],
            tail_send.at[place, half_of],
            tail_recv.at[land, half_of],
            at((buddy_side, server_side, buddy)[place]),
        )

    def take_half(land, half_of):
        last = heads - 1
        rows = pl.ds(half_of * half, half)
        return remote(
            give_ref.at[0, last, rows],
            take_ref.at[land, last, rows],
            tail_send.at[0, half_of],
            tail_recv.at[land, half_of],
            at(server_side),
        )

    def attend(head):
        bank = bank_refs[head]

        def one_tile(place, carry):
            queries, keys, values, biases = [], [], [], []
            for block in range(blocks):
                codes = [
                    asked_ref[place, (head * blocks + block) * lists + entry]
                    for entry in range(lists)
                ]
                queries.append(query_ref[place, head, rows_of(block)])
                keys.append(
                    jnp.concatenate([bank[lax.div(code, 2), 0] for code in codes], axis=0)
                )
                values.append(
                    jnp.concatenate([bank[lax.div(code, 2), 1] for code in codes], axis=0)
                )
                there = [
                    jnp.where(lax.rem(code, 2) == column, 0.0, far_away) for code in codes
                ]
                biases.append(jnp.where(lane < panel, there[0], there[1]))
            outs, lse = partials(queries, keys, values, biases)
            for block in range(blocks):
                give_ref[place, head, rows_of(block)] = outs[block]
            give_lse[place, head] = lse

            if head < heads - 1:
                @pl.when(place < 3)
                def _():
                    for copy in give(place, head):
                        copy.start()

            return carry

        if head < heads - 1:
            lax.fori_loop(0, 4, one_tile, 0)
            return
        one_tile(0, 0)
        give(0, head)[1].start()
        give_half(0, 0).start()
        one_tile(2, 0)
        give(2, head)[1].start()
        give_half(2, 0).start()
        give_half(0, 1).start()
        give_half(2, 1).start()
        one_tile(1, 0)
        give(1, head)[1].start()
        give_half(1, 0).start()
        give_half(1, 1).start()
        one_tile(3, 0)

    def shares_of(head, first_lse, second_lse):
        top = jnp.maximum(jnp.maximum(near_lse[head], first_lse), second_lse)
        shares = [jnp.exp(lse - top) for lse in (near_lse[head], first_lse, second_lse)]
        inverse = 1.0 / (shares[0] + shares[1] + shares[2])
        shares = [share * inverse for share in shares]
        return jnp.concatenate(
            shares + [jnp.zeros((LANES - 24, LANES), jnp.float32)], axis=0
        ).T[:panel]

    def merge(head, turned, first, second, some):
        for block in some:
            rows = rows_of(block)
            total = near_ref[head, rows].astype(jnp.float32) * turned[:, block : block + 1]
            total = total + first(rows).astype(jnp.float32) * turned[:, 8 + block : 9 + block]
            total = total + second(rows).astype(jnp.float32) * turned[:, 16 + block : 17 + block]
            att_ref[head, rows] = total.astype(jnp.bfloat16)

    def hop(which, head):
        goal = core if which == 0 else 1 - core
        return remote(
            att_ref.at[head, pl.ds(pl.multiple_of(goal * half, half), half)],
            moved_ref.at[head, :, pl.ds(pl.multiple_of(core * width, width), width)],
            hop_send.at[which, head],
            hop_recv.at[which, head],
            (nxt, tile, goal),
        )

    def landed(which, head):
        source = core if which == 0 else 1 - core
        return remote(
            att_ref.at[head, pl.ds(0, half)],
            moved_ref.at[head, :, pl.ds(pl.multiple_of(source * width, width), width)],
            hop_send.at[which, head],
            hop_recv.at[which, head],
            (nxt, tile, source),
        )

    step_cols = out_ref.shape[1] // chunks

    def project(head):
        for which in range(2):
            landed(which, head).wait_recv()
        if head == 0:
            proj_load.wait()
            proj_swap.wait()

        def one_chunk(chunk, carry):
            cols = pl.ds(chunk * step_cols, step_cols)
            if head < heads - 1:
                cols = pl.ds(pl.multiple_of(chunk * step_cols, LANES), step_cols)
            product = jnp.dot(
                moved_ref[head],
                proj_ref[head, :, :, cols].reshape(2 * width, step_cols),
                preferred_element_type=jnp.float32,
            )
            if head == 0:
                total_ref[chunk] = product
            elif head < heads - 1:
                total_ref[chunk] += product
            else:
                out_ref[:, cols] = (total_ref[chunk] + product).astype(jnp.bfloat16)
            return carry

        if head < heads - 1:
            lax.fori_loop(0, chunks, one_chunk, 0)
            return
        for chunk in range(chunks):
            one_chunk(chunk, 0)

    def hop_to(half_of, head):
        which = jnp.where(core == half_of, 0, 1)
        return remote(
            att_ref.at[head, pl.ds(half_of * half, half)],
            moved_ref.at[head, :, pl.ds(pl.multiple_of(core * width, width), width)],
            hop_send.at[which, head],
            hop_recv.at[which, head],
            (nxt, tile, half_of),
        )

    def finish(head):
        def join(lands, first, first_lse, second, second_lse):
            for land in lands:
                take(land, head)[1].wait_recv()
            if head < heads - 1:
                for land in lands:
                    take(land, head)[0].wait_recv()
                turned = shares_of(head, first_lse(), second_lse())
                merge(head, turned, first, second, range(blocks))
                hop(0, head).start()
                hop(1, head).start()
                return
            turned = shares_of(head, first_lse(), second_lse())
            for half_of in range(2):
                for land in lands:
                    take_half(land, half_of).wait_recv()
                some = range(half_of * blocks // 2, (half_of + 1) * blocks // 2)
                merge(head, turned, first, second, some)
                hop_to(half_of, head).start()

        @pl.when(inner)
        def _():
            join(
                (1,),
                lambda rows: give_ref[3, head, rows],
                lambda: give_lse[3, head],
                lambda rows: take_ref[1, head, rows],
                lambda: take_lse[1, head],
            )

        @pl.when(outer)
        def _():
            join(
                (0, 1),
                lambda rows: take_ref[0, head, rows],
                lambda: take_lse[0, head],
                lambda rows: take_ref[1, head, rows],
                lambda: take_lse[1, head],
            )

    @pl.when(inner)
    def _():
        relay(1)
        for place in range(3):
            ask(place, at(server_side)).wait_recv()

    def settle(head):
        hop(0, head).wait_send()
        hop(1, head).wait_send()

        @pl.when(outer)
        def _():
            up(head).wait_send()
            q_up(head).wait_send()

        @pl.when(inner)
        def _():
            over(head).wait_send()
            passed(head).wait_send()
            q_side(head).wait_send()
            q_pass(head).wait_send()
            for place in range(3):
                value, lse = give(place, head)
                lse.wait_send()
                if head < heads - 1:
                    value.wait_send()
                else:
                    give_half(place, 0).wait_send()
                    give_half(place, 1).wait_send()

    for head in range(heads):
        @pl.when(inner)
        def _():
            own_bank(head).wait()
            own_query(head).wait()
            over(head).wait_recv()
            passed(head).wait_recv()
            q_side(head).wait_recv()
            q_pass(head).wait_recv()
            attend(head)
            if head + 2 < heads:
                relay(head + 2)

        if head >= 1:
            finish(head - 1)
        if head >= 2:
            project(head - 2)
            settle(head - 2)
    finish(heads - 1)
    project(heads - 2)
    project(heads - 1)

    for head in range(heads - 2, heads):
        settle(head)

    @pl.when(outer)
    def _():
        ask(2, at(server)).wait_send()
        ask(0, at(server_side)).wait_send()

    @pl.when(inner)
    def _():
        ask(1, at(server_side)).wait_send()


def by_columns(fine_qkv, panels, owners, picks, out_proj):
    segments = lax.axis_size("segment")
    heads, blocks, lists = owners.shape[2:]
    rows = fine_qkv.shape[1]
    held = panels[0]
    each, _, _, panel, width = held.shape
    planes = lax.axis_size("tile") // 2
    columns = out_proj.shape[1]
    chunks = 5
    smem = pl.BlockSpec(memory_space=pltpu.SMEM)
    vmem = pl.BlockSpec(memory_space=pltpu.VMEM)
    anywhere = pl.BlockSpec(memory_space=pl.ANY)
    cfg = (segments, heads, blocks, lists, panel, width, each, chunks)
    dma = pltpu.SemaphoreType.DMA
    bf16 = jnp.bfloat16
    merged = pl.pallas_call(
        functools.partial(column_kernel, cfg),
        out_shape=pltpu.VMEM((rows // 2, columns), bf16),
        in_specs=[smem, smem, anywhere, anywhere, anywhere],
        out_specs=vmem,
        scratch_shapes=[
            pltpu.VMEM((3, rows, fine_qkv.shape[3]), bf16),
            pltpu.SMEM((LANES,), jnp.int32),
            pltpu.SMEM((4, LANES), jnp.int32),
            pltpu.VMEM((4, heads, rows, width), bf16),
            pltpu.VMEM((heads, rows, width), bf16),
            pltpu.VMEM((heads, 8, LANES), jnp.float32),
            pltpu.VMEM((4, heads, rows, width), bf16),
            pltpu.VMEM((4, heads, 8, LANES), jnp.float32),
            pltpu.VMEM((2, heads, rows, width), bf16),
            pltpu.VMEM((2, heads, 8, LANES), jnp.float32),
            pltpu.VMEM((heads, rows, width), bf16),
            pltpu.VMEM((heads, rows // 2, 2 * width), bf16),
            pltpu.VMEM((heads, 2, width, columns), bf16),
            pltpu.VMEM((chunks, rows // 2, columns // chunks), jnp.float32),
            dma((2,)),
            dma((2 * heads,)),
            dma((3,)),
            dma((3,)),
            dma,
            dma,
            dma((heads,)),
            dma((heads,)),
            dma((heads,)),
            dma((heads,)),
            dma((heads,)),
            dma((heads,)),
            dma((heads,)),
            dma((heads,)),
            dma((2, heads)),
            dma((2, heads)),
            dma((3, heads)),
            dma((2, heads)),
            dma((3, heads)),
            dma((2, heads)),
            dma((2, heads)),
            dma((2, heads)),
            dma((3, 2)),
            dma((2, 2)),
        ]
        + [pltpu.VMEM((planes * each,) + held.shape[2:], bf16) for _ in range(heads)],
        compiler_params=pltpu.CompilerParams(
            collective_id=1, has_side_effects=True, vmem_limit_bytes=56 * 1024 * 1024
        ),
        name="columns",
    )(
        owners.transpose(0, 1, 3, 4, 2),
        picks.transpose(0, 1, 3, 4, 2),
        fine_qkv.transpose(0, 2, 1, 3)[0],
        held,
        out_proj.reshape(heads, width, columns),
    )
    return merged[None]


def solution(mesh):
    placed = (
        P("segment", "tile", None, "mp"),
        P("segment", "tile", "mp", None, None, None),
        P("segment", "tile", "mp", None, None),
        P("segment", "tile", "mp", None, None),
        P("mp", None),
    )
    small = mesh.shape["tile"] == 8 and mesh.shape["segment"] == 2
    return jax.shard_map(
        by_columns if small else on_device,
        mesh=mesh,
        in_specs=placed,
        out_specs=P("segment", ("tile", "mp"), None),
        check_vma=False,
    )
```

```python
import functools
import math

import jax
import jax.numpy as jnp
from jax import lax
from jax.experimental import pallas as pl
from jax.experimental.pallas import tpu as pltpu
from jax.sharding import PartitionSpec as P

MESH = pl.DeviceIdType.MESH
LANES = 128
AHEAD = 2
QUERY_AHEAD = 5


def request_kernel(capacity, owners_ref, picks_ref, req_ref, slot_ref, count_ref):
    tiles = req_ref.shape[0]
    blocks, lists, heads = owners_ref.shape[2:]
    for tile in range(tiles):
        count_ref[tile] = 0

    def clear(tile, carry):
        for rank in range(capacity):
            req_ref[tile, rank] = 0
        return carry

    lax.fori_loop(0, tiles, clear, 0)
    for head in range(heads):
        for block in range(blocks):
            for entry in range(lists):
                owner = owners_ref[0, 0, block, entry, head]
                rank = count_ref[owner]
                count_ref[owner] = rank + 1
                req_ref[owner, rank] = picks_ref[0, 0, block, entry, head] * heads + head
                slot_ref[(head * blocks + block) * lists + entry] = owner * capacity + rank


def main_kernel(
    cfg,
    req_ref,
    slot_ref,
    fine_hbm,
    held_hbm,
    proj_hbm,
    out_ref,
    fine_ref,
    held_ref,
    relay_ref,
    proj_ref,
    asked_ref,
    asked_smem,
    serve_ref,
    recv_ref,
    att_ref,
    moved_ref,
    psend_ref,
    precv_ref,
    total_ref,
    load_sem,
    smem_sem,
    relay_send,
    relay_recv,
    gate_sem,
    req_send,
    req_recv,
    pan_send,
    pan_recv,
    x_send,
    x_recv,
    mp_send,
    mp_recv,
):
    tiles, segments, capacity, heads, blocks, lists, panel, width, chunks = cfg
    tile = lax.axis_index("tile")
    segment = lax.axis_index("segment")
    core = lax.axis_index("mp")
    half_blocks = blocks // 2
    half = half_blocks * panel
    scale = 1.0 / math.sqrt(width)

    loads = [
        pltpu.make_async_copy(held_hbm, held_ref, load_sem.at[0]),
        pltpu.make_async_copy(fine_hbm, fine_ref, load_sem.at[1]),
        pltpu.make_async_copy(proj_hbm, proj_ref, load_sem.at[2]),
    ]
    for load in loads:
        load.start()

    nxt = lax.rem(segment + 1, segments)
    prv = lax.rem(segment + segments - 1, segments)
    barrier = pltpu.get_barrier_semaphore()

    def greet(step, carry):
        pl.semaphore_signal(
            barrier,
            inc=1,
            device_id=(segment, lax.rem(tile + step, tiles), core),
            device_id_type=MESH,
        )
        return carry

    lax.fori_loop(1, tiles, greet, 0)
    pl.semaphore_signal(barrier, inc=1, device_id=(nxt, tile, core), device_id_type=MESH)
    pl.semaphore_signal(barrier, inc=1, device_id=(prv, tile, core), device_id_type=MESH)
    pl.semaphore_signal(barrier, inc=1, device_id=(segment, tile, 1 - core), device_id_type=MESH)
    pl.semaphore_wait(barrier, tiles + 2)

    half_tiles = tiles // 2
    quarter = tiles // 4
    plane = tile // quarter
    inner = jnp.logical_or(plane == 1, plane == 2)
    partner = jnp.where(plane == 1, tile + quarter, tile - quarter)
    base = (tile // half_tiles) * half_tiles
    far_base = half_tiles - base

    def near_tile(step):
        return base + lax.rem(tile - base + step, half_tiles)

    def far_tile(step):
        return far_base + lax.rem(tile - base + step, half_tiles)

    def mirror(row):
        return lax.rem(row + half_tiles, tiles)

    relay_copy = pltpu.make_async_remote_copy(
        src_ref=held_hbm,
        dst_ref=relay_ref,
        send_sem=relay_send,
        recv_sem=relay_recv,
        device_id=(segment, jnp.where(inner, partner, mirror(tile)), core),
        device_id_type=MESH,
    )

    def request_copy(owner, server, row):
        return pltpu.make_async_remote_copy(
            src_ref=req_ref.at[owner],
            dst_ref=asked_ref.at[row],
            send_sem=req_send.at[owner],
            recv_sem=req_recv.at[row],
            device_id=(segment, server, core),
            device_id_type=MESH,
        )

    def far_request(owner):
        far_plane = owner // quarter
        relayed = jnp.logical_or(far_plane == 1, far_plane == 2)
        through = jnp.where(far_plane == 1, owner + quarter, owner - quarter)
        return request_copy(
            owner, jnp.where(relayed, through, owner), jnp.where(relayed, mirror(tile), tile)
        )

    def start_near(step, carry):
        owner = near_tile(step)
        request_copy(owner, owner, tile).start()
        return carry

    def start_far(step, carry):
        owner = far_tile(step)

        @pl.when(jnp.logical_not(jnp.logical_and(inner, owner == partner)))
        def _():
            far_request(owner).start()

        return carry

    def sent_near(step, carry):
        owner = near_tile(step)
        request_copy(owner, owner, owner).wait_send()
        return carry

    def sent_far(step, carry):
        owner = far_tile(step)

        @pl.when(jnp.logical_not(jnp.logical_and(inner, owner == partner)))
        def _():
            far_request(owner).wait_send()

        return carry

    def wait_near(step, carry):
        owner = near_tile(step)
        request_copy(owner, owner, owner).wait_recv()
        return carry

    def wait_far(step, carry):
        owner = far_tile(step)

        @pl.when(jnp.logical_not(jnp.logical_and(inner, owner == mirror(tile))))
        def _():
            request_copy(owner, owner, owner).wait_recv()

        return carry

    lax.fori_loop(1, half_tiles, start_near, 0)
    lax.fori_loop(0, half_tiles, start_far, 0)
    asked_ref[tile] = req_ref[tile]

    @pl.when(inner)
    def _():
        asked_ref[mirror(tile)] = req_ref[partner]

    lax.fori_loop(1, half_tiles, sent_near, 0)
    lax.fori_loop(0, half_tiles, sent_far, 0)

    @pl.when(inner)
    def _():
        relay_copy.start()

    loads[0].wait()
    lax.fori_loop(1, half_tiles, wait_near, 0)
    lax.fori_loop(0, half_tiles, wait_far, 0)
    to_smem = pltpu.make_async_copy(asked_ref, asked_smem, smem_sem)
    to_smem.start()
    to_smem.wait()

    def panel_copy(row, dest, owner):
        return pltpu.make_async_remote_copy(
            src_ref=serve_ref.at[row],
            dst_ref=recv_ref.at[pl.ds(owner * capacity, capacity)],
            send_sem=pan_send.at[row],
            recv_sem=pan_recv.at[owner],
            device_id=(segment, dest, core),
            device_id_type=MESH,
        )

    def pack(bank_ref, row):
        for rank in range(capacity):
            serve_ref[row, rank] = bank_ref[asked_smem[row, rank]]

    def serve_near(step, carry):
        dest = near_tile(step)
        pack(held_ref, dest)
        panel_copy(dest, dest, tile).start()
        return carry

    def pack_far(step, carry):
        pack(held_ref, far_tile(step))
        return carry

    def start_far_panels(step, carry):
        dest = far_tile(step)
        panel_copy(dest, dest, tile).start()
        return carry

    def serve_relay(step, carry):
        dest = near_tile(step)
        pack(relay_ref, mirror(dest))
        panel_copy(mirror(dest), dest, partner).start()
        return carry

    lax.fori_loop(1, half_tiles, serve_near, 0)
    for rank in range(capacity):
        recv_ref[tile * capacity + rank] = held_ref[asked_smem[tile, rank]]

    @pl.when(jnp.logical_not(inner))
    def _():
        lax.fori_loop(0, half_tiles, pack_far, 0)
        pl.semaphore_wait(gate_sem, 1)
        lax.fori_loop(0, half_tiles, start_far_panels, 0)

    @pl.when(inner)
    def _():
        relay_copy.wait_recv()
        pl.semaphore_signal(
            gate_sem, inc=1, device_id=(segment, mirror(tile), core), device_id_type=MESH
        )
        lax.fori_loop(1, half_tiles, serve_relay, 0)
        for rank in range(capacity):
            recv_ref[partner * capacity + rank] = relay_ref[asked_smem[mirror(tile), rank]]
        relay_copy.wait_send()

    loads[1].wait()
    loads[2].wait()

    def land_near(step, carry):
        peer = near_tile(step)
        copy = panel_copy(peer, peer, peer)
        copy.wait_send()
        copy.wait_recv()
        return carry

    def land_far(step, carry):
        peer = far_tile(step)

        @pl.when(jnp.logical_not(jnp.logical_and(inner, peer == mirror(tile))))
        def _():
            panel_copy(peer, peer, peer).wait_send()

        @pl.when(jnp.logical_not(jnp.logical_and(inner, peer == partner)))
        def _():
            panel_copy(peer, peer, peer).wait_recv()

        return carry

    lax.fori_loop(1, half_tiles, land_near, 0)
    lax.fori_loop(0, half_tiles, land_far, 0)

    def attend(block, group):
        rows = pl.ds(pl.multiple_of(block * panel, panel), panel)
        scores, values = [], []
        for head in group:
            cols = slice(head * width, (head + 1) * width)
            keys, vals = [fine_ref[1, rows, cols]], [fine_ref[2, rows, cols]]
            for entry in range(lists):
                slot = slot_ref[(head * blocks + block) * lists + entry]
                keys.append(recv_ref[slot, 0])
                vals.append(recv_ref[slot, 1])
            values.append(jnp.concatenate(vals, axis=0))
            scores.append(
                lax.dot_general(
                    fine_ref[0, rows, cols],
                    jnp.concatenate(keys, axis=0),
                    (((1,), (1,)), ((), ())),
                    preferred_element_type=jnp.float32,
                )
                * scale
            )
        weights = []
        for score in scores:
            exponent = jnp.exp(score - jnp.max(score, axis=-1, keepdims=True))
            inverse = 1.0 / jnp.sum(exponent, axis=-1, keepdims=True)
            weights.append((exponent * inverse).astype(jnp.bfloat16))
        for at, head in enumerate(group):
            att_ref[rows, head * width : (head + 1) * width] = jnp.dot(
                weights[at], values[at], preferred_element_type=jnp.float32
            ).astype(jnp.bfloat16)

    def hop(place):
        rows = pl.ds(pl.multiple_of((theirs + place) * panel, panel), panel)
        return pltpu.make_async_remote_copy(
            src_ref=att_ref.at[rows],
            dst_ref=moved_ref.at[rows],
            send_sem=x_send.at[place],
            recv_sem=x_recv.at[place],
            device_id=(nxt, tile, core),
            device_id_type=MESH,
        )

    theirs = (1 - core) * half_blocks
    mine = core * half_blocks
    mine_rows = pl.ds(pl.multiple_of(mine * panel, panel), half)
    theirs_rows = pl.ds(pl.multiple_of(theirs * panel, panel), half)
    groups = (tuple(range(heads - 2)), tuple(range(heads - 2, heads)))

    def hop_mine(at):
        group = groups[at]
        cols = pl.ds(group[0] * width, len(group) * width)
        return pltpu.make_async_remote_copy(
            src_ref=att_ref.at[mine_rows, cols],
            dst_ref=moved_ref.at[mine_rows, cols],
            send_sem=x_send.at[half_blocks + at],
            recv_sem=x_recv.at[half_blocks + at],
            device_id=(nxt, tile, core),
            device_id_type=MESH,
        )

    def send_theirs(place, carry):
        attend(theirs + place, tuple(range(heads)))
        hop(place).start()
        return carry

    lax.fori_loop(0, half_blocks, send_theirs, 0)
    for at in range(2):
        def attend_mine(place, carry):
            attend(mine + place, groups[at])
            return carry

        lax.fori_loop(0, half_blocks, attend_mine, 0)
        hop_mine(at).start()

    step_cols = proj_ref.shape[1] // chunks

    def product(rows, group, chunk):
        depth = slice(group[0] * width, (group[-1] + 1) * width)
        return jnp.dot(
            moved_ref[rows, depth],
            proj_ref[depth, chunk * step_cols : (chunk + 1) * step_cols],
            preferred_element_type=jnp.float32,
        )

    def swap(chunk):
        return pltpu.make_async_remote_copy(
            src_ref=psend_ref.at[chunk],
            dst_ref=precv_ref.at[chunk],
            send_sem=mp_send.at[chunk],
            recv_sem=mp_recv.at[chunk],
            device_id=(segment, tile, 1 - core),
            device_id_type=MESH,
        )

    for place in range(half_blocks):
        hop(place).wait()
    for chunk in range(chunks):
        psend_ref[chunk] = product(theirs_rows, tuple(range(heads)), chunk).astype(jnp.bfloat16)
        swap(chunk).start()
    hop_mine(0).wait()
    for chunk in range(chunks):
        total_ref[chunk] = product(mine_rows, groups[0], chunk)
    for chunk in range(chunks):
        swap(chunk).wait()
    hop_mine(1).wait()
    for chunk in range(chunks):
        own = (total_ref[chunk] + product(mine_rows, groups[1], chunk)).astype(jnp.bfloat16)
        out_ref[:, chunk * step_cols : (chunk + 1) * step_cols] = (
            own.astype(jnp.float32) + precv_ref[chunk].astype(jnp.float32)
        ).astype(jnp.bfloat16)


def on_device(fine_qkv, panels, owners, picks, out_proj):
    tiles = lax.axis_size("tile")
    segments = lax.axis_size("segment")
    heads, blocks, lists = owners.shape[2:]
    entries = heads * blocks * lists
    capacity = max(2, (entries + tiles - 1) // tiles)
    rows = fine_qkv.shape[1]
    held = panels.reshape((-1,) + panels.shape[3:])
    panel, width = held.shape[-2:]
    depth, columns = out_proj.shape
    chunks = 5
    smem = pl.BlockSpec(memory_space=pltpu.SMEM)
    vmem = pl.BlockSpec(memory_space=pltpu.VMEM)
    anywhere = pl.BlockSpec(memory_space=pl.ANY)
    requests, slots = pl.pallas_call(
        functools.partial(request_kernel, capacity),
        out_shape=(
            jax.ShapeDtypeStruct((tiles, LANES), jnp.int32),
            jax.ShapeDtypeStruct((entries,), jnp.int32),
        ),
        in_specs=[smem, smem],
        out_specs=(smem, smem),
        scratch_shapes=[pltpu.SMEM((tiles,), jnp.int32)],
        name="requests",
    )(owners.transpose(0, 1, 3, 4, 2), picks.transpose(0, 1, 3, 4, 2))
    cfg = (tiles, segments, capacity, heads, blocks, lists, panel, width, chunks)
    dma = pltpu.SemaphoreType.DMA
    bf16 = jnp.bfloat16
    merged = pl.pallas_call(
        functools.partial(main_kernel, cfg),
        out_shape=jax.ShapeDtypeStruct((rows // 2, columns), bf16),
        in_specs=[vmem, smem, anywhere, anywhere, anywhere],
        out_specs=vmem,
        scratch_shapes=[
            pltpu.VMEM((3, rows, fine_qkv.shape[3]), bf16),
            pltpu.VMEM(held.shape, bf16),
            pltpu.VMEM(held.shape, bf16),
            pltpu.VMEM(out_proj.shape, bf16),
            pltpu.VMEM((tiles, LANES), jnp.int32),
            pltpu.SMEM((tiles, LANES), jnp.int32),
            pltpu.VMEM((tiles, capacity) + held.shape[1:], bf16),
            pltpu.VMEM((tiles * capacity,) + held.shape[1:], bf16),
            pltpu.VMEM((rows, depth), bf16),
            pltpu.VMEM((rows, depth), bf16),
            pltpu.VMEM((chunks, rows // 2, columns // chunks), bf16),
            pltpu.VMEM((chunks, rows // 2, columns // chunks), bf16),
            pltpu.VMEM((chunks, rows // 2, columns // chunks), jnp.float32),
            dma((3,)),
            dma,
            dma,
            dma,
            pltpu.SemaphoreType.REGULAR,
            dma((tiles,)),
            dma((tiles,)),
            dma((tiles,)),
            dma((tiles,)),
            dma((blocks,)),
            dma((blocks,)),
            dma((chunks,)),
            dma((chunks,)),
        ],
        compiler_params=pltpu.CompilerParams(
            collective_id=0, has_side_effects=True, vmem_limit_bytes=56 * 1024 * 1024
        ),
        name="merging",
    )(requests, slots, fine_qkv.transpose(0, 2, 1, 3)[0], held, out_proj)
    return merged[None]


def column_kernel(
    cfg,
    owners_ref,
    picks_ref,
    fine_hbm,
    held_hbm,
    proj_hbm,
    out_ref,
    fine_ref,
    ask_ref,
    asked_ref,
    query_ref,
    near_ref,
    near_lse,
    give_ref,
    give_lse,
    take_ref,
    take_lse,
    att_ref,
    moved_ref,
    proj_ref,
    total_ref,
    load_sem,
    bank_sem,
    list_send,
    list_recv,
    proj_send,
    proj_recv,
    up_send,
    up_recv,
    over_send,
    over_recv,
    pass_send,
    pass_recv,
    qup_send,
    qup_recv,
    qside_send,
    qside_recv,
    give_send,
    take_recv,
    lse_send,
    lse_recv,
    hop_send,
    hop_recv,
    tail_send,
    tail_recv,
    *bank_refs,
):
    segments, heads, blocks, lists, panel, width, picks, chunks = cfg
    tile = lax.axis_index("tile")
    segment = lax.axis_index("segment")
    core = lax.axis_index("mp")
    plane = tile // 2
    column = lax.rem(tile, 2)
    inner = jnp.logical_or(plane == 1, plane == 2)
    outer = jnp.logical_not(inner)
    low = plane < 2
    server = jnp.where(low, 2, 4) + column
    server_side = jnp.where(low, 2, 4) + 1 - column
    buddy = jnp.where(low, 0, 6) + column
    buddy_side = jnp.where(low, 0, 6) + 1 - column
    cross = jnp.where(plane == 1, tile + 2, tile - 2)
    nxt = lax.rem(segment + 1, segments)
    half = blocks * panel // 2
    scale = 1.0 / math.sqrt(width)
    far_away = -1e30

    def at(where_to):
        return (segment, where_to, core)

    def remote(src, dst, send, recv, device):
        return pltpu.make_async_remote_copy(
            src_ref=src,
            dst_ref=dst,
            send_sem=send,
            recv_sem=recv,
            device_id=device,
            device_id_type=MESH,
        )

    def held_of(head):
        return held_hbm.at[:, head]

    def fine_cols(part, head):
        return fine_hbm.at[part, :, pl.ds(head * width, width)]

    def bank_of(head, which):
        return bank_refs[head].at[pl.ds(which * picks, picks)]

    def up(head):
        return remote(
            held_of(head), bank_of(head, plane), up_send.at[head], up_recv.at[head], at(server)
        )

    def over(head):
        return remote(
            held_of(head), bank_of(head, plane), over_send.at[head], over_recv.at[head], at(cross)
        )

    def passed(head):
        far = buddy // 2
        return remote(
            bank_of(head, far), bank_of(head, far), pass_send.at[head], pass_recv.at[head], at(cross)
        )

    def q_up(head):
        return remote(
            fine_cols(0, head), query_ref.at[2, head], qup_send.at[head], qup_recv.at[head], at(server)
        )

    def q_side(head):
        return remote(
            fine_cols(0, head),
            query_ref.at[1, head],
            qside_send.at[1, head],
            qside_recv.at[1, head],
            at(server_side),
        )

    def q_pass(head):
        return remote(
            query_ref.at[2, head],
            query_ref.at[0, head],
            qside_send.at[0, head],
            qside_recv.at[0, head],
            at(server_side),
        )

    def own_bank(head):
        return pltpu.make_async_copy(held_of(head), bank_of(head, plane), bank_sem.at[head])

    def own_query(head):
        return pltpu.make_async_copy(
            fine_cols(0, head), query_ref.at[3, head], bank_sem.at[heads + head]
        )

    def ask(place, device):
        return remote(
            ask_ref, asked_ref.at[place], list_send.at[place], list_recv.at[place], device
        )

    proj_load = pltpu.make_async_copy(proj_hbm, proj_ref.at[:, core], load_sem.at[1])
    proj_swap = remote(
        proj_hbm, proj_ref.at[:, core], proj_send, proj_recv, (segment, tile, 1 - core)
    )
    fine_load = pltpu.make_async_copy(fine_hbm, fine_ref, load_sem.at[0])
    fine_load.start()

    barrier = pltpu.get_barrier_semaphore()

    def greet(device):
        pl.semaphore_signal(barrier, inc=1, device_id=device, device_id_type=MESH)

    greet((nxt, tile, core))
    greet((nxt, tile, 1 - core))
    greet((segment, tile, 1 - core))
    greet(at(server_side))

    @pl.when(outer)
    def _():
        greet(at(server))

    @pl.when(inner)
    def _():
        greet(at(buddy))
        greet(at(buddy_side))
        greet(at(cross))

    def pack(block, carry):
        for head in range(heads):
            for entry in range(lists):
                owner = owners_ref[0, 0, block, entry, head]
                pick = picks_ref[0, 0, block, entry, head]
                place = (head * blocks + block) * lists + entry
                code = (owner - lax.rem(owner, 2)) * picks + pick * 2 + lax.rem(owner, 2)
                ask_ref[place] = code
                asked_ref[3, place] = code
        return carry

    lax.fori_loop(0, blocks, pack, 0)

    @pl.when(outer)
    def _():
        pl.semaphore_wait(barrier, 5)
        ask(2, at(server)).start()
        ask(0, at(server_side)).start()
        q_up(0).start()
        up(0).start()
        for head in range(1, heads):
            up(head).start()
            q_up(head).start()

    @pl.when(inner)
    def _():
        pl.semaphore_wait(barrier, 7)
        ask(1, at(server_side)).start()
        for head in range(AHEAD):
            over(head).start()
        for head in range(QUERY_AHEAD):
            q_side(head).start()
        for head in range(heads):
            own_bank(head).start()
            own_query(head).start()

    def relay(head):
        if head == 0:
            q_up(head).wait_recv()
            q_pass(head).start()
        up(head).wait_recv()
        passed(head).start()
        if head + AHEAD < heads - 1:
            over(head + AHEAD).start()
        if head + AHEAD == heads:
            over(heads - 1).start()
        if head > 0:
            q_up(head).wait_recv()
            q_pass(head).start()
        if head + QUERY_AHEAD < heads:
            q_side(head + QUERY_AHEAD).start()

    @pl.when(inner)
    def _():
        relay(0)

    proj_load.start()
    proj_swap.start()
    lane = lax.broadcasted_iota(jnp.int32, (panel, LANES), 1)

    def partials(queries, keys, values, biases):
        scores = []
        for place in range(blocks):
            score = (
                lax.dot_general(
                    queries[place],
                    keys[place],
                    (((1,), (1,)), ((), ())),
                    preferred_element_type=jnp.float32,
                )
                * scale
            )
            scores.append(score if biases is None else score + biases[place])
        stat = jnp.ones((panel, LANES), jnp.float32)
        weights, inverses = [], []
        for place in range(blocks):
            top = jnp.max(scores[place], axis=-1, keepdims=True)
            exponent = jnp.exp(scores[place] - top)
            total = jnp.sum(exponent, axis=-1, keepdims=True)
            weights.append(exponent.astype(jnp.bfloat16))
            inverses.append(1.0 / total)
            stat = jnp.where(lane == place, top, stat)
            stat = jnp.where(lane == 8 + place, total, stat)
        outs = []
        for place in range(blocks):
            outs.append(
                (
                    jnp.dot(weights[place], values[place], preferred_element_type=jnp.float32)
                    * inverses[place]
                ).astype(jnp.bfloat16)
            )
        turned = jnp.concatenate([stat, stat], axis=0).T
        return outs, turned[0:8] + jnp.log(turned[8:16])

    def rows_of(place):
        return slice(place * panel, (place + 1) * panel)

    fine_load.wait()

    def attend_fine(head, carry):
        cols = pl.ds(pl.multiple_of(head * width, width), width)
        outs, lse = partials(
            [fine_ref[0, rows_of(place), cols] for place in range(blocks)],
            [fine_ref[1, rows_of(place), cols] for place in range(blocks)],
            [fine_ref[2, rows_of(place), cols] for place in range(blocks)],
            None,
        )
        for place in range(blocks):
            near_ref[head, rows_of(place)] = outs[place]
        near_lse[head] = lse
        return carry

    lax.fori_loop(0, heads, attend_fine, 0)

    def give(place, head):
        goal = jnp.where(place == 0, buddy_side, jnp.where(place == 1, server_side, buddy))
        land = jnp.where(place == 2, 0, 1)
        return (
            remote(
                give_ref.at[place, head],
                take_ref.at[land, head],
                give_send.at[place, head],
                take_recv.at[land, head],
                at(goal),
            ),
            remote(
                give_lse.at[place, head],
                take_lse.at[land, head],
                lse_send.at[place, head],
                lse_recv.at[land, head],
                at(goal),
            ),
        )

    def take(land, head):
        return (
            remote(
                give_ref.at[0, head],
                take_ref.at[land, head],
                give_send.at[0, head],
                take_recv.at[land, head],
                at(server_side),
            ),
            remote(
                give_lse.at[0, head],
                take_lse.at[land, head],
                lse_send.at[0, head],
                lse_recv.at[land, head],
                at(server_side),
            ),
        )

    def give_half(place, half_of):
        last = heads - 1
        rows = pl.ds(half_of * half, half)
        land = 0 if place == 2 else 1
        return remote(
            give_ref.at[place, last, rows],
            take_ref.at[land, last, rows],
            tail_send.at[place, half_of],
            tail_recv.at[land, half_of],
            at((buddy_side, server_side, buddy)[place]),
        )

    def take_half(land, half_of):
        last = heads - 1
        rows = pl.ds(half_of * half, half)
        return remote(
            give_ref.at[0, last, rows],
            take_ref.at[land, last, rows],
            tail_send.at[0, half_of],
            tail_recv.at[land, half_of],
            at(server_side),
        )

    def attend(head):
        bank = bank_refs[head]

        def one_tile(place, carry):
            queries, keys, values, biases = [], [], [], []
            for block in range(blocks):
                codes = [
                    asked_ref[place, (head * blocks + block) * lists + entry]
                    for entry in range(lists)
                ]
                queries.append(query_ref[place, head, rows_of(block)])
                keys.append(
                    jnp.concatenate([bank[lax.div(code, 2), 0] for code in codes], axis=0)
                )
                values.append(
                    jnp.concatenate([bank[lax.div(code, 2), 1] for code in codes], axis=0)
                )
                there = [
                    jnp.where(lax.rem(code, 2) == column, 0.0, far_away) for code in codes
                ]
                biases.append(jnp.where(lane < panel, there[0], there[1]))
            outs, lse = partials(queries, keys, values, biases)
            for block in range(blocks):
                give_ref[place, head, rows_of(block)] = outs[block]
            give_lse[place, head] = lse

            if head < heads - 1:
                @pl.when(place < 3)
                def _():
                    for copy in give(place, head):
                        copy.start()

            return carry

        if head < heads - 1:
            lax.fori_loop(0, 4, one_tile, 0)
            return
        one_tile(0, 0)
        give(0, head)[1].start()
        give_half(0, 0).start()
        one_tile(2, 0)
        give(2, head)[1].start()
        give_half(2, 0).start()
        give_half(0, 1).start()
        give_half(2, 1).start()
        one_tile(1, 0)
        give(1, head)[1].start()
        give_half(1, 0).start()
        give_half(1, 1).start()
        one_tile(3, 0)

    def shares_of(head, first_lse, second_lse):
        top = jnp.maximum(jnp.maximum(near_lse[head], first_lse), second_lse)
        shares = [jnp.exp(lse - top) for lse in (near_lse[head], first_lse, second_lse)]
        inverse = 1.0 / (shares[0] + shares[1] + shares[2])
        shares = [share * inverse for share in shares]
        return jnp.concatenate(
            shares + [jnp.zeros((LANES - 24, LANES), jnp.float32)], axis=0
        ).T[:panel]

    def merge(head, turned, first, second, some):
        for block in some:
            rows = rows_of(block)
            total = near_ref[head, rows].astype(jnp.float32) * turned[:, block : block + 1]
            total = total + first(rows).astype(jnp.float32) * turned[:, 8 + block : 9 + block]
            total = total + second(rows).astype(jnp.float32) * turned[:, 16 + block : 17 + block]
            att_ref[head, rows] = total.astype(jnp.bfloat16)

    def hop(which, head):
        goal = core if which == 0 else 1 - core
        return remote(
            att_ref.at[head, pl.ds(pl.multiple_of(goal * half, half), half)],
            moved_ref.at[head, :, pl.ds(pl.multiple_of(core * width, width), width)],
            hop_send.at[which, head],
            hop_recv.at[which, head],
            (nxt, tile, goal),
        )

    def landed(which, head):
        source = core if which == 0 else 1 - core
        return remote(
            att_ref.at[head, pl.ds(0, half)],
            moved_ref.at[head, :, pl.ds(pl.multiple_of(source * width, width), width)],
            hop_send.at[which, head],
            hop_recv.at[which, head],
            (nxt, tile, source),
        )

    step_cols = out_ref.shape[1] // chunks

    def project(head):
        for which in range(2):
            landed(which, head).wait_recv()
        if head == 0:
            proj_load.wait()
            proj_swap.wait()

        def one_chunk(chunk, carry):
            cols = pl.ds(chunk * step_cols, step_cols)
            if head < heads - 2:
                cols = pl.ds(pl.multiple_of(chunk * step_cols, LANES), step_cols)
            product = jnp.dot(
                moved_ref[head],
                proj_ref[head, :, :, cols].reshape(2 * width, step_cols),
                preferred_element_type=jnp.float32,
            )
            if head == 0:
                total_ref[chunk] = product
            elif head < heads - 1:
                total_ref[chunk] += product
            else:
                out_ref[:, cols] = (total_ref[chunk] + product).astype(jnp.bfloat16)
            return carry

        if head < heads - 2:
            lax.fori_loop(0, chunks, one_chunk, 0)
            return
        for chunk in range(chunks):
            one_chunk(chunk, 0)

    def hop_to(half_of, head):
        which = jnp.where(core == half_of, 0, 1)
        return remote(
            att_ref.at[head, pl.ds(half_of * half, half)],
            moved_ref.at[head, :, pl.ds(pl.multiple_of(core * width, width), width)],
            hop_send.at[which, head],
            hop_recv.at[which, head],
            (nxt, tile, half_of),
        )

    def finish(head):
        def join(lands, first, first_lse, second, second_lse):
            for land in lands:
                take(land, head)[1].wait_recv()
            if head < heads - 1:
                for land in lands:
                    take(land, head)[0].wait_recv()
                turned = shares_of(head, first_lse(), second_lse())
                merge(head, turned, first, second, range(blocks))
                hop(0, head).start()
                hop(1, head).start()
                return
            turned = shares_of(head, first_lse(), second_lse())
            for half_of in range(2):
                for land in lands:
                    take_half(land, half_of).wait_recv()
                some = range(half_of * blocks // 2, (half_of + 1) * blocks // 2)
                merge(head, turned, first, second, some)
                hop_to(half_of, head).start()

        @pl.when(inner)
        def _():
            join(
                (1,),
                lambda rows: give_ref[3, head, rows],
                lambda: give_lse[3, head],
                lambda rows: take_ref[1, head, rows],
                lambda: take_lse[1, head],
            )

        @pl.when(outer)
        def _():
            join(
                (0, 1),
                lambda rows: take_ref[0, head, rows],
                lambda: take_lse[0, head],
                lambda rows: take_ref[1, head, rows],
                lambda: take_lse[1, head],
            )

    @pl.when(inner)
    def _():
        relay(1)
        for place in range(3):
            ask(place, at(server_side)).wait_recv()

    def settle(head):
        hop(0, head).wait_send()
        hop(1, head).wait_send()

        @pl.when(outer)
        def _():
            up(head).wait_send()
            q_up(head).wait_send()

        @pl.when(inner)
        def _():
            over(head).wait_send()
            passed(head).wait_send()
            q_side(head).wait_send()
            q_pass(head).wait_send()
            for place in range(3):
                value, lse = give(place, head)
                lse.wait_send()
                if head < heads - 1:
                    value.wait_send()
                else:
                    give_half(place, 0).wait_send()
                    give_half(place, 1).wait_send()

    for head in range(heads):
        @pl.when(inner)
        def _():
            own_bank(head).wait()
            own_query(head).wait()
            over(head).wait_recv()
            passed(head).wait_recv()
            q_side(head).wait_recv()
            q_pass(head).wait_recv()
            attend(head)
            if head + 2 < heads:
                relay(head + 2)

        if head >= 1:
            finish(head - 1)
        if head >= 2:
            project(head - 2)
            settle(head - 2)
    finish(heads - 1)
    project(heads - 2)
    project(heads - 1)

    for head in range(heads - 2, heads):
        settle(head)

    @pl.when(outer)
    def _():
        ask(2, at(server)).wait_send()
        ask(0, at(server_side)).wait_send()

    @pl.when(inner)
    def _():
        ask(1, at(server_side)).wait_send()


def by_columns(fine_qkv, panels, owners, picks, out_proj):
    segments = lax.axis_size("segment")
    heads, blocks, lists = owners.shape[2:]
    rows = fine_qkv.shape[1]
    held = panels[0]
    each, _, _, panel, width = held.shape
    planes = lax.axis_size("tile") // 2
    columns = out_proj.shape[1]
    chunks = 5
    smem = pl.BlockSpec(memory_space=pltpu.SMEM)
    vmem = pl.BlockSpec(memory_space=pltpu.VMEM)
    anywhere = pl.BlockSpec(memory_space=pl.ANY)
    cfg = (segments, heads, blocks, lists, panel, width, each, chunks)
    dma = pltpu.SemaphoreType.DMA
    bf16 = jnp.bfloat16
    merged = pl.pallas_call(
        functools.partial(column_kernel, cfg),
        out_shape=pltpu.VMEM((rows // 2, columns), bf16),
        in_specs=[smem, smem, anywhere, anywhere, anywhere],
        out_specs=vmem,
        scratch_shapes=[
            pltpu.VMEM((3, rows, fine_qkv.shape[3]), bf16),
            pltpu.SMEM((LANES,), jnp.int32),
            pltpu.SMEM((4, LANES), jnp.int32),
            pltpu.VMEM((4, heads, rows, width), bf16),
            pltpu.VMEM((heads, rows, width), bf16),
            pltpu.VMEM((heads, 8, LANES), jnp.float32),
            pltpu.VMEM((4, heads, rows, width), bf16),
            pltpu.VMEM((4, heads, 8, LANES), jnp.float32),
            pltpu.VMEM((2, heads, rows, width), bf16),
            pltpu.VMEM((2, heads, 8, LANES), jnp.float32),
            pltpu.VMEM((heads, rows, width), bf16),
            pltpu.VMEM((heads, rows // 2, 2 * width), bf16),
            pltpu.VMEM((heads, 2, width, columns), bf16),
            pltpu.VMEM((chunks, rows // 2, columns // chunks), jnp.float32),
            dma((2,)),
            dma((2 * heads,)),
            dma((3,)),
            dma((3,)),
            dma,
            dma,
            dma((heads,)),
            dma((heads,)),
            dma((heads,)),
            dma((heads,)),
            dma((heads,)),
            dma((heads,)),
            dma((heads,)),
            dma((heads,)),
            dma((2, heads)),
            dma((2, heads)),
            dma((3, heads)),
            dma((2, heads)),
            dma((3, heads)),
            dma((2, heads)),
            dma((2, heads)),
            dma((2, heads)),
            dma((3, 2)),
            dma((2, 2)),
        ]
        + [pltpu.VMEM((planes * each,) + held.shape[2:], bf16) for _ in range(heads)],
        compiler_params=pltpu.CompilerParams(
            collective_id=1, has_side_effects=True, vmem_limit_bytes=56 * 1024 * 1024
        ),
        name="columns",
    )(
        owners.transpose(0, 1, 3, 4, 2),
        picks.transpose(0, 1, 3, 4, 2),
        fine_qkv.transpose(0, 2, 1, 3)[0],
        held,
        out_proj.reshape(heads, width, columns),
    )
    return merged[None]


def solution(mesh):
    placed = (
        P("segment", "tile", None, "mp"),
        P("segment", "tile", "mp", None, None, None),
        P("segment", "tile", "mp", None, None),
        P("segment", "tile", "mp", None, None),
        P("mp", None),
    )
    small = mesh.shape["tile"] == 8 and mesh.shape["segment"] == 2
    return jax.shard_map(
        by_columns if small else on_device,
        mesh=mesh,
        in_specs=placed,
        out_specs=P("segment", ("tile", "mp"), None),
        check_vma=False,
    )
```
